32 devices in a mesh: row: 4 (over y, core), col: 8 (over z, x).
Axes of the slice: x: 2, y: 2, z: 4, core: 2. Of those that a mesh axis runs over, the one named last changes fastest.
Arguments:
- tokens: bfloat16 [16384, 768], P(('row', 'col')), may hold values from -6 to 6
- parents: int32 [4, 16], P('row'), may hold values from -1 to 14, as said below
- w_qkv: bfloat16 [768, 2304], P('row', 'col'), may hold values from -0.21875 to 0.21875
- w_out: bfloat16 [768, 768], P('row', 'col'), may hold values from -0.875 to 0.875
- w_up: bfloat16 [768, 3072], P('row', 'col'), may hold values from -0.21875 to 0.21875
- w_down: bfloat16 [3072, 768], P('row', 'col'), may hold values from -0.109375 to 0.109375
- ln_gain: bfloat16 [2, 768], P(None, 'col'), may hold values from 0.099609375 to 1.8984375
- ln_bias: bfloat16 [2, 768], P(None, 'col'), may hold values from -3 to 3
- proj_bias: bfloat16 [4, 768], P(None, 'col'), may hold values from -3 to 3
- ff_bias: bfloat16 [3072], P('col'), may hold values from -3 to 3
- cotangent: bfloat16 [16384, 768], P(('row', 'col')), may hold values from -6 to 6
Outputs:
- output: bfloat16 [16384, 768], P(('row', 'col'))
- grad_tokens: bfloat16 [16384, 768], P(('row', 'col'))
- grad_w_qkv: float32 [768, 2304], P('row', 'col')
- grad_w_out: float32 [768, 768], P('row', 'col')
- grad_w_up: float32 [768, 3072], P('row', 'col')
- grad_w_down: float32 [3072, 768], P('row', 'col')
- grad_ln_gain: float32 [2, 768], P(None, 'col')
- grad_ln_bias: float32 [2, 768], P(None, 'col')
- grad_proj_bias: float32 [4, 768], P(None, 'col')
- grad_ff_bias: float32 [3072], P('col')
The draws below stay inside these ranges and needn't reach their ends.
Inputs may be any that keep to these rules, and one draw needn't show every extreme that they name: `parents`: for each tree, segments 0 to 3 are the trunk: segment 0 has parent -1 and each other trunk segment continues the one before. The remaining segments are 4 branches that continue segment 4 - 1 and, for each branch, 2 leaves that continue it; segment 16 - 2 is a branch and segment 16 - 1 one of its leaves, the others come in any order.
All inputs are finite; a program needn't handle non-finite values.
Results may differ from the reference program's by a relative error of at most 0.017.
Values may be sent and summed in bfloat16 or wider, within the bound.
No kernel may reach another device: no remote copies, remote signals or barrier semaphores. Data moves between devices by JAX's collectives and lax.ppermute only.
A program may use at most 192 MiB of HBM per device.

```python
import jax
import jax.numpy as jnp
from jax import lax

D = 768
HEADS = 12
HEAD_DIM = 64
FF = 3072
SEG = 256
BRANCHES = 4
LEAVES = 2
TRUNK_SEGS = 4
SEGS = 16
TREE_TOKENS = 4096
TREES = 4
TOKENS = 16384


def draw_parents(key, part):

    def one_tree(tree_key):
        side_count = BRANCHES + BRANCHES * LEAVES
        others = jnp.concatenate([jnp.arange(1, BRANCHES, dtype=jnp.int32), jnp.arange(BRANCHES + 1, side_count, dtype=jnp.int32)])
        shuffled = jax.random.permutation(tree_key, others).astype(jnp.int32)
        arrangement = jnp.concatenate([shuffled, jnp.array([0, BRANCHES], dtype=jnp.int32)])
        location = jnp.argsort(arrangement).astype(jnp.int32)
        branch_of = jnp.maximum(arrangement - BRANCHES, 0) // LEAVES
        leaf_parent = TRUNK_SEGS + location[branch_of]
        side_links = jnp.where(arrangement < BRANCHES, TRUNK_SEGS - 1, leaf_parent).astype(jnp.int32)
        trunk_links = jnp.arange(TRUNK_SEGS, dtype=jnp.int32) - 1
        return jnp.concatenate([trunk_links, side_links])
    return jax.vmap(one_tree)(jax.random.split(key, TREES)).astype(jnp.int32)


def shard_levels(own_key, dims, cuts, low, largest):
    def one(dim, parts):
        steps = jax.random.uniform(jax.random.fold_in(jax.random.fold_in(own_key, 6), dim), (parts,), jnp.float32, low / len(cuts), largest / len(cuts))
        return jnp.repeat(jnp.exp(steps), dims[dim] // parts).reshape((-1,) + (1,) * (len(dims) - dim - 1))

    factor_of = one(*cuts[0])
    for cut in cuts[1:]:
        factor_of = factor_of * one(*cut)
    return factor_of


def bell_draw(stream_key, dims, scale, bound, pieces=(), kind=jnp.bfloat16):
    drawn = jax.random.normal(stream_key, dims, jnp.float32) * scale
    if len(pieces) > 0:
        drawn = shard_levels(stream_key, dims, pieces, -0.22, 0.18) * drawn
    return jnp.clip(drawn, min=-bound, max=bound).astype(kind)


def setup_inputs(seed: int = 0) -> dict:
    key_list = jax.random.split(jax.random.key(seed), 12)
    return {
        "tokens": bell_draw(key_list[0], (TOKENS, D), 1.0, 6.0, ((0, 32),)),
        "parents": draw_parents(jax.random.fold_in(key_list[11], 71), 0),
        "w_qkv": bell_draw(key_list[2], (D, 3 * D), D ** -0.5, 0.21875, ((0, 4), (1, 8))),
        "w_out": bell_draw(key_list[3], (D, D), (D // 16) ** -0.5, 0.875, ((0, 4), (1, 8))),
        "w_up": bell_draw(key_list[4], (D, FF), D ** -0.5, 0.21875, ((0, 4), (1, 8))),
        "w_down": bell_draw(key_list[5], (FF, D), FF ** -0.5, 0.109375, ((0, 4), (1, 8))),
        "ln_gain": jnp.clip(1.0 + 0.18 * jax.random.normal(key_list[6], (2, D), jnp.float32), 0.099609375, 1.8984375).astype(jnp.bfloat16),
        "ln_bias": bell_draw(key_list[7], (2, D), 0.5, 3.0, ((1, 8),)),
        "proj_bias": bell_draw(key_list[8], (4, D), 0.5, 3.0, ((1, 8),)),
        "ff_bias": bell_draw(key_list[9], (FF,), 0.5, 3.0, ((0, 8),)),
        "cotangent": bell_draw(key_list[10], (TOKENS, D), 1.0, 6.0, ((0, 32),)),
    }


EPSILON = 1e-12
NEGATIVE = -1e+30

@jax.custom_vjp
def low(v):
    return lax.optimization_barrier(v.astype(jnp.bfloat16)).astype(jnp.float32)

@jax.custom_vjp
def low_back(v):
    return v

def low_keep(v):
    return (low(v), None)

def low_pass(kept, grad):
    return (grad,)

def back_keep(v):
    return (v, None)

def back_low(kept, grad):
    return (low(grad),)
low.defvjp(low_keep, low_pass)
low_back.defvjp(back_keep, back_low)

def layer_norm(values, scaling, shifting):
    centre = values - lax.optimization_barrier(jnp.mean(values, axis=-1, keepdims=True))
    spread = lax.optimization_barrier(jnp.mean(centre * centre, axis=-1, keepdims=True))
    return centre * lax.rsqrt(spread + EPSILON) * scaling + shifting

def ancestry(parents):
    segment_count = parents.shape[0]
    labels = jnp.arange(segment_count, dtype=jnp.int32)
    closure = jnp.eye(segment_count, dtype=jnp.float32) + (parents[:, None] == labels[None, :]).astype(jnp.float32)
    for repeat in range(segment_count.bit_length()):
        closure = jnp.minimum(jnp.dot(closure, closure, precision=lax.Precision.HIGHEST), 1.0)
    return closure

def allowed(query_pos, key_pos, closure):
    labels = jnp.arange(closure.shape[0], dtype=jnp.int32)
    query_seg = query_pos // SEG
    key_seg = key_pos // SEG
    query_hot = (query_seg[:, None] == labels[None, :]).astype(jnp.float32)
    key_hot = (key_seg[:, None] == labels[None, :]).astype(jnp.float32)
    reach = jnp.dot(jnp.dot(query_hot, closure, precision=lax.Precision.HIGHEST), key_hot.T, precision=lax.Precision.HIGHEST)
    causal = (query_seg[:, None] != key_seg[None, :]) | (key_pos[None, :] <= query_pos[:, None])
    return (reach > 0.5) & causal

def forward_tree(inputs, closure, w_qkv, w_out, w_up, w_down, ln_gain, ln_bias, proj_bias, ff_bias):
    highest = lax.Precision.HIGHEST
    head_shape = (TREE_TOKENS, HEADS, HEAD_DIM)
    block_rows = 2 * SEG
    normed = low(layer_norm(inputs, ln_gain[0], ln_bias[0]))
    projected = low_back(jnp.dot(normed, w_qkv, precision=highest))
    queries = low(projected[:, :D] + proj_bias[0]).reshape(head_shape)
    key_rows = low(projected[:, D:2 * D]).reshape(head_shape)
    value_rows = low(projected[:, 2 * D:] + proj_bias[1]).reshape(head_shape)
    key_pos = jnp.arange(TREE_TOKENS, dtype=jnp.int32)

    def attend(first_pos):
        query_block = lax.dynamic_slice_in_dim(queries, first_pos.astype(jnp.int32), block_rows, 0)
        products = low_back(jnp.einsum('qhd,khd->hqk', query_block, key_rows, precision=highest))
        visible = allowed(first_pos + jnp.arange(block_rows, dtype=jnp.int32), key_pos, closure)
        scores = jnp.where(visible[None], products * HEAD_DIM ** (-0.5), NEGATIVE)
        chances = low(jax.nn.softmax(scores, axis=-1))
        return jnp.einsum('hqk,khd->qhd', chances, value_rows, precision=highest)
    attended = lax.map(jax.checkpoint(attend), jnp.arange(SEGS // 2, dtype=jnp.int32) * block_rows)
    attended = low(low_back(attended.reshape(TREE_TOKENS, D)))
    mixed_rows = inputs + low_back(jnp.dot(attended, w_out, precision=highest)) + proj_bias[2]
    second = low(layer_norm(mixed_rows, ln_gain[1], ln_bias[1]))
    hidden = low_back(jnp.dot(second, w_up, precision=highest)) + ff_bias
    activated = low(jax.nn.gelu(hidden, approximate=False))
    return mixed_rows + low_back(jnp.dot(activated, w_down, precision=highest)) + proj_bias[3]

def reference(tokens, parents, w_qkv, w_out, w_up, w_down, ln_gain, ln_bias, proj_bias, ff_bias, cotangent):
    float_params = (w_qkv.astype(jnp.float32), w_out.astype(jnp.float32), w_up.astype(jnp.float32), w_down.astype(jnp.float32), ln_gain.astype(jnp.float32), ln_bias.astype(jnp.float32), proj_bias.astype(jnp.float32), ff_bias.astype(jnp.float32))
    inputs = tokens.astype(jnp.float32).reshape(TREES, TREE_TOKENS, D)
    upstream = cotangent.astype(jnp.float32).reshape(TREES, TREE_TOKENS, D)

    def per_tree(summed, items):
        tree_inputs, tree_upstream, tree_parents = items
        closure = ancestry(tree_parents)

        def forward(layer_in, *weights):
            return forward_tree(layer_in, closure, *weights)
        result, pullback = jax.vjp(forward, tree_inputs, *float_params)
        gradients = pullback(tree_upstream)
        summed = tuple((earlier + gradient for earlier, gradient in zip(summed, gradients[1:])))
        return (summed, (result.astype(jnp.bfloat16), gradients[0].astype(jnp.bfloat16)))
    zeroed = tuple((jnp.zeros_like(param_array) for param_array in float_params))
    summed, (results, grad_inputs) = lax.scan(per_tree, zeroed, (inputs, upstream, parents))
    return (results.reshape(TOKENS, D), grad_inputs.reshape(TOKENS, D), summed[0], summed[1], summed[2], summed[3], summed[4], summed[5], summed[6], summed[7])
```

```python
import jax
import jax.numpy as jnp
from jax import lax
from jax.experimental import pallas as pl
from jax.experimental.pallas import tpu as pltpu
from jax.sharding import PartitionSpec as P

D = 768
HEADS = 12
HEAD_DIM = 64
SEG = 256
SEGS = 16
TREE_TOKENS = 4096


EPSILON = 1e-12
NEGATIVE = -1e30


def layer_norm(values, scaling, shifting):
    centre = values - jnp.mean(values, axis=-1, keepdims=True)
    spread = jnp.mean(centre * centre, axis=-1, keepdims=True)
    return centre * lax.rsqrt(spread + EPSILON) * scaling + shifting


def exact_gelu(values):
    return jax.nn.gelu(values, approximate=False)


def ancestry(parents):
    segment_count = parents.shape[0]
    labels = jnp.arange(segment_count, dtype=jnp.int32)
    closure = jnp.eye(segment_count, dtype=jnp.float32) + (
        parents[:, None] == labels[None, :]
    ).astype(jnp.float32)
    for repeat in range(segment_count.bit_length()):
        closure = jnp.minimum(jnp.dot(closure, closure, precision=lax.Precision.HIGHEST), 1.0)
    return closure


def allowed(query_pos, key_pos, closure):
    labels = jnp.arange(closure.shape[0], dtype=jnp.int32)
    query_seg = query_pos // SEG
    key_seg = key_pos // SEG
    query_hot = (query_seg[:, None] == labels[None, :]).astype(jnp.float32)
    key_hot = (key_seg[:, None] == labels[None, :]).astype(jnp.float32)
    reach = jnp.dot(
        jnp.dot(query_hot, closure, precision=lax.Precision.HIGHEST),
        key_hot.T,
        precision=lax.Precision.HIGHEST,
    )
    causal = (query_seg[:, None] != key_seg[None, :]) | (key_pos[None, :] <= query_pos[:, None])
    return (reach > 0.5) & causal


def plain_body(
    tokens, parents, w_qkv, w_out, w_up, w_down, ln_gain, ln_bias, proj_bias, ff_bias, cotangent
):
    local_rows = tokens.shape[0]
    score_scale = HEAD_DIM ** (-0.5)
    head_shape = (local_rows, HEADS, HEAD_DIM)
    block_rows = 2 * SEG
    block_count = SEGS // 2
    cols_qkv, cols_out, cols_up, cols_down, norm_gains, shifts, biases, ff_shift = (
        lax.all_gather(w_qkv, "col", axis=1, tiled=True),
        lax.all_gather(w_out, "col", axis=1, tiled=True),
        lax.all_gather(w_up, "col", axis=1, tiled=True),
        lax.all_gather(w_down, "col", axis=1, tiled=True),
        lax.all_gather(ln_gain, "col", axis=1, tiled=True),
        lax.all_gather(ln_bias, "col", axis=1, tiled=True),
        lax.all_gather(proj_bias, "col", axis=1, tiled=True),
        lax.all_gather(ff_bias, "col", axis=0, tiled=True),
    )
    full_qkv, full_out, full_up, full_down = (
        lax.all_gather(cols_qkv, "row", axis=0, tiled=True),
        lax.all_gather(cols_out, "row", axis=0, tiled=True),
        lax.all_gather(cols_up, "row", axis=0, tiled=True),
        lax.all_gather(cols_down, "row", axis=0, tiled=True),
    )
    norm_gains = norm_gains.astype(jnp.float32)
    shifts = shifts.astype(jnp.float32)
    biases = biases.astype(jnp.float32)
    ff_shift = ff_shift.astype(jnp.float32)
    inputs = tokens.astype(jnp.float32)
    normed_low = layer_norm(inputs, norm_gains[0], shifts[0]).astype(jnp.bfloat16)
    projected = jnp.dot(normed_low, full_qkv, preferred_element_type=jnp.float32)
    queries = (projected[:, :D] + biases[0]).astype(jnp.bfloat16).reshape(head_shape)
    keys_own = projected[:, D : 2 * D].astype(jnp.bfloat16).reshape(head_shape)
    values_own = (projected[:, 2 * D :] + biases[1]).astype(jnp.bfloat16).reshape(head_shape)
    keys_all, values_all = (
        lax.all_gather(keys_own, "col", axis=0, tiled=True),
        lax.all_gather(values_own, "col", axis=0, tiled=True),
    )
    key_blocks = keys_all.reshape(block_count, block_rows, HEADS, HEAD_DIM)
    value_blocks = values_all.reshape(block_count, block_rows, HEADS, HEAD_DIM)
    block_starts = jnp.arange(block_count, dtype=jnp.int32) * block_rows
    within = jnp.arange(block_rows, dtype=jnp.int32)
    query_pos = lax.axis_index("col") * local_rows + jnp.arange(local_rows, dtype=jnp.int32)
    closure = ancestry(parents[0])

    def scores_of(query_block, key_block, query_positions, key_positions):
        products = jnp.einsum(
            "qhd,khd->hqk", query_block, key_block, preferred_element_type=jnp.float32
        )
        return (products * score_scale, allowed(query_positions, key_positions, closure)[None])

    def probabilities(query_block, key_block, query_positions, key_positions, log_block):
        scores, visible = scores_of(query_block, key_block, query_positions, key_positions)
        return jnp.where(visible, jnp.exp(scores - log_block[..., None]), 0.0)

    def extent(running, pieces):
        highest_score, mass_total = running
        key_block, first_pos = pieces
        scores, visible = scores_of(queries, key_block, query_pos, first_pos + within)
        masked = jnp.where(visible, scores, NEGATIVE)
        new_highest = jnp.maximum(highest_score, jnp.max(masked, axis=-1))
        exp_terms = jnp.where(visible, jnp.exp(masked - new_highest[..., None]), 0.0)
        new_total = mass_total * jnp.exp(highest_score - new_highest) + jnp.sum(exp_terms, axis=-1)
        return ((new_highest, new_total), None)

    start_state = (
        jnp.full((HEADS, local_rows), NEGATIVE, jnp.float32),
        jnp.zeros((HEADS, local_rows), jnp.float32),
    )
    (highest_score, mass_total), unused = lax.scan(extent, start_state, (key_blocks, block_starts))
    log_total = highest_score + jnp.log(mass_total)

    def attend(running, pieces):
        key_block, value_block, first_pos = pieces
        chances = probabilities(
            queries, key_block, query_pos, first_pos + within, log_total
        ).astype(jnp.bfloat16)
        return (
            running
            + jnp.einsum("hqk,khd->qhd", chances, value_block, preferred_element_type=jnp.float32),
            None,
        )

    attended, unused = lax.scan(
        attend, jnp.zeros(head_shape, jnp.float32), (key_blocks, value_blocks, block_starts)
    )
    attended_low = attended.reshape(local_rows, D).astype(jnp.bfloat16)
    mixed_rows = (
        inputs + jnp.dot(attended_low, full_out, preferred_element_type=jnp.float32) + biases[2]
    )
    second_low = layer_norm(mixed_rows, norm_gains[1], shifts[1]).astype(jnp.bfloat16)
    hidden_pre = jnp.dot(second_low, full_up, preferred_element_type=jnp.float32) + ff_shift
    activated_low = exact_gelu(hidden_pre).astype(jnp.bfloat16)
    output = (
        mixed_rows
        + jnp.dot(activated_low, full_down, preferred_element_type=jnp.float32)
        + biases[3]
    )
    upstream = cotangent.astype(jnp.float32)
    grad_down = jnp.einsum(
        "tf,td->fd", activated_low, cotangent, preferred_element_type=jnp.float32
    )
    grad_act = jnp.einsum("td,fd->tf", cotangent, full_down, preferred_element_type=jnp.float32)
    unused, gelu_back = jax.vjp(exact_gelu, hidden_pre)
    grad_pre = gelu_back(grad_act)[0]
    grad_pre_low = grad_pre.astype(jnp.bfloat16)
    grad_up = jnp.einsum("td,tf->df", second_low, grad_pre_low, preferred_element_type=jnp.float32)
    grad_second = jnp.einsum("tf,df->td", grad_pre_low, full_up, preferred_element_type=jnp.float32)
    unused, second_back = jax.vjp(layer_norm, mixed_rows, norm_gains[1], shifts[1])
    grad_mixed_norm, grad_gain_two, grad_shift_two = second_back(grad_second)
    grad_mixed = upstream + grad_mixed_norm
    grad_mixed_low = grad_mixed.astype(jnp.bfloat16)
    grad_out = jnp.einsum(
        "td,te->de", attended_low, grad_mixed_low, preferred_element_type=jnp.float32
    )
    grad_att_low = (
        jnp.einsum("te,de->td", grad_mixed_low, full_out, preferred_element_type=jnp.float32)
        .astype(jnp.bfloat16)
        .reshape(head_shape)
    )
    deltas = jnp.einsum("qhd,qhd->hq", grad_att_low.astype(jnp.float32), attended)

    def score_grads(
        query_block,
        key_block,
        value_block,
        grad_block,
        query_positions,
        key_positions,
        log_block,
        delta_block,
    ):
        chances = probabilities(query_block, key_block, query_positions, key_positions, log_block)
        grad_chances = jnp.einsum(
            "qhd,khd->hqk", grad_block, value_block, preferred_element_type=jnp.float32
        )
        grad_scores = (chances * (grad_chances - delta_block[..., None]) * score_scale).astype(
            jnp.bfloat16
        )
        return (chances.astype(jnp.bfloat16), grad_scores)

    def backward_block(running, pieces):
        key_block, value_block, first_pos = pieces
        chances_low, grad_scores = score_grads(
            queries,
            key_block,
            value_block,
            grad_att_low,
            query_pos,
            first_pos + within,
            log_total,
            deltas,
        )
        running = running + jnp.einsum(
            "hqk,khd->qhd", grad_scores, key_block, preferred_element_type=jnp.float32
        )
        key_term = jnp.einsum(
            "hqk,qhd->khd", grad_scores, queries, preferred_element_type=jnp.float32
        )
        value_term = jnp.einsum(
            "hqk,qhd->khd", chances_low, grad_att_low, preferred_element_type=jnp.float32
        )
        return (running, (key_term, value_term))

    grad_queries, (key_terms, value_terms) = lax.scan(
        backward_block, jnp.zeros(head_shape, jnp.float32), (key_blocks, value_blocks, block_starts)
    )
    grad_keys, grad_values = (
        lax.psum_scatter(
            key_terms.reshape(TREE_TOKENS, D).astype(jnp.bfloat16),
            "col",
            scatter_dimension=0,
            tiled=True,
        ).astype(jnp.float32),
        lax.psum_scatter(
            value_terms.reshape(TREE_TOKENS, D).astype(jnp.bfloat16),
            "col",
            scatter_dimension=0,
            tiled=True,
        ).astype(jnp.float32),
    )
    grad_queries = grad_queries.reshape(local_rows, D)
    grad_projected_low = jnp.concatenate([grad_queries, grad_keys, grad_values], axis=1).astype(
        jnp.bfloat16
    )
    grad_qkv = jnp.einsum(
        "td,te->de", normed_low, grad_projected_low, preferred_element_type=jnp.float32
    )
    grad_normed = jnp.einsum(
        "te,de->td", grad_projected_low, full_qkv, preferred_element_type=jnp.float32
    )
    unused, first_back = jax.vjp(layer_norm, inputs, norm_gains[0], shifts[0])
    grad_input_norm, grad_gain_one, grad_shift_one = first_back(grad_normed)
    grad_tokens = (grad_mixed + grad_input_norm).astype(jnp.bfloat16)
    gain_terms = jnp.stack([grad_gain_one, grad_gain_two])
    shift_terms = jnp.stack([grad_shift_one, grad_shift_two])
    bias_terms = jnp.stack(
        [
            jnp.sum(grad_queries, axis=0),
            jnp.sum(grad_values, axis=0),
            jnp.sum(grad_mixed, axis=0),
            jnp.sum(upstream, axis=0),
        ]
    )
    ff_terms = jnp.sum(grad_pre, axis=0)
    part_qkv, part_out, part_up, part_down, part_gain, part_shift, part_bias, part_ff = (
        lax.psum_scatter(
            grad_qkv.astype(jnp.bfloat16), "col", scatter_dimension=1, tiled=True
        ).astype(jnp.float32),
        lax.psum_scatter(
            grad_out.astype(jnp.bfloat16), "col", scatter_dimension=1, tiled=True
        ).astype(jnp.float32),
        lax.psum_scatter(
            grad_up.astype(jnp.bfloat16), "col", scatter_dimension=1, tiled=True
        ).astype(jnp.float32),
        lax.psum_scatter(
            grad_down.astype(jnp.bfloat16), "col", scatter_dimension=1, tiled=True
        ).astype(jnp.float32),
        lax.psum_scatter(
            gain_terms.astype(jnp.bfloat16), "col", scatter_dimension=1, tiled=True
        ).astype(jnp.float32),
        lax.psum_scatter(
            shift_terms.astype(jnp.bfloat16), "col", scatter_dimension=1, tiled=True
        ).astype(jnp.float32),
        lax.psum_scatter(
            bias_terms.astype(jnp.bfloat16), "col", scatter_dimension=1, tiled=True
        ).astype(jnp.float32),
        lax.psum_scatter(
            ff_terms.astype(jnp.bfloat16), "col", scatter_dimension=0, tiled=True
        ).astype(jnp.float32),
    )
    grad_w_qkv, grad_w_out, grad_w_up, grad_w_down = (
        lax.psum_scatter(
            part_qkv.astype(jnp.bfloat16), "row", scatter_dimension=0, tiled=True
        ).astype(jnp.float32),
        lax.psum_scatter(
            part_out.astype(jnp.bfloat16), "row", scatter_dimension=0, tiled=True
        ).astype(jnp.float32),
        lax.psum_scatter(
            part_up.astype(jnp.bfloat16), "row", scatter_dimension=0, tiled=True
        ).astype(jnp.float32),
        lax.psum_scatter(
            part_down.astype(jnp.bfloat16), "row", scatter_dimension=0, tiled=True
        ).astype(jnp.float32),
    )
    grad_gain, grad_shift, grad_bias, grad_ff = lax.psum(
        (part_gain, part_shift, part_bias, part_ff), "row"
    )
    return (
        output.astype(jnp.bfloat16),
        grad_tokens,
        grad_w_qkv,
        grad_w_out,
        grad_w_up,
        grad_w_down,
        grad_gain,
        grad_shift,
        grad_bias,
        grad_ff,
    )


F32=jnp.float32; BF=jnp.bfloat16
NEG=NEGATIVE
NT=(((1,),(1,)),((),()))
NN=(((1,),(0,)),((),()))
def dg(a,b,dims): return lax.dot_general(a,b,dims,preferred_element_type=F32)

def chunks_of(trunk):
    return [0,1,2,3] if trunk else [0,1,2,3,4,5]

def score_chunk(c, trunk, k_ref, qh, meta):
    if c<4:
        st=dg(k_ref[c*SEG:(c+1)*SEG,:], qh, NT)
        if trunk:
            kp=c*SEG+lax.broadcasted_iota(jnp.int32,(SEG,2*SEG),0)
            qp=meta[1]+lax.broadcasted_iota(jnp.int32,(SEG,2*SEG),1)
            st=jnp.where(kp<=qp,st,NEG)
        return st
    base=4*SEG+(c-4)*2*SEG
    parts=[]
    for i in range(2):
        s=dg(k_ref[base+i*SEG:base+(i+1)*SEG,:], qh[i*SEG:(i+1)*SEG,:], NT)
        if c==4:
            s=s+jnp.where(meta[2+i]>0,0.0,NEG).astype(F32)
        else:
            kp=lax.broadcasted_iota(jnp.int32,(SEG,SEG),0)
            qp=lax.broadcasted_iota(jnp.int32,(SEG,SEG),1)
            s=jnp.where(kp<=qp,s,NEG)
        parts.append(s)
    return jnp.concatenate(parts,axis=1)

def fwd_kernel(meta, q_ref,k_ref,v_ref,o_ref,lse_ref):
    def run(trunk):
        q=q_ref[...]*jnp.asarray(0.125,BF)
        lane=lax.broadcasted_iota(jnp.int32,q.shape,1)
        vt=v_ref[...].T
        res=[]
        for h in range(2):
            qh=jnp.where((lane<64)==(h==0),q,jnp.asarray(0,BF))
            cs=chunks_of(trunk)
            st=[score_chunk(c,trunk,k_ref,qh,meta) for c in cs]
            m=st[0]
            for s in st[1:]: m=jnp.maximum(m,s)
            m=jnp.max(m,axis=0,keepdims=True)
            l=jnp.zeros((1,2*SEG),F32);
            ot=jnp.zeros((128,2*SEG),F32); own=[jnp.zeros((128,SEG),F32)]*2
            for c,s in zip(cs,st):
                p=jnp.exp(s-m)
                l=l+jnp.sum(p,axis=0,keepdims=True)
                pb=p.astype(BF)
                if c<4:
                    ot=ot+dg(vt[:,c*SEG:(c+1)*SEG],pb,NN)
                else:
                    base=4*SEG+(c-4)*2*SEG
                    own=[own[i]+dg(vt[:,base+i*SEG:base+(i+1)*SEG],pb[:,i*SEG:(i+1)*SEG],NN) for i in range(2)]
            ot=(ot+jnp.concatenate(own,axis=1))*(1.0/l)
            res.append(ot)
            lse_ref[0,h:h+1,:]=m+jnp.log(l)
        row=lax.broadcasted_iota(jnp.int32,res[0].shape,0)
        o_ref[...]=jnp.where(row<64,res[0],res[1]).T.astype(BF)
    @pl.when(meta[0]>0)
    def _(): run(True)
    @pl.when(meta[0]==0)
    def _(): run(False)

def bwd_kernel(meta, q_ref,k_ref,v_ref,do_ref,o_ref,lse_ref,dq_ref,dk_ref,dv_ref):
    def run(trunk):
        q=q_ref[...]*jnp.asarray(0.125,BF)
        do=do_ref[...]
        lane=lax.broadcasted_iota(jnp.int32,q.shape,1)
        zero=jnp.asarray(0,BF)
        dd=(do.astype(F32)*o_ref[...].astype(F32)).T
        kt=k_ref[...].T
        qh=[jnp.where((lane<64)==(h==0),q,zero) for h in range(2)]
        doh=[jnp.where((lane<64)==(h==0),do,zero) for h in range(2)]
        delta=[jnp.sum(dd[h*64:(h+1)*64],axis=0,keepdims=True) for h in range(2)]
        qcat=jnp.concatenate(qh,axis=0); docat=jnp.concatenate(doh,axis=0)
        dqt=[jnp.zeros((128,2*SEG),F32)]*2
        own=[[jnp.zeros((128,SEG),F32)]*2]*2
        for c in chunks_of(trunk):
            pbs=[];dsbs=[]
            for h in range(2):
                st=score_chunk(c,trunk,k_ref,qh[h],meta)
                p=jnp.exp(st-lse_ref[0,h:h+1,:])
                if c<4:
                    dp=dg(v_ref[c*SEG:(c+1)*SEG,:],doh[h],NT)
                else:
                    base=4*SEG+(c-4)*2*SEG
                    dp=jnp.concatenate([dg(v_ref[base+i*SEG:base+(i+1)*SEG,:],doh[h][i*SEG:(i+1)*SEG,:],NT) for i in range(2)],axis=1)
                ds=p*(dp-delta[h])
                pbs.append(p.astype(BF)); dsbs.append(ds.astype(BF))
            if c<4:
                r=slice(c*SEG,(c+1)*SEG)
                dv_ref[r,:]=dg(jnp.concatenate(pbs,axis=1),docat,NN).astype(BF)
                dk_ref[r,:]=dg(jnp.concatenate(dsbs,axis=1),qcat,NN).astype(BF)
                for h in range(2): dqt[h]=dqt[h]+dg(kt[:,r],dsbs[h],NN)
            else:
                base=4*SEG+(c-4)*2*SEG
                for i in range(2):
                    r=slice(base+i*SEG,base+(i+1)*SEG); cc=slice(i*SEG,(i+1)*SEG)
                    dv_ref[r,:]=dg(jnp.concatenate([x[:,cc] for x in pbs],axis=1),jnp.concatenate([x[cc] for x in doh],axis=0),NN).astype(BF)
                    dk_ref[r,:]=dg(jnp.concatenate([x[:,cc] for x in dsbs],axis=1),jnp.concatenate([x[cc] for x in qh],axis=0),NN).astype(BF)
                own=[[own[h][i]+dg(kt[:,base+i*SEG:base+(i+1)*SEG],dsbs[h][:,i*SEG:(i+1)*SEG],NN) for i in range(2)] for h in range(2)]
        if trunk:
            dv_ref[4*SEG:,:]=jnp.zeros((4*SEG,128),BF)
            dk_ref[4*SEG:,:]=jnp.zeros((4*SEG,128),BF)
        dqt=[dqt[h]+jnp.concatenate(own[h],axis=1) for h in range(2)]
        row=lax.broadcasted_iota(jnp.int32,dqt[0].shape,0)
        dq_ref[...]=(jnp.where(row<64,dqt[0],dqt[1]).T*0.125).astype(BF)
    @pl.when(meta[0]>0)
    def _(): run(True)
    @pl.when(meta[0]==0)
    def _(): run(False)

def attn_fwd(meta,q,k,v,interpret=False):
    n=q.shape[1]//128; nk=k.shape[0]; nq=q.shape[0]
    gs=pltpu.PrefetchScalarGridSpec(num_scalar_prefetch=1,grid=(n,),
        in_specs=[pl.BlockSpec((nq,128),lambda j,m:(0,j)),pl.BlockSpec((nk,128),lambda j,m:(0,j)),pl.BlockSpec((nk,128),lambda j,m:(0,j))],
        out_specs=[pl.BlockSpec((nq,128),lambda j,m:(0,j)),pl.BlockSpec((1,2,nq),lambda j,m:(j,0,0))])
    return pl.pallas_call(fwd_kernel,grid_spec=gs,out_shape=[jax.ShapeDtypeStruct(q.shape,BF),jax.ShapeDtypeStruct((n,2,nq),F32)],
        cost_estimate=pl.CostEstimate(flops=2*2*12*256*256*256*12,bytes_accessed=8<<20,transcendentals=10<<20),
        compiler_params=pltpu.CompilerParams(vmem_limit_bytes=60<<20),interpret=interpret,name="attn_fwd")(meta,q,k,v)
def attn_bwd(meta,q,k,v,do,o,lse,interpret=False):
    n=q.shape[1]//128; nk=k.shape[0]; nq=q.shape[0]
    qs=pl.BlockSpec((nq,128),lambda j,m:(0,j)); ks=pl.BlockSpec((nk,128),lambda j,m:(0,j))
    gs=pltpu.PrefetchScalarGridSpec(num_scalar_prefetch=1,grid=(n,),
        in_specs=[qs,ks,ks,qs,qs,pl.BlockSpec((1,2,nq),lambda j,m:(j,0,0))],
        out_specs=[qs,ks,ks])
    return pl.pallas_call(bwd_kernel,grid_spec=gs,out_shape=[jax.ShapeDtypeStruct(q.shape,BF),jax.ShapeDtypeStruct(k.shape,BF),jax.ShapeDtypeStruct(k.shape,BF)],
        cost_estimate=pl.CostEstimate(flops=5*2*12*256*256*256*12,bytes_accessed=16<<20,transcendentals=10<<20),
        compiler_params=pltpu.CompilerParams(vmem_limit_bytes=60<<20),interpret=interpret,name="attn_bwd")(meta,q,k,v,do,o,lse)

SEGMENT_HALF = 2 * SEG


def normalise(values, scaling, shifting):
    centre = values - jnp.mean(values, axis=-1, keepdims=True)
    spread = jnp.mean(centre * centre, axis=-1, keepdims=True)
    scale = lax.rsqrt(spread + EPSILON)
    return centre * scale, scale


def norm_back(unit, scale, scaling, grad):
    scaled = grad * scaling
    mean_one = jnp.mean(scaled, axis=-1, keepdims=True)
    mean_two = jnp.mean(scaled * unit, axis=-1, keepdims=True)
    return scale * (scaled - mean_one - unit * mean_two)


def tree_body(
    tokens, parents, w_qkv, w_out, w_up, w_down, ln_gain, ln_bias, proj_bias, ff_bias, cotangent
):
    both = ("row", "col")
    col = lax.axis_index("col")
    rows = lax.axis_size("row")
    cols = lax.axis_size("col")
    local_rows = tokens.shape[0]
    all_tokens = lax.all_gather(tokens, "col", axis=0, tiled=True)
    vectors = jnp.concatenate(
        [ln_gain, ln_bias, proj_bias, ff_bias.reshape(-1, ln_gain.shape[1])], axis=0
    )
    vectors = lax.all_gather(vectors, "col", axis=0, tiled=False)
    small = vectors[:, :8].transpose(1, 0, 2).reshape(8, D).astype(jnp.float32)
    gains, shifts, biases = small[0:2], small[2:4], small[4:8]
    ff_shift = vectors[:, 8:].reshape(-1).astype(jnp.float32)

    def gathered(shard):
        blocks = lax.all_gather(shard, both, axis=0, tiled=False)
        a, b = shard.shape
        return blocks.reshape(rows, cols, a, b)

    blocks = gathered(w_qkv.T)
    qkv_t = blocks.transpose(1, 2, 0, 3).reshape(3 * D, D)
    blocks = gathered(w_out.T)
    out_t = blocks.transpose(1, 2, 0, 3).reshape(D, D)
    blocks = gathered(w_up)
    full_up = blocks.transpose(0, 2, 1, 3).reshape(D, -1)
    blocks = gathered(w_down.T)
    down_t = blocks.transpose(1, 2, 0, 3).reshape(D, -1)

    parent = parents[0]
    first = 2 * col
    own_parent = [jnp.maximum(parent[first + i], 0) for i in range(2)]
    is_leaf = [(own_parent[i] >= 4).astype(jnp.int32) for i in range(2)]
    meta = jnp.stack(
        [(col < 2).astype(jnp.int32), col.astype(jnp.int32) * local_rows, is_leaf[0], is_leaf[1]]
    )
    key_tokens = jnp.concatenate(
        [all_tokens[: 4 * SEG]]
        + [lax.dynamic_slice_in_dim(all_tokens, own_parent[i] * SEG, SEG, 0) for i in range(2)]
        + [tokens],
        axis=0,
    )
    unit_one, scale_one = normalise(key_tokens.astype(jnp.float32), None, None)
    normed = (unit_one * gains[0] + shifts[0]).astype(jnp.bfloat16)
    normed_own = normed[-local_rows:]
    queries = (
        lax.dot_general(
            normed_own, qkv_t[:D], (((1,), (1,)), ((), ())), preferred_element_type=jnp.float32
        )
        + biases[0]
    ).astype(jnp.bfloat16)
    key_rows = lax.dot_general(
        normed, qkv_t[D : 2 * D], (((1,), (1,)), ((), ())), preferred_element_type=jnp.float32
    ).astype(jnp.bfloat16)
    value_rows = (
        lax.dot_general(
            normed, qkv_t[2 * D :], (((1,), (1,)), ((), ())), preferred_element_type=jnp.float32
        )
        + biases[1]
    ).astype(jnp.bfloat16)
    attended_low, log_total = attn_fwd(meta, queries, key_rows, value_rows)

    inputs = tokens.astype(jnp.float32)
    mixed_rows = (
        inputs
        + lax.dot_general(
            attended_low, out_t, (((1,), (1,)), ((), ())), preferred_element_type=jnp.float32
        )
        + biases[2]
    )
    unit_two, scale_two = normalise(mixed_rows, None, None)
    second_low = (unit_two * gains[1] + shifts[1]).astype(jnp.bfloat16)
    hidden_pre = jnp.dot(second_low, full_up, preferred_element_type=jnp.float32) + ff_shift
    activated_low = exact_gelu(hidden_pre).astype(jnp.bfloat16)
    output = (
        mixed_rows
        + lax.dot_general(
            activated_low, down_t, (((1,), (1,)), ((), ())), preferred_element_type=jnp.float32
        )
        + biases[3]
    )
    upstream = cotangent.astype(jnp.float32)
    grad_down_t = jnp.einsum(
        "td,tf->df", cotangent, activated_low, preferred_element_type=jnp.float32
    )
    grad_act = jnp.dot(cotangent, down_t, preferred_element_type=jnp.float32)
    unused, gelu_back = jax.vjp(exact_gelu, hidden_pre)
    grad_pre = gelu_back(grad_act)[0]
    grad_pre_low = grad_pre.astype(jnp.bfloat16)
    grad_up = jnp.einsum("td,tf->df", second_low, grad_pre_low, preferred_element_type=jnp.float32)
    grad_second = jnp.einsum("tf,df->td", grad_pre_low, full_up, preferred_element_type=jnp.float32)
    grad_mixed = upstream + norm_back(unit_two, scale_two, gains[1], grad_second)
    grad_mixed_low = grad_mixed.astype(jnp.bfloat16)
    grad_out_t = jnp.einsum(
        "te,td->ed", grad_mixed_low, attended_low, preferred_element_type=jnp.float32
    )
    grad_att_low = jnp.dot(grad_mixed_low, out_t, preferred_element_type=jnp.float32).astype(
        jnp.bfloat16
    )
    grad_q, grad_k, grad_v = attn_bwd(
        meta, queries, key_rows, value_rows, grad_att_low, attended_low, log_total
    )
    grad_normed = jnp.dot(grad_k, qkv_t[D : 2 * D], preferred_element_type=jnp.float32) + jnp.dot(
        grad_v, qkv_t[2 * D :], preferred_element_type=jnp.float32
    )
    part = grad_normed.astype(jnp.bfloat16)
    spread_out = jnp.zeros((cols * local_rows, D), jnp.bfloat16)
    spread_out = lax.dynamic_update_slice_in_dim(spread_out, part[: 4 * SEG], 0, 0)
    for i in range(2):
        start = own_parent[i] * SEG
        piece = part[4 * SEG + i * SEG : 5 * SEG + i * SEG]
        earlier = lax.dynamic_slice_in_dim(spread_out, start, SEG, 0)
        spread_out = lax.dynamic_update_slice_in_dim(spread_out, earlier + piece, start, 0)
    received = lax.psum_scatter(spread_out, "col", scatter_dimension=0, tiled=True)
    grad_normed_own = (
        grad_normed[-local_rows:]
        + jnp.dot(grad_q, qkv_t[:D], preferred_element_type=jnp.float32)
        + received.astype(jnp.float32)
    )
    grad_qkv_t = jnp.concatenate(
        [
            jnp.einsum("te,td->ed", grad_q, normed_own, preferred_element_type=jnp.float32),
            jnp.einsum("te,td->ed", grad_k, normed, preferred_element_type=jnp.float32),
            jnp.einsum("te,td->ed", grad_v, normed, preferred_element_type=jnp.float32),
        ],
        axis=0,
    )
    unit_own, scale_own = unit_one[-local_rows:], scale_one[-local_rows:]
    grad_tokens = (
        grad_mixed + norm_back(unit_own, scale_own, gains[0], grad_normed_own)
    ).astype(jnp.bfloat16)

    def scattered(blocks):
        return lax.psum_scatter(
            blocks.astype(jnp.bfloat16), both, scatter_dimension=0, tiled=True
        ).astype(jnp.float32)

    def split_out(array, row_dim, col_dim):
        a, b = array.shape
        if row_dim == 1:
            return array.reshape(cols, a // cols, rows, b // rows).transpose(2, 0, 1, 3)
        return array.reshape(rows, a // rows, cols, b // cols).transpose(0, 2, 1, 3)

    def reduced(array, row_dim, col_dim):
        blocks = split_out(array.astype(jnp.bfloat16), row_dim, col_dim)
        r, c, a, b = blocks.shape
        return scattered(blocks.reshape(r * c * a, b))

    grad_w_down = reduced(grad_down_t, 1, 0).T
    grad_w_up = reduced(grad_up, 0, 1)
    grad_w_out = reduced(grad_out_t, 1, 0).T
    grad_w_qkv = reduced(grad_qkv_t, 1, 0).T

    terms = jnp.concatenate(
        [
            jnp.sum(grad_normed_own * unit_own, axis=0),
            jnp.sum(grad_second * unit_two, axis=0),
            jnp.sum(grad_normed_own, axis=0),
            jnp.sum(grad_second, axis=0),
            jnp.sum(grad_q.astype(jnp.float32), axis=0),
            jnp.sum(grad_v.astype(jnp.float32), axis=0),
            jnp.sum(grad_mixed, axis=0),
            jnp.sum(upstream, axis=0),
            jnp.sum(grad_pre, axis=0),
        ]
    )
    terms = lax.psum(terms, both)
    small = terms[: 8 * D].reshape(8, cols, D // cols)
    small = lax.dynamic_slice_in_dim(small, col, 1, 1)[:, 0]
    ff_len = ff_bias.shape[0]
    grad_ff = lax.dynamic_slice_in_dim(terms[8 * D :], col * ff_len, ff_len, 0)
    return (
        output.astype(jnp.bfloat16),
        grad_tokens,
        grad_w_qkv,
        grad_w_out,
        grad_w_up,
        grad_w_down,
        small[0:2],
        small[2:4],
        small[4:8],
        grad_ff,
    )


def solution(mesh):
    fits = mesh.shape["col"] * 2 == SEGS
    body = tree_body if fits else plain_body
    return jax.shard_map(
        body,
        mesh=mesh,
        in_specs=(
            P(("row", "col"), None),
            P("row", None),
            P("row", "col"),
            P("row", "col"),
            P("row", "col"),
            P("row", "col"),
            P(None, "col"),
            P(None, "col"),
            P(None, "col"),
            P("col"),
            P(("row", "col"), None),
        ),
        out_specs=(
            P(("row", "col"), None),
            P(("row", "col"), None),
            P("row", "col"),
            P("row", "col"),
            P("row", "col"),
            P("row", "col"),
            P(None, "col"),
            P(None, "col"),
            P(None, "col"),
            P("col"),
        ),
        check_vma=False,
    )
```

```python
import jax
import jax.numpy as jnp
from jax import lax
from jax.experimental import pallas as pl
from jax.experimental.pallas import tpu as pltpu
from jax.sharding import PartitionSpec as P

D = 768
HEADS = 12
HEAD_DIM = 64
SEG = 256
SEGS = 16
TREE_TOKENS = 4096


EPSILON = 1e-12
NEGATIVE = -1e30


def layer_norm(values, scaling, shifting):
    centre = values - jnp.mean(values, axis=-1, keepdims=True)
    spread = jnp.mean(centre * centre, axis=-1, keepdims=True)
    return centre * lax.rsqrt(spread + EPSILON) * scaling + shifting


def exact_gelu(values):
    return jax.nn.gelu(values, approximate=False)


def ancestry(parents):
    segment_count = parents.shape[0]
    labels = jnp.arange(segment_count, dtype=jnp.int32)
    closure = jnp.eye(segment_count, dtype=jnp.float32) + (
        parents[:, None] == labels[None, :]
    ).astype(jnp.float32)
    for repeat in range(segment_count.bit_length()):
        closure = jnp.minimum(jnp.dot(closure, closure, precision=lax.Precision.HIGHEST), 1.0)
    return closure


def allowed(query_pos, key_pos, closure):
    labels = jnp.arange(closure.shape[0], dtype=jnp.int32)
    query_seg = query_pos // SEG
    key_seg = key_pos // SEG
    query_hot = (query_seg[:, None] == labels[None, :]).astype(jnp.float32)
    key_hot = (key_seg[:, None] == labels[None, :]).astype(jnp.float32)
    reach = jnp.dot(
        jnp.dot(query_hot, closure, precision=lax.Precision.HIGHEST),
        key_hot.T,
        precision=lax.Precision.HIGHEST,
    )
    causal = (query_seg[:, None] != key_seg[None, :]) | (key_pos[None, :] <= query_pos[:, None])
    return (reach > 0.5) & causal


def plain_body(
    tokens, parents, w_qkv, w_out, w_up, w_down, ln_gain, ln_bias, proj_bias, ff_bias, cotangent
):
    local_rows = tokens.shape[0]
    score_scale = HEAD_DIM ** (-0.5)
    head_shape = (local_rows, HEADS, HEAD_DIM)
    block_rows = 2 * SEG
    block_count = SEGS // 2
    cols_qkv, cols_out, cols_up, cols_down, norm_gains, shifts, biases, ff_shift = (
        lax.all_gather(w_qkv, "col", axis=1, tiled=True),
        lax.all_gather(w_out, "col", axis=1, tiled=True),
        lax.all_gather(w_up, "col", axis=1, tiled=True),
        lax.all_gather(w_down, "col", axis=1, tiled=True),
        lax.all_gather(ln_gain, "col", axis=1, tiled=True),
        lax.all_gather(ln_bias, "col", axis=1, tiled=True),
        lax.all_gather(proj_bias, "col", axis=1, tiled=True),
        lax.all_gather(ff_bias, "col", axis=0, tiled=True),
    )
    full_qkv, full_out, full_up, full_down = (
        lax.all_gather(cols_qkv, "row", axis=0, tiled=True),
        lax.all_gather(cols_out, "row", axis=0, tiled=True),
        lax.all_gather(cols_up, "row", axis=0, tiled=True),
        lax.all_gather(cols_down, "row", axis=0, tiled=True),
    )
    norm_gains = norm_gains.astype(jnp.float32)
    shifts = shifts.astype(jnp.float32)
    biases = biases.astype(jnp.float32)
    ff_shift = ff_shift.astype(jnp.float32)
    inputs = tokens.astype(jnp.float32)
    normed_low = layer_norm(inputs, norm_gains[0], shifts[0]).astype(jnp.bfloat16)
    projected = jnp.dot(normed_low, full_qkv, preferred_element_type=jnp.float32)
    queries = (projected[:, :D] + biases[0]).astype(jnp.bfloat16).reshape(head_shape)
    keys_own = projected[:, D : 2 * D].astype(jnp.bfloat16).reshape(head_shape)
    values_own = (projected[:, 2 * D :] + biases[1]).astype(jnp.bfloat16).reshape(head_shape)
    keys_all, values_all = (
        lax.all_gather(keys_own, "col", axis=0, tiled=True),
        lax.all_gather(values_own, "col", axis=0, tiled=True),
    )
    key_blocks = keys_all.reshape(block_count, block_rows, HEADS, HEAD_DIM)
    value_blocks = values_all.reshape(block_count, block_rows, HEADS, HEAD_DIM)
    block_starts = jnp.arange(block_count, dtype=jnp.int32) * block_rows
    within = jnp.arange(block_rows, dtype=jnp.int32)
    query_pos = lax.axis_index("col") * local_rows + jnp.arange(local_rows, dtype=jnp.int32)
    closure = ancestry(parents[0])

    def scores_of(query_block, key_block, query_positions, key_positions):
        products = jnp.einsum(
            "qhd,khd->hqk", query_block, key_block, preferred_element_type=jnp.float32
        )
        return (products * score_scale, allowed(query_positions, key_positions, closure)[None])

    def probabilities(query_block, key_block, query_positions, key_positions, log_block):
        scores, visible = scores_of(query_block, key_block, query_positions, key_positions)
        return jnp.where(visible, jnp.exp(scores - log_block[..., None]), 0.0)

    def extent(running, pieces):
        highest_score, mass_total = running
        key_block, first_pos = pieces
        scores, visible = scores_of(queries, key_block, query_pos, first_pos + within)
        masked = jnp.where(visible, scores, NEGATIVE)
        new_highest = jnp.maximum(highest_score, jnp.max(masked, axis=-1))
        exp_terms = jnp.where(visible, jnp.exp(masked - new_highest[..., None]), 0.0)
        new_total = mass_total * jnp.exp(highest_score - new_highest) + jnp.sum(exp_terms, axis=-1)
        return ((new_highest, new_total), None)

    start_state = (
        jnp.full((HEADS, local_rows), NEGATIVE, jnp.float32),
        jnp.zeros((HEADS, local_rows), jnp.float32),
    )
    (highest_score, mass_total), unused = lax.scan(extent, start_state, (key_blocks, block_starts))
    log_total = highest_score + jnp.log(mass_total)

    def attend(running, pieces):
        key_block, value_block, first_pos = pieces
        chances = probabilities(
            queries, key_block, query_pos, first_pos + within, log_total
        ).astype(jnp.bfloat16)
        return (
            running
            + jnp.einsum("hqk,khd->qhd", chances, value_block, preferred_element_type=jnp.float32),
            None,
        )

    attended, unused = lax.scan(
        attend, jnp.zeros(head_shape, jnp.float32), (key_blocks, value_blocks, block_starts)
    )
    attended_low = attended.reshape(local_rows, D).astype(jnp.bfloat16)
    mixed_rows = (
        inputs + jnp.dot(attended_low, full_out, preferred_element_type=jnp.float32) + biases[2]
    )
    second_low = layer_norm(mixed_rows, norm_gains[1], shifts[1]).astype(jnp.bfloat16)
    hidden_pre = jnp.dot(second_low, full_up, preferred_element_type=jnp.float32) + ff_shift
    activated_low = exact_gelu(hidden_pre).astype(jnp.bfloat16)
    output = (
        mixed_rows
        + jnp.dot(activated_low, full_down, preferred_element_type=jnp.float32)
        + biases[3]
    )
    upstream = cotangent.astype(jnp.float32)
    grad_down = jnp.einsum(
        "tf,td->fd", activated_low, cotangent, preferred_element_type=jnp.float32
    )
    grad_act = jnp.einsum("td,fd->tf", cotangent, full_down, preferred_element_type=jnp.float32)
    unused, gelu_back = jax.vjp(exact_gelu, hidden_pre)
    grad_pre = gelu_back(grad_act)[0]
    grad_pre_low = grad_pre.astype(jnp.bfloat16)
    grad_up = jnp.einsum("td,tf->df", second_low, grad_pre_low, preferred_element_type=jnp.float32)
    grad_second = jnp.einsum("tf,df->td", grad_pre_low, full_up, preferred_element_type=jnp.float32)
    unused, second_back = jax.vjp(layer_norm, mixed_rows, norm_gains[1], shifts[1])
    grad_mixed_norm, grad_gain_two, grad_shift_two = second_back(grad_second)
    grad_mixed = upstream + grad_mixed_norm
    grad_mixed_low = grad_mixed.astype(jnp.bfloat16)
    grad_out = jnp.einsum(
        "td,te->de", attended_low, grad_mixed_low, preferred_element_type=jnp.float32
    )
    grad_att_low = (
        jnp.einsum("te,de->td", grad_mixed_low, full_out, preferred_element_type=jnp.float32)
        .astype(jnp.bfloat16)
        .reshape(head_shape)
    )
    deltas = jnp.einsum("qhd,qhd->hq", grad_att_low.astype(jnp.float32), attended)

    def score_grads(
        query_block,
        key_block,
        value_block,
        grad_block,
        query_positions,
        key_positions,
        log_block,
        delta_block,
    ):
        chances = probabilities(query_block, key_block, query_positions, key_positions, log_block)
        grad_chances = jnp.einsum(
            "qhd,khd->hqk", grad_block, value_block, preferred_element_type=jnp.float32
        )
        grad_scores = (chances * (grad_chances - delta_block[..., None]) * score_scale).astype(
            jnp.bfloat16
        )
        return (chances.astype(jnp.bfloat16), grad_scores)

    def backward_block(running, pieces):
        key_block, value_block, first_pos = pieces
        chances_low, grad_scores = score_grads(
            queries,
            key_block,
            value_block,
            grad_att_low,
            query_pos,
            first_pos + within,
            log_total,
            deltas,
        )
        running = running + jnp.einsum(
            "hqk,khd->qhd", grad_scores, key_block, preferred_element_type=jnp.float32
        )
        key_term = jnp.einsum(
            "hqk,qhd->khd", grad_scores, queries, preferred_element_type=jnp.float32
        )
        value_term = jnp.einsum(
            "hqk,qhd->khd", chances_low, grad_att_low, preferred_element_type=jnp.float32
        )
        return (running, (key_term, value_term))

    grad_queries, (key_terms, value_terms) = lax.scan(
        backward_block, jnp.zeros(head_shape, jnp.float32), (key_blocks, value_blocks, block_starts)
    )
    grad_keys, grad_values = (
        lax.psum_scatter(
            key_terms.reshape(TREE_TOKENS, D).astype(jnp.bfloat16),
            "col",
            scatter_dimension=0,
            tiled=True,
        ).astype(jnp.float32),
        lax.psum_scatter(
            value_terms.reshape(TREE_TOKENS, D).astype(jnp.bfloat16),
            "col",
            scatter_dimension=0,
            tiled=True,
        ).astype(jnp.float32),
    )
    grad_queries = grad_queries.reshape(local_rows, D)
    grad_projected_low = jnp.concatenate([grad_queries, grad_keys, grad_values], axis=1).astype(
        jnp.bfloat16
    )
    grad_qkv = jnp.einsum(
        "td,te->de", normed_low, grad_projected_low, preferred_element_type=jnp.float32
    )
    grad_normed = jnp.einsum(
        "te,de->td", grad_projected_low, full_qkv, preferred_element_type=jnp.float32
    )
    unused, first_back = jax.vjp(layer_norm, inputs, norm_gains[0], shifts[0])
    grad_input_norm, grad_gain_one, grad_shift_one = first_back(grad_normed)
    grad_tokens = (grad_mixed + grad_input_norm).astype(jnp.bfloat16)
    gain_terms = jnp.stack([grad_gain_one, grad_gain_two])
    shift_terms = jnp.stack([grad_shift_one, grad_shift_two])
    bias_terms = jnp.stack(
        [
            jnp.sum(grad_queries, axis=0),
            jnp.sum(grad_values, axis=0),
            jnp.sum(grad_mixed, axis=0),
            jnp.sum(upstream, axis=0),
        ]
    )
    ff_terms = jnp.sum(grad_pre, axis=0)
    part_qkv, part_out, part_up, part_down, part_gain, part_shift, part_bias, part_ff = (
        lax.psum_scatter(
            grad_qkv.astype(jnp.bfloat16), "col", scatter_dimension=1, tiled=True
        ).astype(jnp.float32),
        lax.psum_scatter(
            grad_out.astype(jnp.bfloat16), "col", scatter_dimension=1, tiled=True
        ).astype(jnp.float32),
        lax.psum_scatter(
            grad_up.astype(jnp.bfloat16), "col", scatter_dimension=1, tiled=True
        ).astype(jnp.float32),
        lax.psum_scatter(
            grad_down.astype(jnp.bfloat16), "col", scatter_dimension=1, tiled=True
        ).astype(jnp.float32),
        lax.psum_scatter(
            gain_terms.astype(jnp.bfloat16), "col", scatter_dimension=1, tiled=True
        ).astype(jnp.float32),
        lax.psum_scatter(
            shift_terms.astype(jnp.bfloat16), "col", scatter_dimension=1, tiled=True
        ).astype(jnp.float32),
        lax.psum_scatter(
            bias_terms.astype(jnp.bfloat16), "col", scatter_dimension=1, tiled=True
        ).astype(jnp.float32),
        lax.psum_scatter(
            ff_terms.astype(jnp.bfloat16), "col", scatter_dimension=0, tiled=True
        ).astype(jnp.float32),
    )
    grad_w_qkv, grad_w_out, grad_w_up, grad_w_down = (
        lax.psum_scatter(
            part_qkv.astype(jnp.bfloat16), "row", scatter_dimension=0, tiled=True
        ).astype(jnp.float32),
        lax.psum_scatter(
            part_out.astype(jnp.bfloat16), "row", scatter_dimension=0, tiled=True
        ).astype(jnp.float32),
        lax.psum_scatter(
            part_up.astype(jnp.bfloat16), "row", scatter_dimension=0, tiled=True
        ).astype(jnp.float32),
        lax.psum_scatter(
            part_down.astype(jnp.bfloat16), "row", scatter_dimension=0, tiled=True
        ).astype(jnp.float32),
    )
    grad_gain, grad_shift, grad_bias, grad_ff = lax.psum(
        (part_gain, part_shift, part_bias, part_ff), "row"
    )
    return (
        output.astype(jnp.bfloat16),
        grad_tokens,
        grad_w_qkv,
        grad_w_out,
        grad_w_up,
        grad_w_down,
        grad_gain,
        grad_shift,
        grad_bias,
        grad_ff,
    )


F32=jnp.float32; BF=jnp.bfloat16
NEG=NEGATIVE
NT=(((1,),(1,)),((),()))
NN=(((1,),(0,)),((),()))
def dg(a,b,dims): return lax.dot_general(a,b,dims,preferred_element_type=F32)

def chunks_of(trunk):
    return [0,1,2,3] if trunk else [0,1,2,3,4,5]

def score_chunk(c, trunk, k_ref, qh, meta):
    if c<4:
        st=dg(k_ref[c*SEG:(c+1)*SEG,:], qh, NT)
        if trunk:
            kp=(c^meta[4])*SEG+lax.broadcasted_iota(jnp.int32,(SEG,2*SEG),0)
            qp=meta[1]+lax.broadcasted_iota(jnp.int32,(SEG,2*SEG),1)
            st=jnp.where(kp<=qp,st,NEG)
        return st
    base=4*SEG+(c-4)*2*SEG
    parts=[]
    for i in range(2):
        s=dg(k_ref[base+i*SEG:base+(i+1)*SEG,:], qh[i*SEG:(i+1)*SEG,:], NT)
        if c==4:
            s=s+jnp.where(meta[2+i]>0,0.0,NEG).astype(F32)
        else:
            kp=lax.broadcasted_iota(jnp.int32,(SEG,SEG),0)
            qp=lax.broadcasted_iota(jnp.int32,(SEG,SEG),1)
            s=jnp.where(kp<=qp,s,NEG)
        parts.append(s)
    return jnp.concatenate(parts,axis=1)

def fwd_kernel(meta, q_ref,k_ref,v_ref,o_ref,lse_ref):
    def run(trunk):
        q=q_ref[...]*jnp.asarray(0.125,BF)
        lane=lax.broadcasted_iota(jnp.int32,q.shape,1)
        vt=v_ref[...].T
        res=[]
        for h in range(2):
            qh=jnp.where((lane<64)==(h==0),q,jnp.asarray(0,BF))
            cs=chunks_of(trunk)
            st=[score_chunk(c,trunk,k_ref,qh,meta) for c in cs]
            m=st[0]
            for s in st[1:]: m=jnp.maximum(m,s)
            m=jnp.max(m,axis=0,keepdims=True)
            l=jnp.zeros((1,2*SEG),F32);
            ot=jnp.zeros((128,2*SEG),F32); own=[jnp.zeros((128,SEG),F32)]*2
            for c,s in zip(cs,st):
                p=jnp.exp(s-m)
                l=l+jnp.sum(p,axis=0,keepdims=True)
                pb=p.astype(BF)
                if c<4:
                    ot=ot+dg(vt[:,c*SEG:(c+1)*SEG],pb,NN)
                else:
                    base=4*SEG+(c-4)*2*SEG
                    own=[own[i]+dg(vt[:,base+i*SEG:base+(i+1)*SEG],pb[:,i*SEG:(i+1)*SEG],NN) for i in range(2)]
            ot=(ot+jnp.concatenate(own,axis=1))*(1.0/l)
            res.append(ot)
            lse_ref[0,h:h+1,:]=m+jnp.log(l)
        row=lax.broadcasted_iota(jnp.int32,res[0].shape,0)
        o_ref[...]=jnp.where(row<64,res[0],res[1]).T.astype(BF)
    @pl.when(meta[0]>0)
    def _(): run(True)
    @pl.when(meta[0]==0)
    def _(): run(False)

def bwd_kernel(meta, q_ref,k_ref,v_ref,do_ref,o_ref,lse_ref,dq_ref,dk_ref,dv_ref):
    def run(trunk):
        q=q_ref[...]*jnp.asarray(0.125,BF)
        do=do_ref[...]
        lane=lax.broadcasted_iota(jnp.int32,q.shape,1)
        zero=jnp.asarray(0,BF)
        dd=(do.astype(F32)*o_ref[...].astype(F32)).T
        kt=k_ref[...].T
        qh=[jnp.where((lane<64)==(h==0),q,zero) for h in range(2)]
        doh=[jnp.where((lane<64)==(h==0),do,zero) for h in range(2)]
        delta=[jnp.sum(dd[h*64:(h+1)*64],axis=0,keepdims=True) for h in range(2)]
        qcat=jnp.concatenate(qh,axis=0); docat=jnp.concatenate(doh,axis=0)
        dqt=[jnp.zeros((128,2*SEG),F32)]*2
        own=[[jnp.zeros((128,SEG),F32)]*2]*2
        for c in chunks_of(trunk):
            pbs=[];dsbs=[]
            for h in range(2):
                st=score_chunk(c,trunk,k_ref,qh[h],meta)
                p=jnp.exp(st-lse_ref[0,h:h+1,:])
                if c<4:
                    dp=dg(v_ref[c*SEG:(c+1)*SEG,:],doh[h],NT)
                else:
                    base=4*SEG+(c-4)*2*SEG
                    dp=jnp.concatenate([dg(v_ref[base+i*SEG:base+(i+1)*SEG,:],doh[h][i*SEG:(i+1)*SEG,:],NT) for i in range(2)],axis=1)
                ds=p*(dp-delta[h])
                pbs.append(p.astype(BF)); dsbs.append(ds.astype(BF))
            if c<4:
                r=slice(c*SEG,(c+1)*SEG)
                dv_ref[r,:]=dg(jnp.concatenate(pbs,axis=1),docat,NN).astype(BF)
                dk_ref[r,:]=dg(jnp.concatenate(dsbs,axis=1),qcat,NN).astype(BF)
                for h in range(2): dqt[h]=dqt[h]+dg(kt[:,r],dsbs[h],NN)
            else:
                base=4*SEG+(c-4)*2*SEG
                for i in range(2):
                    r=slice(base+i*SEG,base+(i+1)*SEG); cc=slice(i*SEG,(i+1)*SEG)
                    dv_ref[r,:]=dg(jnp.concatenate([x[:,cc] for x in pbs],axis=1),jnp.concatenate([x[cc] for x in doh],axis=0),NN).astype(BF)
                    dk_ref[r,:]=dg(jnp.concatenate([x[:,cc] for x in dsbs],axis=1),jnp.concatenate([x[cc] for x in qh],axis=0),NN).astype(BF)
                own=[[own[h][i]+dg(kt[:,base+i*SEG:base+(i+1)*SEG],dsbs[h][:,i*SEG:(i+1)*SEG],NN) for i in range(2)] for h in range(2)]
        if trunk:
            dv_ref[4*SEG:,:]=jnp.zeros((4*SEG,128),BF)
            dk_ref[4*SEG:,:]=jnp.zeros((4*SEG,128),BF)
        dqt=[dqt[h]+jnp.concatenate(own[h],axis=1) for h in range(2)]
        row=lax.broadcasted_iota(jnp.int32,dqt[0].shape,0)
        dq_ref[...]=(jnp.where(row<64,dqt[0],dqt[1]).T*0.125).astype(BF)
    @pl.when(meta[0]>0)
    def _(): run(True)
    @pl.when(meta[0]==0)
    def _(): run(False)

def attn_fwd(meta,q,k,v,interpret=False):
    n=q.shape[1]//128; nk=k.shape[0]; nq=q.shape[0]
    gs=pltpu.PrefetchScalarGridSpec(num_scalar_prefetch=1,grid=(n,),
        in_specs=[pl.BlockSpec((nq,128),lambda j,m:(0,j)),pl.BlockSpec((nk,128),lambda j,m:(0,j)),pl.BlockSpec((nk,128),lambda j,m:(0,j))],
        out_specs=[pl.BlockSpec((nq,128),lambda j,m:(0,j)),pl.BlockSpec((1,2,nq),lambda j,m:(j,0,0))])
    return pl.pallas_call(fwd_kernel,grid_spec=gs,out_shape=[jax.ShapeDtypeStruct(q.shape,BF),jax.ShapeDtypeStruct((n,2,nq),F32)],
        cost_estimate=pl.CostEstimate(flops=2*2*12*256*256*256*12,bytes_accessed=8<<20,transcendentals=10<<20),
        compiler_params=pltpu.CompilerParams(vmem_limit_bytes=60<<20),interpret=interpret,name="attn_fwd")(meta,q,k,v)
def attn_bwd(meta,q,k,v,do,o,lse,interpret=False):
    n=q.shape[1]//128; nk=k.shape[0]; nq=q.shape[0]
    qs=pl.BlockSpec((nq,128),lambda j,m:(0,j)); ks=pl.BlockSpec((nk,128),lambda j,m:(0,j))
    gs=pltpu.PrefetchScalarGridSpec(num_scalar_prefetch=1,grid=(n,),
        in_specs=[qs,ks,ks,qs,qs,pl.BlockSpec((1,2,nq),lambda j,m:(j,0,0))],
        out_specs=[qs,ks,ks])
    return pl.pallas_call(bwd_kernel,grid_spec=gs,out_shape=[jax.ShapeDtypeStruct(q.shape,BF),jax.ShapeDtypeStruct(k.shape,BF),jax.ShapeDtypeStruct(k.shape,BF)],
        cost_estimate=pl.CostEstimate(flops=5*2*12*256*256*256*12,bytes_accessed=16<<20,transcendentals=10<<20),
        compiler_params=pltpu.CompilerParams(vmem_limit_bytes=60<<20),interpret=interpret,name="attn_bwd")(meta,q,k,v,do,o,lse)


def row_norm(values):
    centre = values - jnp.mean(values, axis=-1, keepdims=True)
    spread = jnp.mean(centre * centre, axis=-1, keepdims=True)
    scale = lax.rsqrt(spread + EPSILON)
    return centre * scale, scale


def row_norm_back(unit, scale, scaled):
    mean_one = jnp.mean(scaled, axis=-1, keepdims=True)
    mean_two = jnp.mean(scaled * unit, axis=-1, keepdims=True)
    return scale * (scaled - mean_one - unit * mean_two)


def call(kernel, name, grid, ins, outs, scratch=(), prefetch=0, flops=0, size=16 << 20, args=()):
    grid_spec = pltpu.PrefetchScalarGridSpec(
        num_scalar_prefetch=prefetch,
        grid=grid,
        in_specs=ins,
        out_specs=[spec for spec, unused in outs],
        scratch_shapes=list(scratch),
    )
    return pl.pallas_call(
        kernel,
        grid_spec=grid_spec,
        out_shape=[jax.ShapeDtypeStruct(*shape) for unused, shape in outs],
        cost_estimate=pl.CostEstimate(flops=flops, bytes_accessed=size, transcendentals=0),
        compiler_params=pltpu.CompilerParams(vmem_limit_bytes=58 << 20),
        name=name,
    )(*args)


def whole(shape):
    return pl.BlockSpec(shape, lambda *unused: (0,) * len(shape))


def join_kernel(pieces_ref, qkv_ref, out_ref):
    cols = pieces_ref.shape[1]
    cut = qkv_ref.shape[1] // cols
    qkv_ref[...] = jnp.concatenate([pieces_ref[0, c, :, :cut] for c in range(cols)], axis=1)
    out_ref[...] = jnp.concatenate([pieces_ref[0, c, :, cut:] for c in range(cols)], axis=1)


def join_pieces(pieces, height):
    rows, cols, unused, width = pieces.shape
    full = rows * height
    return call(
        join_kernel,
        "join_pieces",
        (rows,),
        [pl.BlockSpec((1, cols, height, width), lambda r: (r, 0, 1, 0))],
        [
            (pl.BlockSpec((height, 3 * full), lambda r: (r, 0)), ((full, 3 * full), BF)),
            (pl.BlockSpec((height, full), lambda r: (r, 0)), ((full, full), BF)),
        ],
        args=(pieces,),
    )


def project_kernel(a_ref, b_ref, c_ref, d_ref, small_ref, weight_ref, q_ref, k_ref, v_ref, n_ref):
    step = pl.program_id(0)
    width = a_ref.shape[1]

    def run(ref, last):
        unit, unused = row_norm(ref[...].astype(F32))
        normed = (unit * small_ref[0:1] + small_ref[2:3]).astype(BF)
        n_ref[...] = normed
        k_ref[...] = dg(normed, weight_ref[:, width : 2 * width], NN).astype(BF)
        v_ref[...] = (dg(normed, weight_ref[:, 2 * width :], NN) + small_ref[5:6]).astype(BF)
        if last:
            q_ref[...] = (dg(normed, weight_ref[:, :width], NN) + small_ref[4:5]).astype(BF)

    for i, ref in enumerate((a_ref, b_ref, c_ref, d_ref)):

        @pl.when(step == i)
        def _(ref=ref, i=i):
            run(ref, i == 3)


def project(sources, small, qkv):
    tokens, width = sources[0].shape
    block = pl.BlockSpec((tokens, width), lambda i: (i, 0))
    tall = ((4 * tokens, width), BF)
    return call(
        project_kernel,
        "project",
        (4,),
        [whole((tokens, width))] * 4 + [whole(small.shape), whole(qkv.shape)],
        [(whole((tokens, width)), ((tokens, width), BF)), (block, tall), (block, tall), (block, tall)],
        flops=2 * 9 * tokens * width * width,
        args=(*sources, small, qkv),
    )


def unproject_kernel(a_ref, b_ref, c_ref, dk_ref, dv_ref, small_ref, weight_ref, part_ref, terms_ref):
    step = pl.program_id(0)
    width = a_ref.shape[1]

    @pl.when(step == 0)
    def _():
        terms_ref[...] = jnp.zeros_like(terms_ref)

    dk, dv = dk_ref[...], dv_ref[...]
    grad = dg(dk, weight_ref[:, width : 2 * width], NT) + dg(dv, weight_ref[:, 2 * width :], NT)
    part_ref[...] = grad.astype(BF)
    terms_ref[1:2] += jnp.sum(grad, axis=0, keepdims=True)
    terms_ref[2:3] += jnp.sum(dv.astype(F32), axis=0, keepdims=True)
    for i, ref in enumerate((a_ref, b_ref, c_ref)):

        @pl.when(step == i)
        def _(ref=ref):
            unit, unused = row_norm(ref[...].astype(F32))
            terms_ref[0:1] += jnp.sum(grad * unit, axis=0, keepdims=True)


def unproject(sources, dk, dv, small, qkv):
    tokens, width = sources[0].shape
    block = pl.BlockSpec((tokens, width), lambda i: (i, 0))
    return call(
        unproject_kernel,
        "unproject",
        (3,),
        [whole((tokens, width))] * 3 + [block, block, whole(small.shape), whole(qkv.shape)],
        [(block, ((3 * tokens, width), BF)), (whole((8, width)), ((8, width), F32))],
        flops=2 * 6 * tokens * width * width,
        args=(*sources, dk, dv, small, qkv),
    )


def weigh_kernel(
    me, dq_ref, dk_ref, dv_ref, n_ref, tokens_ref, grad_out_ref, weight_ref,
    own_ref, other_ref, grad_ref, terms_ref, kept, turned,
):
    step = pl.program_id(0)
    tokens, width = dq_ref.shape

    @pl.when(step == 0)
    def _():
        dq, dk, dv = dq_ref[...], dk_ref[-tokens:], dv_ref[-tokens:]
        grad = (
            dg(dq, weight_ref[:, :width], NT)
            + dg(dk, weight_ref[:, width : 2 * width], NT)
            + dg(dv, weight_ref[:, 2 * width :], NT)
        )
        grad_ref[...] = grad
        unit, unused = row_norm(tokens_ref[...].astype(F32))
        terms_ref[...] = jnp.zeros_like(terms_ref)
        terms_ref[0:1] = jnp.sum(grad * unit, axis=0, keepdims=True)
        terms_ref[1:2] = jnp.sum(grad, axis=0, keepdims=True)
        terms_ref[2:3] = jnp.sum(dv.astype(F32), axis=0, keepdims=True)
        terms_ref[3:4] = jnp.sum(dq.astype(F32), axis=0, keepdims=True)
        turned[...] = n_ref[...].T
        kept[:, :width] = dg(turned[:, -tokens:], dq, NN).astype(BF)

    @pl.when(step == 1)
    def _():
        kept[:, width : 2 * width] = dg(turned[...], dk_ref[...], NN).astype(BF)

    @pl.when(step == 2)
    def _():
        kept[:, 2 * width :] = dg(turned[...], dv_ref[...], NN).astype(BF)
        height = own_ref.shape[1]
        cols = own_ref.shape[0] // 2
        tall, low_part = 3 * width // cols, width // cols
        for c in range(cols):
            parts = [
                jnp.concatenate(
                    [
                        kept[r * height : (r + 1) * height, c * tall : (c + 1) * tall],
                        grad_out_ref[r * height : (r + 1) * height, c * low_part : (c + 1) * low_part],
                    ],
                    axis=1,
                )
                for r in range(4)
            ]
            a, c_part = in_order(me[1], parts[0], parts[2])
            b, d_part = in_order(me[1], parts[1], parts[3])
            for y_step, pair in ((0, (a, b)), (1, (c_part, d_part))):
                mine, theirs = in_order(me[2], *pair)
                own_ref[place_of(c, y_step, me[2], me)] = mine
                other_ref[place_of(c, y_step, me[2] ^ 1, me)] = theirs


def weigh(me, dq, dk, dv, normed, tokens, grad_out, qkv, cols):
    count, width = dq.shape
    shape = (2 * cols, width // 4, 4 * width // cols)
    return call(
        weigh_kernel,
        "weigh",
        (3,),
        [whole(x.shape) for x in (dq, dk, dv, normed, tokens, grad_out, qkv)],
        [
            (whole(shape), (shape, BF)),
            (whole(shape), (shape, BF)),
            (whole((count, width)), ((count, width), F32)),
            (whole((8, width)), ((8, width), F32)),
        ],
        scratch=[pltpu.VMEM((width, 3 * width), BF), pltpu.VMEM((width, normed.shape[0]), BF)],
        prefetch=1,
        flops=2 * 12 * count * width * width,
        args=(me, dq, dk, dv, normed, tokens, grad_out, qkv),
    )


def finish_kernel(
    meta, trunk_ref, near_ref, far_ref, own_ref, mixed_ref, tokens_ref, small_ref, out_ref
):
    received = []
    for i in range(2):
        slot = meta[1 + i]
        place = pl.ds(pl.multiple_of((jnp.maximum(slot, 0) & 1) * SEG, SEG), SEG)
        branch = jnp.where(slot >= 2, far_ref[place, :], near_ref[place, :]).astype(F32)
        branch = jnp.where(slot >= 0, branch, 0.0)
        trunk = trunk_ref[i * SEG : (i + 1) * SEG, :].astype(F32)
        received.append(jnp.where(meta[0] == 0, trunk, branch))
    grad = own_ref[...] + jnp.concatenate(received, axis=0)
    unit, scale = row_norm(tokens_ref[...].astype(F32))
    back = row_norm_back(unit, scale, grad * small_ref[0:1])
    out_ref[...] = (mixed_ref[...] + back).astype(BF)


def finish(meta, trunk, near, far, own, mixed, tokens, small):
    return call(
        finish_kernel,
        "finish",
        (1,),
        [whole(x.shape) for x in (trunk, near, far, own, mixed, tokens, small)],
        [(whole(tokens.shape), (tokens.shape, BF))],
        prefetch=1,
        args=(meta, trunk, near, far, own, mixed, tokens, small),
    )[0]


def gelu_parts(v):
    x = v * 0.7071067811865476
    chance = 0.5 + 0.5 * lax.erf(x)
    density = jnp.exp(-x * x) * 0.3989422804014327
    return chance, v * density


def feed_kernel(
    tokens_ref, attended_ref, out_ref, small_ref, upstream_ref, up_ref, down_ref, shift_ref,
    output_ref, grad_mixed_ref, grad_att_ref, grad_out_ref, sums_ref, terms_ref, grads_ref,
    second_ref, second_t, upstream_t, mixed_ref, sum_ref, back_ref,
    up_slot, down_slot, up_sem, down_sem,
):
    step = pl.program_id(0)
    last = pl.num_programs(0) - 1
    slot = step % 2
    height, width = up_ref.shape[2], up_ref.shape[3]

    @pl.when(step == 0)
    def _():
        mixed = (
            tokens_ref[...].astype(F32) + dg(attended_ref[...], out_ref[...], NN)
        ) + small_ref[6:7]
        mixed_ref[...] = mixed
        unit, unused = row_norm(mixed)
        second_ref[...] = (unit * small_ref[1:2] + small_ref[3:4]).astype(BF)
        second_t[...] = second_ref[...].T
        upstream_t[...] = upstream_ref[...].T
        sum_ref[...] = jnp.zeros_like(sum_ref)
        back_ref[...] = jnp.zeros_like(back_ref)

    def up_copy(which, at):
        return pltpu.make_async_copy(
            up_slot.at[which],
            grads_ref.at[:, pl.ds(2 * at, 2), pl.ds(0, height), :],
            up_sem.at[which],
        )

    def down_copy(which, at):
        return pltpu.make_async_copy(
            down_slot.at[which],
            grads_ref.at[at, :, pl.ds(height, height), :],
            down_sem.at[which],
        )

    @pl.when(step >= 2)
    def _():
        up_copy(slot, step - 2).wait()
        down_copy(slot, step - 2).wait()

    full = up_ref.shape[0] * height
    up = jnp.concatenate([up_ref[:, i].reshape(full, width) for i in range(2)], axis=1)
    half = height // 2
    down = jnp.concatenate(
        [down_ref[0, :, i * half : (i + 1) * half, :].reshape(full, width) for i in range(2)],
        axis=1,
    )
    second, upstream = second_ref[...], upstream_ref[...]
    hidden = jnp.dot(second, up, preferred_element_type=F32) + shift_ref[...]
    grad_act = jnp.dot(upstream, down, preferred_element_type=F32)
    chance, slope = gelu_parts(hidden)
    active = (hidden * chance).astype(BF)
    grad_pre = grad_act * (chance + slope)
    grad_low = grad_pre.astype(BF)
    terms_ref[...] = jnp.sum(grad_pre, axis=0, keepdims=True)
    sum_ref[...] += dg(active, down, NT)
    back_ref[...] += dg(grad_low, up, NT)
    grad_up = jnp.dot(second_t[...], grad_low, preferred_element_type=F32).astype(BF)
    grad_down = jnp.dot(upstream_t[...], active, preferred_element_type=F32).astype(BF)
    for i in range(2):
        cut = slice(i * width, (i + 1) * width)
        up_slot[slot, :, i] = grad_up[:, cut].reshape(up_ref.shape[0], height, width)
        down_slot[slot, :, i * half : (i + 1) * half, :] = grad_down[:, cut].reshape(
            down_ref.shape[1], half, width
        )
    up_copy(slot, step).start()
    down_copy(slot, step).start()

    @pl.when(step == last)
    def _():
        up_copy(1 - slot, step - 1).wait()
        down_copy(1 - slot, step - 1).wait()
        mixed = mixed_ref[...]
        unit, scale = row_norm(mixed)
        output_ref[...] = (mixed + sum_ref[...] + small_ref[7:8]).astype(BF)
        grad_second = back_ref[...]
        upstream_f = upstream_ref[...].astype(F32)
        grad_mixed = upstream_f + row_norm_back(unit, scale, grad_second * small_ref[1:2])
        grad_mixed_ref[...] = grad_mixed
        mixed_low = grad_mixed.astype(BF)
        grad_att_ref[...] = dg(mixed_low, out_ref[...], NT).astype(BF)
        grad_out_ref[...] = jnp.dot(
            attended_ref[...].T, mixed_low, preferred_element_type=F32
        ).astype(BF)
        sums_ref[...] = jnp.zeros_like(sums_ref)
        sums_ref[0:1] = jnp.sum(grad_second * unit, axis=0, keepdims=True)
        sums_ref[1:2] = jnp.sum(grad_second, axis=0, keepdims=True)
        sums_ref[2:3] = jnp.sum(grad_mixed, axis=0, keepdims=True)
        sums_ref[3:4] = jnp.sum(upstream_f, axis=0, keepdims=True)
        up_copy(slot, step).wait()
        down_copy(slot, step).wait()


def feed_forward(tokens_in, attended, w_out, small, upstream, up_weights, down_weights, shift):
    tokens, width = tokens_in.shape
    rows, cols, half, wide = down_weights.shape
    block = whole((tokens, width))
    grid_spec = pltpu.PrefetchScalarGridSpec(
        num_scalar_prefetch=0,
        grid=(rows,),
        in_specs=[
            block,
            block,
            whole((width, width)),
            whole(small.shape),
            block,
            pl.BlockSpec((rows, 2, half, wide), lambda r: (0, r, 0, 0)),
            pl.BlockSpec((1, cols, half, wide), lambda r: (r, 0, 0, 0)),
            pl.BlockSpec((1, 2 * wide), lambda r: (0, r)),
        ],
        out_specs=[
            block,
            block,
            block,
            whole((width, width)),
            whole((8, width)),
            pl.BlockSpec((1, 2 * wide), lambda r: (0, r)),
            pl.BlockSpec(memory_space=pl.ANY),
        ],
        scratch_shapes=[
            pltpu.VMEM((tokens, width), BF),
            pltpu.VMEM((width, tokens), BF),
            pltpu.VMEM((width, tokens), BF),
            pltpu.VMEM((tokens, width), F32),
            pltpu.VMEM((tokens, width), F32),
            pltpu.VMEM((tokens, width), F32),
            pltpu.VMEM((2, rows, 2, half, wide), BF),
            pltpu.VMEM((2, cols, half, wide), BF),
            pltpu.SemaphoreType.DMA((2,)),
            pltpu.SemaphoreType.DMA((2,)),
        ],
    )
    return pl.pallas_call(
        feed_kernel,
        grid_spec=grid_spec,
        out_shape=[
            jax.ShapeDtypeStruct((tokens, width), BF),
            jax.ShapeDtypeStruct((tokens, width), F32),
            jax.ShapeDtypeStruct((tokens, width), BF),
            jax.ShapeDtypeStruct((width, width), BF),
            jax.ShapeDtypeStruct((8, width), F32),
            jax.ShapeDtypeStruct((1, cols * wide), F32),
            jax.ShapeDtypeStruct((rows, cols, 2 * half, wide), BF),
        ],
        cost_estimate=pl.CostEstimate(
            flops=12 * tokens * width * cols * wide,
            bytes_accessed=24 << 20,
            transcendentals=2 * tokens * cols * wide,
        ),
        compiler_params=pltpu.CompilerParams(vmem_limit_bytes=60 << 20),
        name="feed_forward",
    )(tokens_in, attended, w_out, small, upstream, up_weights, down_weights, shift)


def swap(value, axis, bit):
    size = lax.axis_size(axis)
    return lax.ppermute(value, axis, [(i, i ^ bit) for i in range(size)])


def exchange(value, first):
    rows, cols = lax.axis_size("row"), lax.axis_size("col")
    pairs = []
    for r in range(rows):
        for c in range(cols):
            along_x = (r & 1 == 0) == first
            other = (r, c ^ 1) if along_x else (r ^ 2, c)
            pairs.append((r * cols + c, other[0] * cols + other[1]))
    return lax.ppermute(value, ("row", "col"), pairs)


def add_low(a, b):
    return (a.astype(jnp.float32) + b.astype(jnp.float32)).astype(jnp.bfloat16)


def place_of(col_index, y_step, of_core, me):
    d = col_index ^ me[0]
    x_step = d & 1
    near = jnp.where(of_core == 0, x_step, y_step)
    far = jnp.where(of_core == 0, y_step, x_step)
    return (d >> 1) | (near << 2) | (far << 3)


def in_order(flag, first, second):
    return jnp.where(flag > 0, second, first), jnp.where(flag > 0, first, second)


def halves(value, flags):
    return [
        jnp.where(flags[i] > 0, value[i * SEG : (i + 1) * SEG], jnp.zeros((), value.dtype))
        for i in range(2)
    ]


def placed(value, targets, numbers):
    out = []
    for number in numbers:
        parts = halves(value, [(targets[i] == number).astype(jnp.int32) for i in range(2)])
        out.append(parts[0] + parts[1])
    return jnp.concatenate(out, axis=0)


def level_move(value, pairs):
    cols = lax.axis_size("col")
    x_size = 2
    full = [
        (a * x_size + x, b * x_size + x)
        for a, b in pairs
        for x in range(x_size)
        if max(a, b) * x_size < cols
    ]
    return lax.ppermute(value, "col", full)


def share_tokens(tokens, own_slot, level):
    branch = placed(tokens, own_slot, (0, 1)) + swap(placed(tokens, own_slot, (2, 3)), "col", 1)
    hop = level_move(tokens, [(0, 2)])
    moved = level_move(
        jnp.where(level == 1, branch, jnp.where(level == 0, tokens, hop)), [(0, 1), (1, 2), (2, 3)]
    )
    down = level_move(branch, [(3, 2)])
    trunk = jnp.where(level == 0, tokens, jnp.where(level == 2, hop, moved))
    branch_up = branch + jnp.where(level == 2, moved, jnp.zeros((), moved.dtype))
    up_two = level_move(branch_up, [(2, 3)])
    down_two = level_move(branch + down, [(2, 1)])
    trunk_far = swap(trunk, "col", 1)
    branch = (branch_up + down) + (up_two + down_two)
    return trunk, trunk_far, branch, swap(branch, "col", 1)


def together(*values):
    return lax.optimization_barrier(values)


def tail_rounds(part, parent_slot, level, make_pieces, vectors_of):
    parent_part = part[4 * SEG :]
    keep, send = (placed(parent_part, parent_slot, pair) for pair in ((0, 1), (2, 3)))
    trunk, trunk_send, send = together(part[: 2 * SEG], part[2 * SEG : 4 * SEG], send)
    branch_in = swap(send, "col", 1)
    own, other, extra = make_pieces(trunk)
    terms = vectors_of(extra)

    branch = add_low(keep, branch_in)
    branch, trunk_send, other, terms = together(branch, trunk_send, other, terms)
    moves = (
        level_move(branch, [(1, 2)]),
        level_move(branch, [(3, 2)]),
        swap(trunk_send, "col", 1),
        swap(other, "row", 1),
        swap(terms, "row", 1),
    )
    up, down, trunk_in, own_in, terms_in = together(*moves)

    branch_up, branch_down = add_low(branch, up), add_low(branch, down)
    trunk = add_low(trunk, trunk_in)
    half = own.shape[0] // 2
    held = add_low(own[:half], own_in[:half])
    leaving = add_low(own[half:], own_in[half:])
    terms = terms + terms_in
    branch_up, branch_down, trunk, leaving, terms = together(
        branch_up, branch_down, trunk, leaving, terms
    )
    moves = (
        level_move(branch_up, [(2, 3)]),
        level_move(branch_down, [(2, 1)]),
        level_move(trunk, [(1, 0), (3, 2)]),
        exchange(leaving, False),
        swap(terms, "row", 2),
    )
    up_two, down_two, trunk_in, held_in, terms_in = together(*moves)

    branch = (
        branch_up.astype(jnp.float32)
        + down.astype(jnp.float32)
        + up_two.astype(jnp.float32)
        + down_two.astype(jnp.float32)
    ).astype(jnp.bfloat16)
    trunk = add_low(trunk, trunk_in)
    half = half // 2
    leaving = add_low(held[half:], held_in[half:])
    held = add_low(held[:half], held_in[:half])
    terms = terms + terms_in
    branch, trunk, leaving, terms = together(branch, trunk, leaving, terms)
    moves = (
        level_move(trunk, [(2, 0)]),
        swap(branch, "col", 1),
        exchange(leaving, True),
        swap(terms, "col", 1),
    )
    trunk_in, branch_far, held_in, terms_in = together(*moves)

    trunk = add_low(trunk, trunk_in)
    terms = terms + terms_in
    leaving = [add_low(held[k], held_in[k]) for k in range(1, 4)]
    kept = held[0].astype(jnp.float32) + held_in[0].astype(jnp.float32)
    *leaving, terms = together(*leaving, terms)
    moves = [swap(leaving[k - 1], "col", 2 * k) for k in range(1, 4)]
    terms_in = swap(terms, "col", 4)
    for moved in moves:
        kept = kept + moved.astype(jnp.float32)
    terms = terms + terms_in
    terms = terms + swap(terms, "col", 2)
    return trunk, branch, branch_far, kept, terms, extra


def tree_body(
    tokens, parents, w_qkv, w_out, w_up, w_down, ln_gain, ln_bias, proj_bias, ff_bias, cotangent
):
    row, col = lax.axis_index("row"), lax.axis_index("col")
    rows, cols = lax.axis_size("row"), lax.axis_size("col")
    local_rows = tokens.shape[0]
    side, level = col & 1, col >> 1
    me = jnp.stack([col, row >> 1, row & 1]).astype(jnp.int32)

    parent = parents[0]
    numbers = jnp.arange(SEGS, dtype=jnp.int32)
    is_branch = (numbers >= 4) & (parent == 3)
    slots = jnp.cumsum(is_branch.astype(jnp.int32)) - 1
    own_parent = [parent[2 * col + i] for i in range(2)]
    is_leaf = [(own_parent[i] >= 4) for i in range(2)]
    own_slot = [
        jnp.where(is_branch[2 * col + i], slots[2 * col + i] ^ (2 * side), -1) for i in range(2)
    ]
    parent_slot = [
        jnp.where(is_leaf[i], slots[jnp.maximum(own_parent[i], 0)] ^ (2 * side), -1)
        for i in range(2)
    ]
    meta = jnp.stack(
        [
            (col < 2).astype(jnp.int32),
            col.astype(jnp.int32) * local_rows,
            is_leaf[0].astype(jnp.int32),
            is_leaf[1].astype(jnp.int32),
            2 * side.astype(jnp.int32),
        ]
    )

    narrow, wide = w_up.shape
    with jax.named_scope("gather_early_weights"):
        vectors = jnp.concatenate(
            [ln_gain, ln_bias, proj_bias, ff_bias.reshape(-1, ln_gain.shape[1])], axis=0
        ).reshape(-1, wide)
        count = vectors.shape[0]
        early = jnp.concatenate(
            [
                w_up,
                jnp.concatenate([w_qkv, w_out], axis=1),
                vectors,
                jnp.zeros((16 - count, wide), vectors.dtype),
            ],
            axis=0,
        )
        early = lax.all_gather(early, ("row", "col"), axis=0, tiled=False)
        early = early.reshape(rows, cols, *early.shape[1:])
        vectors = early[0, :, 2 * narrow : 2 * narrow + count]
        vectors = vectors.reshape(cols, -1, ln_gain.shape[1])
        small = vectors[:, :8].transpose(1, 0, 2).reshape(8, D).astype(jnp.float32)
        ff_shift = vectors[:, 8:].reshape(1, -1).astype(jnp.float32)
        full_qkv, full_out = join_pieces(early, narrow)
    with jax.named_scope("gather_tokens"):
        trunk, trunk_far, branch, branch_far = share_tokens(tokens, own_slot, level)
        branch = jnp.concatenate([branch, branch_far], axis=0)
        parent_tokens = jnp.concatenate(
            [
                lax.dynamic_slice_in_dim(branch, jnp.maximum(parent_slot[i], 0) * SEG, SEG, 0)
                for i in range(2)
            ],
            axis=0,
        )
    with jax.named_scope("gather_late_weights"):
        late = jnp.concatenate([w_down.T[:, :wide], w_down.T[:, wide:]], axis=0)
        late = lax.all_gather(late, ("row", "col"), axis=0, tiled=False)
        late = late.reshape(rows, cols, *late.shape[1:])

    sources = (trunk, trunk_far, parent_tokens, tokens)
    queries, key_rows, value_rows, normed = project(sources, small, full_qkv)
    attended, log_total = attn_fwd(meta, queries, key_rows, value_rows)
    output, grad_mixed, grad_att, grad_out, sums, ff_terms, late_grads = feed_forward(
        tokens, attended, full_out, small, cotangent, early, late, ff_shift
    )
    with jax.named_scope("scatter_late_weights"):
        late_sum = lax.psum_scatter(
            late_grads.reshape(rows * cols, *late_grads.shape[2:]),
            ("row", "col"),
            scatter_dimension=0,
            tiled=False,
        ).astype(jnp.float32)
        up_rows, down_rows = w_up.shape[0], w_down.shape[1]
        grad_w_up = late_sum[:up_rows]
        grad_w_down = jnp.concatenate(
            [late_sum[up_rows : up_rows + down_rows], late_sum[up_rows + down_rows :]], axis=1
        ).T
    grad_q, grad_k, grad_v = attn_bwd(
        meta, queries, key_rows, value_rows, grad_att, attended, log_total
    )
    part, part_terms = unproject(sources[:3], grad_k, grad_v, small, full_qkv)

    def make_pieces(after):
        dq, dk, dv, unused = together(grad_q, grad_k, grad_v, after)
        own, other, grad_normed, own_terms = weigh(
            me, dq, dk, dv, normed, tokens, grad_out, full_qkv, cols
        )
        return own, other, (grad_normed, own_terms)

    def vectors_of(extra):
        return jnp.concatenate([part_terms + extra[1], sums, ff_terms.reshape(-1, D)], axis=0)

    with jax.named_scope("sum_gradients"):
        trunk_grad, branch_grad, branch_grad_far, early_sum, terms, extra = tail_rounds(
            part, parent_slot, level, make_pieces, vectors_of
        )
    tall = w_qkv.shape[1]
    grad_w_qkv, grad_w_out = early_sum[:, :tall], early_sum[:, tall:]
    finish_meta = jnp.stack([level, own_slot[0], own_slot[1]]).astype(jnp.int32)
    grad_tokens = finish(
        finish_meta, trunk_grad, branch_grad, branch_grad_far, extra[0], grad_mixed, tokens, small
    )
    with jax.named_scope("vectors"):
        cut = ln_gain.shape[1]
        mine = lax.dynamic_slice_in_dim(terms[:16], col * cut, cut, 1)
        grad_ff = lax.dynamic_slice_in_dim(
            terms[16:].reshape(-1), col * ff_bias.shape[0], ff_bias.shape[0], 0
        )
        grad_gain = jnp.stack([mine[0], mine[8]])
        grad_shift = jnp.stack([mine[1], mine[9]])
        grad_bias = jnp.stack([mine[3], mine[2], mine[10], mine[11]])
    return (
        output,
        grad_tokens,
        grad_w_qkv,
        grad_w_out,
        grad_w_up,
        grad_w_down,
        grad_gain,
        grad_shift,
        grad_bias,
        grad_ff,
    )


def solution(mesh):
    fits = mesh.shape["col"] == 8 and mesh.shape["row"] == 4
    body = tree_body if fits else plain_body
    return jax.shard_map(
        body,
        mesh=mesh,
        in_specs=(
            P(("row", "col"), None),
            P("row", None),
            P("row", "col"),
            P("row", "col"),
            P("row", "col"),
            P("row", "col"),
            P(None, "col"),
            P(None, "col"),
            P(None, "col"),
            P("col"),
            P(("row", "col"), None),
        ),
        out_specs=(
            P(("row", "col"), None),
            P(("row", "col"), None),
            P("row", "col"),
            P("row", "col"),
            P("row", "col"),
            P("row", "col"),
            P(None, "col"),
            P(None, "col"),
            P(None, "col"),
            P("col"),
        ),
        check_vma=False,
    )
```

```python
import jax
import jax.numpy as jnp
from jax import lax
from jax.experimental import pallas as pl
from jax.experimental.pallas import tpu as pltpu
from jax.sharding import PartitionSpec as P

D = 768
HEADS = 12
HEAD_DIM = 64
SEG = 256
SEGS = 16
TREE_TOKENS = 4096


EPSILON = 1e-12
NEGATIVE = -1e30


def layer_norm(values, scaling, shifting):
    centre = values - jnp.mean(values, axis=-1, keepdims=True)
    spread = jnp.mean(centre * centre, axis=-1, keepdims=True)
    return centre * lax.rsqrt(spread + EPSILON) * scaling + shifting


def exact_gelu(values):
    return jax.nn.gelu(values, approximate=False)


def ancestry(parents):
    segment_count = parents.shape[0]
    labels = jnp.arange(segment_count, dtype=jnp.int32)
    closure = jnp.eye(segment_count, dtype=jnp.float32) + (
        parents[:, None] == labels[None, :]
    ).astype(jnp.float32)
    for repeat in range(segment_count.bit_length()):
        closure = jnp.minimum(jnp.dot(closure, closure, precision=lax.Precision.HIGHEST), 1.0)
    return closure


def allowed(query_pos, key_pos, closure):
    labels = jnp.arange(closure.shape[0], dtype=jnp.int32)
    query_seg = query_pos // SEG
    key_seg = key_pos // SEG
    query_hot = (query_seg[:, None] == labels[None, :]).astype(jnp.float32)
    key_hot = (key_seg[:, None] == labels[None, :]).astype(jnp.float32)
    reach = jnp.dot(
        jnp.dot(query_hot, closure, precision=lax.Precision.HIGHEST),
        key_hot.T,
        precision=lax.Precision.HIGHEST,
    )
    causal = (query_seg[:, None] != key_seg[None, :]) | (key_pos[None, :] <= query_pos[:, None])
    return (reach > 0.5) & causal


def plain_body(
    tokens, parents, w_qkv, w_out, w_up, w_down, ln_gain, ln_bias, proj_bias, ff_bias, cotangent
):
    local_rows = tokens.shape[0]
    score_scale = HEAD_DIM ** (-0.5)
    head_shape = (local_rows, HEADS, HEAD_DIM)
    block_rows = 2 * SEG
    block_count = SEGS // 2
    cols_qkv, cols_out, cols_up, cols_down, norm_gains, shifts, biases, ff_shift = (
        lax.all_gather(w_qkv, "col", axis=1, tiled=True),
        lax.all_gather(w_out, "col", axis=1, tiled=True),
        lax.all_gather(w_up, "col", axis=1, tiled=True),
        lax.all_gather(w_down, "col", axis=1, tiled=True),
        lax.all_gather(ln_gain, "col", axis=1, tiled=True),
        lax.all_gather(ln_bias, "col", axis=1, tiled=True),
        lax.all_gather(proj_bias, "col", axis=1, tiled=True),
        lax.all_gather(ff_bias, "col", axis=0, tiled=True),
    )
    full_qkv, full_out, full_up, full_down = (
        lax.all_gather(cols_qkv, "row", axis=0, tiled=True),
        lax.all_gather(cols_out, "row", axis=0, tiled=True),
        lax.all_gather(cols_up, "row", axis=0, tiled=True),
        lax.all_gather(cols_down, "row", axis=0, tiled=True),
    )
    norm_gains = norm_gains.astype(jnp.float32)
    shifts = shifts.astype(jnp.float32)
    biases = biases.astype(jnp.float32)
    ff_shift = ff_shift.astype(jnp.float32)
    inputs = tokens.astype(jnp.float32)
    normed_low = layer_norm(inputs, norm_gains[0], shifts[0]).astype(jnp.bfloat16)
    projected = jnp.dot(normed_low, full_qkv, preferred_element_type=jnp.float32)
    queries = (projected[:, :D] + biases[0]).astype(jnp.bfloat16).reshape(head_shape)
    keys_own = projected[:, D : 2 * D].astype(jnp.bfloat16).reshape(head_shape)
    values_own = (projected[:, 2 * D :] + biases[1]).astype(jnp.bfloat16).reshape(head_shape)
    keys_all, values_all = (
        lax.all_gather(keys_own, "col", axis=0, tiled=True),
        lax.all_gather(values_own, "col", axis=0, tiled=True),
    )
    key_blocks = keys_all.reshape(block_count, block_rows, HEADS, HEAD_DIM)
    value_blocks = values_all.reshape(block_count, block_rows, HEADS, HEAD_DIM)
    block_starts = jnp.arange(block_count, dtype=jnp.int32) * block_rows
    within = jnp.arange(block_rows, dtype=jnp.int32)
    query_pos = lax.axis_index("col") * local_rows + jnp.arange(local_rows, dtype=jnp.int32)
    closure = ancestry(parents[0])

    def scores_of(query_block, key_block, query_positions, key_positions):
        products = jnp.einsum(
            "qhd,khd->hqk", query_block, key_block, preferred_element_type=jnp.float32
        )
        return (products * score_scale, allowed(query_positions, key_positions, closure)[None])

    def probabilities(query_block, key_block, query_positions, key_positions, log_block):
        scores, visible = scores_of(query_block, key_block, query_positions, key_positions)
        return jnp.where(visible, jnp.exp(scores - log_block[..., None]), 0.0)

    def extent(running, pieces):
        highest_score, mass_total = running
        key_block, first_pos = pieces
        scores, visible = scores_of(queries, key_block, query_pos, first_pos + within)
        masked = jnp.where(visible, scores, NEGATIVE)
        new_highest = jnp.maximum(highest_score, jnp.max(masked, axis=-1))
        exp_terms = jnp.where(visible, jnp.exp(masked - new_highest[..., None]), 0.0)
        new_total = mass_total * jnp.exp(highest_score - new_highest) + jnp.sum(exp_terms, axis=-1)
        return ((new_highest, new_total), None)

    start_state = (
        jnp.full((HEADS, local_rows), NEGATIVE, jnp.float32),
        jnp.zeros((HEADS, local_rows), jnp.float32),
    )
    (highest_score, mass_total), unused = lax.scan(extent, start_state, (key_blocks, block_starts))
    log_total = highest_score + jnp.log(mass_total)

    def attend(running, pieces):
        key_block, value_block, first_pos = pieces
        chances = probabilities(
            queries, key_block, query_pos, first_pos + within, log_total
        ).astype(jnp.bfloat16)
        return (
            running
            + jnp.einsum("hqk,khd->qhd", chances, value_block, preferred_element_type=jnp.float32),
            None,
        )

    attended, unused = lax.scan(
        attend, jnp.zeros(head_shape, jnp.float32), (key_blocks, value_blocks, block_starts)
    )
    attended_low = attended.reshape(local_rows, D).astype(jnp.bfloat16)
    mixed_rows = (
        inputs + jnp.dot(attended_low, full_out, preferred_element_type=jnp.float32) + biases[2]
    )
    second_low = layer_norm(mixed_rows, norm_gains[1], shifts[1]).astype(jnp.bfloat16)
    hidden_pre = jnp.dot(second_low, full_up, preferred_element_type=jnp.float32) + ff_shift
    activated_low = exact_gelu(hidden_pre).astype(jnp.bfloat16)
    output = (
        mixed_rows
        + jnp.dot(activated_low, full_down, preferred_element_type=jnp.float32)
        + biases[3]
    )
    upstream = cotangent.astype(jnp.float32)
    grad_down = jnp.einsum(
        "tf,td->fd", activated_low, cotangent, preferred_element_type=jnp.float32
    )
    grad_act = jnp.einsum("td,fd->tf", cotangent, full_down, preferred_element_type=jnp.float32)
    unused, gelu_back = jax.vjp(exact_gelu, hidden_pre)
    grad_pre = gelu_back(grad_act)[0]
    grad_pre_low = grad_pre.astype(jnp.bfloat16)
    grad_up = jnp.einsum("td,tf->df", second_low, grad_pre_low, preferred_element_type=jnp.float32)
    grad_second = jnp.einsum("tf,df->td", grad_pre_low, full_up, preferred_element_type=jnp.float32)
    unused, second_back = jax.vjp(layer_norm, mixed_rows, norm_gains[1], shifts[1])
    grad_mixed_norm, grad_gain_two, grad_shift_two = second_back(grad_second)
    grad_mixed = upstream + grad_mixed_norm
    grad_mixed_low = grad_mixed.astype(jnp.bfloat16)
    grad_out = jnp.einsum(
        "td,te->de", attended_low, grad_mixed_low, preferred_element_type=jnp.float32
    )
    grad_att_low = (
        jnp.einsum("te,de->td", grad_mixed_low, full_out, preferred_element_type=jnp.float32)
        .astype(jnp.bfloat16)
        .reshape(head_shape)
    )
    deltas = jnp.einsum("qhd,qhd->hq", grad_att_low.astype(jnp.float32), attended)

    def score_grads(
        query_block,
        key_block,
        value_block,
        grad_block,
        query_positions,
        key_positions,
        log_block,
        delta_block,
    ):
        chances = probabilities(query_block, key_block, query_positions, key_positions, log_block)
        grad_chances = jnp.einsum(
            "qhd,khd->hqk", grad_block, value_block, preferred_element_type=jnp.float32
        )
        grad_scores = (chances * (grad_chances - delta_block[..., None]) * score_scale).astype(
            jnp.bfloat16
        )
        return (chances.astype(jnp.bfloat16), grad_scores)

    def backward_block(running, pieces):
        key_block, value_block, first_pos = pieces
        chances_low, grad_scores = score_grads(
            queries,
            key_block,
            value_block,
            grad_att_low,
            query_pos,
            first_pos + within,
            log_total,
            deltas,
        )
        running = running + jnp.einsum(
            "hqk,khd->qhd", grad_scores, key_block, preferred_element_type=jnp.float32
        )
        key_term = jnp.einsum(
            "hqk,qhd->khd", grad_scores, queries, preferred_element_type=jnp.float32
        )
        value_term = jnp.einsum(
            "hqk,qhd->khd", chances_low, grad_att_low, preferred_element_type=jnp.float32
        )
        return (running, (key_term, value_term))

    grad_queries, (key_terms, value_terms) = lax.scan(
        backward_block, jnp.zeros(head_shape, jnp.float32), (key_blocks, value_blocks, block_starts)
    )
    grad_keys, grad_values = (
        lax.psum_scatter(
            key_terms.reshape(TREE_TOKENS, D).astype(jnp.bfloat16),
            "col",
            scatter_dimension=0,
            tiled=True,
        ).astype(jnp.float32),
        lax.psum_scatter(
            value_terms.reshape(TREE_TOKENS, D).astype(jnp.bfloat16),
            "col",
            scatter_dimension=0,
            tiled=True,
        ).astype(jnp.float32),
    )
    grad_queries = grad_queries.reshape(local_rows, D)
    grad_projected_low = jnp.concatenate([grad_queries, grad_keys, grad_values], axis=1).astype(
        jnp.bfloat16
    )
    grad_qkv = jnp.einsum(
        "td,te->de", normed_low, grad_projected_low, preferred_element_type=jnp.float32
    )
    grad_normed = jnp.einsum(
        "te,de->td", grad_projected_low, full_qkv, preferred_element_type=jnp.float32
    )
    unused, first_back = jax.vjp(layer_norm, inputs, norm_gains[0], shifts[0])
    grad_input_norm, grad_gain_one, grad_shift_one = first_back(grad_normed)
    grad_tokens = (grad_mixed + grad_input_norm).astype(jnp.bfloat16)
    gain_terms = jnp.stack([grad_gain_one, grad_gain_two])
    shift_terms = jnp.stack([grad_shift_one, grad_shift_two])
    bias_terms = jnp.stack(
        [
            jnp.sum(grad_queries, axis=0),
            jnp.sum(grad_values, axis=0),
            jnp.sum(grad_mixed, axis=0),
            jnp.sum(upstream, axis=0),
        ]
    )
    ff_terms = jnp.sum(grad_pre, axis=0)
    part_qkv, part_out, part_up, part_down, part_gain, part_shift, part_bias, part_ff = (
        lax.psum_scatter(
            grad_qkv.astype(jnp.bfloat16), "col", scatter_dimension=1, tiled=True
        ).astype(jnp.float32),
        lax.psum_scatter(
            grad_out.astype(jnp.bfloat16), "col", scatter_dimension=1, tiled=True
        ).astype(jnp.float32),
        lax.psum_scatter(
            grad_up.astype(jnp.bfloat16), "col", scatter_dimension=1, tiled=True
        ).astype(jnp.float32),
        lax.psum_scatter(
            grad_down.astype(jnp.bfloat16), "col", scatter_dimension=1, tiled=True
        ).astype(jnp.float32),
        lax.psum_scatter(
            gain_terms.astype(jnp.bfloat16), "col", scatter_dimension=1, tiled=True
        ).astype(jnp.float32),
        lax.psum_scatter(
            shift_terms.astype(jnp.bfloat16), "col", scatter_dimension=1, tiled=True
        ).astype(jnp.float32),
        lax.psum_scatter(
            bias_terms.astype(jnp.bfloat16), "col", scatter_dimension=1, tiled=True
        ).astype(jnp.float32),
        lax.psum_scatter(
            ff_terms.astype(jnp.bfloat16), "col", scatter_dimension=0, tiled=True
        ).astype(jnp.float32),
    )
    grad_w_qkv, grad_w_out, grad_w_up, grad_w_down = (
        lax.psum_scatter(
            part_qkv.astype(jnp.bfloat16), "row", scatter_dimension=0, tiled=True
        ).astype(jnp.float32),
        lax.psum_scatter(
            part_out.astype(jnp.bfloat16), "row", scatter_dimension=0, tiled=True
        ).astype(jnp.float32),
        lax.psum_scatter(
            part_up.astype(jnp.bfloat16), "row", scatter_dimension=0, tiled=True
        ).astype(jnp.float32),
        lax.psum_scatter(
            part_down.astype(jnp.bfloat16), "row", scatter_dimension=0, tiled=True
        ).astype(jnp.float32),
    )
    grad_gain, grad_shift, grad_bias, grad_ff = lax.psum(
        (part_gain, part_shift, part_bias, part_ff), "row"
    )
    return (
        output.astype(jnp.bfloat16),
        grad_tokens,
        grad_w_qkv,
        grad_w_out,
        grad_w_up,
        grad_w_down,
        grad_gain,
        grad_shift,
        grad_bias,
        grad_ff,
    )


F32=jnp.float32; BF=jnp.bfloat16
NEG=NEGATIVE
NT=(((1,),(1,)),((),()))
NN=(((1,),(0,)),((),()))


def dg(a, b, dims):
    return lax.dot_general(a, b, dims, preferred_element_type=F32)


def chunk_rows(c, i):
    start = c * SEG if c < 4 else (4 + (c - 4) * 2 + i) * SEG
    return slice(start, start + SEG)


def pair_dot(c, keys_ref, rows):
    if c < 4:
        return dg(keys_ref[chunk_rows(c, 0), :], rows, NT)
    return jnp.concatenate(
        [
            dg(keys_ref[chunk_rows(c, i), :], rows[i * SEG : (i + 1) * SEG, :], NT)
            for i in range(2)
        ],
        axis=1,
    )


def score_chunk(c, k_ref, qh):
    scores = pair_dot(c, k_ref, qh)
    if c < 5:
        return scores
    key = lax.broadcasted_iota(jnp.int32, scores.shape, 0)
    query = lax.broadcasted_iota(jnp.int32, scores.shape, 1)
    return jnp.where(key <= (query & (SEG - 1)), scores, NEG)


def chunk_bias(c, meta):
    second = lax.broadcasted_iota(jnp.int32, (1, 2 * SEG), 1) // SEG
    if c < 4:
        return jnp.where((c ^ meta[1]) < meta[0] + second, 0.0, NEG)
    if c == 4:
        return jnp.where(jnp.where(second > 0, meta[3], meta[2]) > 0, 0.0, NEG)
    return jnp.zeros((1, 2 * SEG), F32)


def halves_of(value):
    lane = lax.broadcasted_iota(jnp.int32, value.shape, 1)
    zero = jnp.zeros((), value.dtype)
    return [jnp.where((lane < 64) == (h == 0), value, zero) for h in range(2)]


def fwd_kernel(meta, q_ref, k_ref, v_ref, o_ref, inverse_ref, p_ref):
    turned = v_ref[...].T
    biases = [chunk_bias(c, meta) for c in range(6)]
    results, inverses = [], []
    for h, qh in enumerate(halves_of(q_ref[...] * jnp.asarray(0.125, BF))):
        scores = [score_chunk(c, k_ref, qh) for c in range(6)]
        top = jnp.full((1, 2 * SEG), NEG, F32)
        for s, bias in zip(scores, biases):
            top = jnp.maximum(top, jnp.max(s, axis=0, keepdims=True) + bias)
        mass = jnp.zeros((1, 2 * SEG), F32)
        shared = jnp.zeros((128, 2 * SEG), F32)
        own = [jnp.zeros((128, SEG), F32)] * 2
        for c, s in enumerate(scores):
            p = jnp.exp(s - (top - biases[c]))
            mass = mass + jnp.sum(p, axis=0, keepdims=True)
            low = p.astype(BF)
            p_ref[0, (6 * h + c) * SEG : (6 * h + c + 1) * SEG, :] = low
            if c < 4:
                shared = shared + dg(turned[:, chunk_rows(c, 0)], low, NN)
            else:
                own = [
                    own[i] + dg(turned[:, chunk_rows(c, i)], low[:, i * SEG : (i + 1) * SEG], NN)
                    for i in range(2)
                ]
        inverse = jnp.broadcast_to(1.0 / mass, shared.shape)
        inverses.append(inverse)
        results.append((shared + jnp.concatenate(own, axis=1)) * inverse)
    row = lax.broadcasted_iota(jnp.int32, results[0].shape, 0)
    o_ref[...] = jnp.where(row < 64, results[0], results[1]).T.astype(BF)
    inverse_ref[...] = jnp.where(row < 64, inverses[0], inverses[1]).T


def bwd_kernel(q_ref, k_ref, v_ref, do_ref, o_ref, inverse_ref, p_ref, dq_ref, dk_ref, dv_ref):
    do = (do_ref[...].astype(F32) * inverse_ref[...]).astype(BF)
    products = (do.astype(F32) * o_ref[...].astype(F32)).T
    turned = k_ref[...].T
    qh = halves_of(q_ref[...] * jnp.asarray(0.125, BF))
    doh = halves_of(do)
    delta = [jnp.sum(products[h * 64 : (h + 1) * 64], axis=0, keepdims=True) for h in range(2)]
    shared = [jnp.zeros((128, 2 * SEG), F32)] * 2
    own = [[jnp.zeros((128, SEG), F32)] * 2] * 2
    for c in range(6):
        chances, slopes = [], []
        for h in range(2):
            p = p_ref[0, (6 * h + c) * SEG : (6 * h + c + 1) * SEG, :]
            ds = p.astype(F32) * (pair_dot(c, v_ref, doh[h]) - delta[h])
            chances.append(p)
            slopes.append(ds.astype(BF))
        for i in range(1 if c < 4 else 2):
            r = chunk_rows(c, i)
            cut = slice(0, 2 * SEG) if c < 4 else slice(i * SEG, (i + 1) * SEG)
            for ref, left, right in ((dv_ref, chances, doh), (dk_ref, slopes, qh)):
                ref[r, :] = dg(
                    jnp.concatenate([x[:, cut] for x in left], axis=1),
                    jnp.concatenate([x[cut] for x in right], axis=0),
                    NN,
                ).astype(BF)
        if c < 4:
            shared = [shared[h] + dg(turned[:, chunk_rows(c, 0)], slopes[h], NN) for h in range(2)]
        else:
            own = [
                [
                    own[h][i]
                    + dg(turned[:, chunk_rows(c, i)], slopes[h][:, i * SEG : (i + 1) * SEG], NN)
                    for i in range(2)
                ]
                for h in range(2)
            ]
    total_q = [shared[h] + jnp.concatenate(own[h], axis=1) for h in range(2)]
    row = lax.broadcasted_iota(jnp.int32, total_q[0].shape, 0)
    dq_ref[...] = (jnp.where(row < 64, total_q[0], total_q[1]).T * 0.125).astype(BF)


def attn_specs(rows, keys):
    return (
        pl.BlockSpec((rows, 128), lambda j, *unused: (0, j)),
        pl.BlockSpec((keys, 128), lambda j, *unused: (0, j)),
        pl.BlockSpec((1, 12 * SEG, rows), lambda j, *unused: (j, 0, 0)),
    )


def attn_fwd(meta, q, k, v):
    rows, width = q.shape
    pairs = width // 128
    q_spec, k_spec, p_spec = attn_specs(rows, k.shape[0])
    return call(
        fwd_kernel,
        "attn_fwd",
        (pairs,),
        [q_spec, k_spec, k_spec],
        [
            (q_spec, (q.shape, BF)),
            (q_spec, (q.shape, F32)),
            (p_spec, ((pairs, 12 * SEG, rows), BF)),
        ],
        prefetch=1,
        flops=2 * 2 * 12 * 12 * SEG**3,
        size=32 << 20,
        args=(meta, q, k, v),
    )


def attn_bwd(q, k, v, do, o, inverse, p):
    rows, width = q.shape
    pairs = width // 128
    q_spec, k_spec, p_spec = attn_specs(rows, k.shape[0])
    return call(
        bwd_kernel,
        "attn_bwd",
        (pairs,),
        [q_spec, k_spec, k_spec, q_spec, q_spec, q_spec, p_spec],
        [(q_spec, (q.shape, BF)), (k_spec, (k.shape, BF)), (k_spec, (k.shape, BF))],
        flops=4 * 2 * 12 * 12 * SEG**3,
        size=40 << 20,
        args=(q, k, v, do, o, inverse, p),
    )


def row_norm(values):
    centre = values - jnp.mean(values, axis=-1, keepdims=True)
    spread = jnp.mean(centre * centre, axis=-1, keepdims=True)
    scale = lax.rsqrt(spread + EPSILON)
    return centre * scale, scale


def row_norm_back(unit, scale, scaled):
    mean_one = jnp.mean(scaled, axis=-1, keepdims=True)
    mean_two = jnp.mean(scaled * unit, axis=-1, keepdims=True)
    return scale * (scaled - mean_one - unit * mean_two)


def call(kernel, name, grid, ins, outs, scratch=(), prefetch=0, flops=0, size=16 << 20, args=()):
    grid_spec = pltpu.PrefetchScalarGridSpec(
        num_scalar_prefetch=prefetch,
        grid=grid,
        in_specs=ins,
        out_specs=[spec for spec, unused in outs],
        scratch_shapes=list(scratch),
    )
    return pl.pallas_call(
        kernel,
        grid_spec=grid_spec,
        out_shape=[jax.ShapeDtypeStruct(*shape) for unused, shape in outs],
        cost_estimate=pl.CostEstimate(flops=flops, bytes_accessed=size, transcendentals=0),
        compiler_params=pltpu.CompilerParams(vmem_limit_bytes=58 << 20),
        name=name,
    )(*args)


def whole(shape):
    return pl.BlockSpec(shape, lambda *unused: (0,) * len(shape))


def join_kernel(pieces_ref, qkv_ref, out_ref):
    cols = pieces_ref.shape[1]
    cut = qkv_ref.shape[1] // cols
    qkv_ref[...] = jnp.concatenate([pieces_ref[0, c, :, :cut] for c in range(cols)], axis=1)
    out_ref[...] = jnp.concatenate([pieces_ref[0, c, :, cut:] for c in range(cols)], axis=1)


def join_pieces(pieces, height):
    rows, cols, unused, width = pieces.shape
    full = rows * height
    return call(
        join_kernel,
        "join_pieces",
        (rows,),
        [pl.BlockSpec((1, cols, height, width), lambda r: (r, 0, 1, 0))],
        [
            (pl.BlockSpec((height, 3 * full), lambda r: (r, 0)), ((full, 3 * full), BF)),
            (pl.BlockSpec((height, full), lambda r: (r, 0)), ((full, full), BF)),
        ],
        args=(pieces,),
    )


def turn_kernel(value_ref, turned_ref, sum_ref):
    turned_ref[...] = value_ref[...].T
    sum_ref[...] = jnp.sum(value_ref[...].astype(F32), axis=0, keepdims=True)


def turn(value):
    rows, width = value.shape
    return call(
        turn_kernel,
        "turn",
        (1,),
        [whole(value.shape)],
        [
            (whole((width, rows)), ((width, rows), BF)),
            (whole((1, width)), ((1, width), F32)),
        ],
        args=(value,),
    )


def select_source(step, sources, kept):
    for i, ref in enumerate(sources):

        @pl.when(step == i)
        def _(ref=ref):
            kept[...] = ref[...]

    return row_norm(kept[...].astype(F32))[0]


def project_kernel(a_ref, b_ref, c_ref, d_ref, small_ref, weight_ref, q_ref, k_ref, v_ref, n_ref, kept):
    step = pl.program_id(0)
    width = a_ref.shape[1]
    unit = select_source(step, (a_ref, b_ref, c_ref, d_ref), kept)
    normed = (unit * small_ref[0:1] + small_ref[2:3]).astype(BF)
    n_ref[...] = normed
    k_ref[...] = dg(normed, weight_ref[:, width : 2 * width], NN).astype(BF)
    v_ref[...] = (dg(normed, weight_ref[:, 2 * width :], NN) + small_ref[5:6]).astype(BF)

    @pl.when(step == pl.num_programs(0) - 1)
    def _():
        q_ref[...] = (dg(normed, weight_ref[:, :width], NN) + small_ref[4:5]).astype(BF)


def project(sources, small, qkv):
    tokens, width = sources[0].shape
    count = len(sources)
    block = pl.BlockSpec((tokens, width), lambda i: (i, 0))
    tall = ((count * tokens, width), BF)
    return call(
        project_kernel,
        "project",
        (count,),
        [whole((tokens, width))] * count + [whole(small.shape), whole(qkv.shape)],
        [(whole((tokens, width)), ((tokens, width), BF)), (block, tall), (block, tall), (block, tall)],
        scratch=[pltpu.VMEM((tokens, width), BF)],
        flops=2 * (2 * count + 1) * tokens * width * width,
        args=(*sources, small, qkv),
    )


def unproject_kernel(
    a_ref, b_ref, c_ref, dk_ref, dv_ref, k_ref, v_ref, part_ref, terms_ref, kept
):
    step = pl.program_id(0)

    @pl.when(step == 0)
    def _():
        terms_ref[...] = jnp.zeros_like(terms_ref)

    dk, dv = dk_ref[...], dv_ref[...]
    grad = dg(dk, k_ref[...], NT) + dg(dv, v_ref[...], NT)
    part_ref[...] = grad.astype(BF)
    unit = select_source(step, (a_ref, b_ref, c_ref), kept)
    terms_ref[0:1] += jnp.sum(grad * unit, axis=0, keepdims=True)
    terms_ref[1:2] += jnp.sum(grad, axis=0, keepdims=True)
    terms_ref[2:3] += jnp.sum(dv.astype(F32), axis=0, keepdims=True)


def unproject(sources, dk, dv, qkv):
    tokens, width = sources[0].shape
    count = len(sources)
    block = pl.BlockSpec((tokens, width), lambda i: (i, 0))
    return call(
        unproject_kernel,
        "unproject",
        (count,),
        [whole((tokens, width))] * count
        + [block, block]
        + [pl.BlockSpec((width, width), lambda i, n=n: (0, n)) for n in (1, 2)],
        [(block, ((count * tokens, width), BF)), (whole((8, width)), ((8, width), F32))],
        scratch=[pltpu.VMEM((tokens, width), BF)],
        flops=2 * 2 * count * tokens * width * width,
        args=(*sources, dk, dv, qkv, qkv),
    )


def weigh_kernel(
    me, dq_ref, dk_ref, dv_ref, n_ref, tokens_ref, grad_out_ref, weight_ref,
    own_ref, other_ref, grad_ref, terms_ref, kept, turned,
):
    step = pl.program_id(0)
    tokens, width = dq_ref.shape

    @pl.when(step == 0)
    def _():
        dq, dk, dv = dq_ref[...], dk_ref[-tokens:], dv_ref[-tokens:]
        grad = (
            dg(dq, weight_ref[:, :width], NT)
            + dg(dk, weight_ref[:, width : 2 * width], NT)
            + dg(dv, weight_ref[:, 2 * width :], NT)
        )
        grad_ref[...] = grad
        unit, unused = row_norm(tokens_ref[...].astype(F32))
        terms_ref[...] = jnp.zeros_like(terms_ref)
        terms_ref[0:1] = jnp.sum(grad * unit, axis=0, keepdims=True)
        terms_ref[1:2] = jnp.sum(grad, axis=0, keepdims=True)
        terms_ref[2:3] = jnp.sum(dv.astype(F32), axis=0, keepdims=True)
        terms_ref[3:4] = jnp.sum(dq.astype(F32), axis=0, keepdims=True)
        turned[...] = n_ref[...].T
        kept[:, :width] = dg(turned[:, -tokens:], dq, NN).astype(BF)

    @pl.when(step == 1)
    def _():
        kept[:, width : 2 * width] = dg(turned[...], dk_ref[...], NN).astype(BF)

    @pl.when(step == 2)
    def _():
        kept[:, 2 * width :] = dg(turned[...], dv_ref[...], NN).astype(BF)
        height = own_ref.shape[1]
        cols = own_ref.shape[0] // 2
        tall, low_part = 3 * width // cols, width // cols
        for c in range(cols):
            parts = [
                jnp.concatenate(
                    [
                        kept[r * height : (r + 1) * height, c * tall : (c + 1) * tall],
                        grad_out_ref[r * height : (r + 1) * height, c * low_part : (c + 1) * low_part],
                    ],
                    axis=1,
                )
                for r in range(4)
            ]
            a, c_part = in_order(me[1], parts[0], parts[2])
            b, d_part = in_order(me[1], parts[1], parts[3])
            for y_step, pair in ((0, (a, b)), (1, (c_part, d_part))):
                mine, theirs = in_order(me[2], *pair)
                own_ref[place_of(c, y_step, me[2], me)] = mine
                other_ref[place_of(c, y_step, me[2] ^ 1, me)] = theirs


def weigh(me, dq, dk, dv, normed, tokens, grad_out, qkv, cols):
    count, width = dq.shape
    shape = (2 * cols, width // 4, 4 * width // cols)
    return call(
        weigh_kernel,
        "weigh",
        (3,),
        [whole(x.shape) for x in (dq, dk, dv, normed, tokens, grad_out, qkv)],
        [
            (whole(shape), (shape, BF)),
            (whole(shape), (shape, BF)),
            (whole((count, width)), ((count, width), F32)),
            (whole((8, width)), ((8, width), F32)),
        ],
        scratch=[pltpu.VMEM((width, 3 * width), BF), pltpu.VMEM((width, normed.shape[0]), BF)],
        prefetch=1,
        flops=2 * 12 * count * width * width,
        args=(me, dq, dk, dv, normed, tokens, grad_out, qkv),
    )


def finish_kernel(
    meta, trunk_ref, near_ref, far_ref, own_ref, mixed_ref, tokens_ref, small_ref, out_ref
):
    slot = meta[1 + pl.program_id(0)]
    place = pl.ds(pl.multiple_of((jnp.maximum(slot, 0) & 1) * SEG, SEG), SEG)
    branch = jnp.where(slot >= 2, far_ref[place, :], near_ref[place, :]).astype(F32)
    branch = jnp.where(slot >= 0, branch, 0.0)
    trunk = trunk_ref[...].astype(F32)
    grad = own_ref[...] + jnp.where(meta[0] == 0, trunk, branch)
    unit, scale = row_norm(tokens_ref[...].astype(F32))
    back = row_norm_back(unit, scale, grad * small_ref[0:1])
    out_ref[...] = (mixed_ref[...] + back).astype(BF)


def finish(meta, trunk, near, far, own, mixed, tokens, small):
    width = tokens.shape[1]
    part = pl.BlockSpec((SEG, width), lambda i, meta: (i, 0))
    full = whole(near.shape)
    return call(
        finish_kernel,
        "finish",
        (2,),
        [part, full, full, part, part, part, whole(small.shape)],
        [(part, (tokens.shape, BF))],
        prefetch=1,
        args=(meta, trunk, near, far, own, mixed, tokens, small),
    )[0]


def gelu_parts(v):
    x = v * 0.7071067811865476
    chance = 0.5 + 0.5 * lax.erf(x)
    density = jnp.exp(-x * x) * 0.3989422804014327
    return chance, v * density


def feed_kernel(
    tokens_ref, attended_ref, out_ref, small_ref, upstream_ref, upstream_t, summed_ref, up_ref, down_ref,
    shift_ref,
    output_ref, grad_mixed_ref, grad_att_ref, grad_out_ref, sums_ref, terms_ref, grads_ref,
    second_ref, second_t, mixed_ref, sum_ref, back_ref,
    up_slot, down_slot, up_sem, down_sem,
):
    step = pl.program_id(0)
    last = pl.num_programs(0) - 1
    slot = step % 2
    height, width = up_ref.shape[2], up_ref.shape[3]

    @pl.when(step == 0)
    def _():
        mixed = (
            tokens_ref[...].astype(F32) + dg(attended_ref[...], out_ref[...], NN)
        ) + small_ref[6:7]
        mixed_ref[...] = mixed
        unit, unused = row_norm(mixed)
        second_ref[...] = (unit * small_ref[1:2] + small_ref[3:4]).astype(BF)
        second_t[...] = second_ref[...].T
        sum_ref[...] = jnp.zeros_like(sum_ref)
        back_ref[...] = jnp.zeros_like(back_ref)

    def up_copy(which, at):
        return pltpu.make_async_copy(
            up_slot.at[which],
            grads_ref.at[:, pl.ds(2 * at, 2), pl.ds(0, height), :],
            up_sem.at[which],
        )

    def down_copy(which, at):
        return pltpu.make_async_copy(
            down_slot.at[which],
            grads_ref.at[at, :, pl.ds(height, height), :],
            down_sem.at[which],
        )

    @pl.when(step >= 2)
    def _():
        up_copy(slot, step - 2).wait()
        down_copy(slot, step - 2).wait()

    full = up_ref.shape[0] * height
    up = jnp.concatenate([up_ref[:, i].reshape(full, width) for i in range(2)], axis=1)
    half = height // 2
    down = jnp.concatenate(
        [down_ref[0, :, i * half : (i + 1) * half, :].reshape(full, width) for i in range(2)],
        axis=1,
    )
    second, upstream = second_ref[...], upstream_ref[...]
    hidden = jnp.dot(second, up, preferred_element_type=F32) + shift_ref[...]
    grad_act = jnp.dot(upstream, down, preferred_element_type=F32)
    chance, slope = gelu_parts(hidden)
    active = (hidden * chance).astype(BF)
    grad_pre = grad_act * (chance + slope)
    grad_low = grad_pre.astype(BF)
    terms_ref[...] = jnp.sum(grad_pre, axis=0, keepdims=True)
    sum_ref[...] += dg(active, down, NT)
    back_ref[...] += dg(grad_low, up, NT)
    grad_up = jnp.dot(second_t[...], grad_low, preferred_element_type=F32).astype(BF)
    grad_down = jnp.dot(upstream_t[...], active, preferred_element_type=F32).astype(BF)
    for i in range(2):
        cut = slice(i * width, (i + 1) * width)
        up_slot[slot, :, i] = grad_up[:, cut].reshape(up_ref.shape[0], height, width)
        down_slot[slot, :, i * half : (i + 1) * half, :] = grad_down[:, cut].reshape(
            down_ref.shape[1], half, width
        )
    up_copy(slot, step).start()
    down_copy(slot, step).start()

    @pl.when(step == last)
    def _():
        up_copy(1 - slot, step - 1).wait()
        down_copy(1 - slot, step - 1).wait()
        mixed = mixed_ref[...]
        unit, scale = row_norm(mixed)
        output_ref[...] = (mixed + sum_ref[...] + small_ref[7:8]).astype(BF)
        grad_second = back_ref[...]
        upstream_f = upstream_ref[...].astype(F32)
        grad_mixed = upstream_f + row_norm_back(unit, scale, grad_second * small_ref[1:2])
        grad_mixed_ref[...] = grad_mixed
        mixed_low = grad_mixed.astype(BF)
        grad_att_ref[...] = dg(mixed_low, out_ref[...], NT).astype(BF)
        grad_out_ref[...] = jnp.dot(
            attended_ref[...].T, mixed_low, preferred_element_type=F32
        ).astype(BF)
        sums_ref[...] = jnp.zeros_like(sums_ref)
        sums_ref[0:1] = jnp.sum(grad_second * unit, axis=0, keepdims=True)
        sums_ref[1:2] = jnp.sum(grad_second, axis=0, keepdims=True)
        sums_ref[2:3] = jnp.sum(grad_mixed, axis=0, keepdims=True)
        sums_ref[3:4] = summed_ref[...]
        up_copy(slot, step).wait()
        down_copy(slot, step).wait()


def feed_forward(
    tokens_in, attended, w_out, small, upstream, turned, summed, up_weights, down_weights, shift
):
    tokens, width = tokens_in.shape
    rows, cols, half, wide = down_weights.shape
    block = whole((tokens, width))
    grid_spec = pltpu.PrefetchScalarGridSpec(
        num_scalar_prefetch=0,
        grid=(rows,),
        in_specs=[
            block,
            block,
            whole((width, width)),
            whole(small.shape),
            block,
            whole(turned.shape),
            whole(summed.shape),
            pl.BlockSpec((rows, 2, half, wide), lambda r: (0, r, 0, 0)),
            pl.BlockSpec((1, cols, half, wide), lambda r: (r, 0, 0, 0)),
            pl.BlockSpec((1, 2 * wide), lambda r: (0, r)),
        ],
        out_specs=[
            block,
            block,
            block,
            whole((width, width)),
            whole((8, width)),
            pl.BlockSpec((1, 2 * wide), lambda r: (0, r)),
            pl.BlockSpec(memory_space=pl.ANY),
        ],
        scratch_shapes=[
            pltpu.VMEM((tokens, width), BF),
            pltpu.VMEM((width, tokens), BF),
            pltpu.VMEM((tokens, width), F32),
            pltpu.VMEM((tokens, width), F32),
            pltpu.VMEM((tokens, width), F32),
            pltpu.VMEM((2, rows, 2, half, wide), BF),
            pltpu.VMEM((2, cols, half, wide), BF),
            pltpu.SemaphoreType.DMA((2,)),
            pltpu.SemaphoreType.DMA((2,)),
        ],
    )
    return pl.pallas_call(
        feed_kernel,
        grid_spec=grid_spec,
        out_shape=[
            jax.ShapeDtypeStruct((tokens, width), BF),
            jax.ShapeDtypeStruct((tokens, width), F32),
            jax.ShapeDtypeStruct((tokens, width), BF),
            jax.ShapeDtypeStruct((width, width), BF),
            jax.ShapeDtypeStruct((8, width), F32),
            jax.ShapeDtypeStruct((1, cols * wide), F32),
            jax.ShapeDtypeStruct((rows, cols, 2 * half, wide), BF),
        ],
        cost_estimate=pl.CostEstimate(
            flops=12 * tokens * width * cols * wide,
            bytes_accessed=24 << 20,
            transcendentals=2 * tokens * cols * wide,
        ),
        compiler_params=pltpu.CompilerParams(vmem_limit_bytes=60 << 20),
        name="feed_forward",
    )(tokens_in, attended, w_out, small, upstream, turned, summed, up_weights, down_weights, shift)


def swap(value, axis, bit):
    size = lax.axis_size(axis)
    return lax.ppermute(value, axis, [(i, i ^ bit) for i in range(size)])


def exchange(value, first):
    rows, cols = lax.axis_size("row"), lax.axis_size("col")
    pairs = []
    for r in range(rows):
        for c in range(cols):
            along_x = (r & 1 == 0) == first
            other = (r, c ^ 1) if along_x else (r ^ 2, c)
            pairs.append((r * cols + c, other[0] * cols + other[1]))
    return lax.ppermute(value, ("row", "col"), pairs)


def add_low(a, b):
    return (a.astype(jnp.float32) + b.astype(jnp.float32)).astype(jnp.bfloat16)


def place_of(col_index, y_step, of_core, me):
    d = col_index ^ me[0]
    x_step = d & 1
    near = jnp.where(of_core == 0, x_step, y_step)
    far = jnp.where(of_core == 0, y_step, x_step)
    return (d >> 1) | (near << 2) | (far << 3)


def in_order(flag, first, second):
    return jnp.where(flag > 0, second, first), jnp.where(flag > 0, first, second)


def halves(value, flags):
    return [
        jnp.where(flags[i] > 0, value[i * SEG : (i + 1) * SEG], jnp.zeros((), value.dtype))
        for i in range(2)
    ]


def placed(value, targets, numbers):
    out = []
    for number in numbers:
        parts = halves(value, [(targets[i] == number).astype(jnp.int32) for i in range(2)])
        out.append(parts[0] + parts[1])
    return jnp.concatenate(out, axis=0)


def level_move(value, pairs):
    cols = lax.axis_size("col")
    x_size = 2
    full = [
        (a * x_size + x, b * x_size + x)
        for a, b in pairs
        for x in range(x_size)
        if max(a, b) * x_size < cols
    ]
    return lax.ppermute(value, "col", full)


def together(*values):
    return lax.optimization_barrier(values)


def share_tokens(tokens, cotangent, own_slot, level):
    branch = placed(tokens, own_slot, (0, 1))
    branch_in = swap(placed(tokens, own_slot, (2, 3)), "col", 1)
    hop = level_move(tokens, [(0, 2)])
    branch_in, hop, cotangent = together(branch_in, hop, cotangent)
    turned, summed = turn(cotangent)
    branch_in, hop, turned = together(branch_in, hop, turned)
    branch = branch + branch_in
    moved = level_move(
        jnp.where(level == 1, branch, jnp.where(level == 0, tokens, hop)), [(0, 1), (1, 2), (2, 3)]
    )
    down = level_move(branch, [(3, 2)])
    trunk = jnp.where(level == 0, tokens, jnp.where(level == 2, hop, moved))
    branch_up = branch + jnp.where(level == 2, moved, jnp.zeros((), moved.dtype))
    up_two = level_move(branch_up, [(2, 3)])
    down_two = level_move(branch + down, [(2, 1)])
    trunk_far = swap(trunk, "col", 1)
    branch = (branch_up + down) + (up_two + down_two)
    return trunk, trunk_far, branch, swap(branch, "col", 1), turned, summed


def total(*parts):
    out = parts[0].astype(jnp.float32)
    for value in parts[1:]:
        out = out + value.astype(jnp.float32)
    return out


def tail_rounds(part, parent_slot, level, make_pieces, vectors_of):
    parent_part = part[4 * SEG :]
    keep, send = (placed(parent_part, parent_slot, pair) for pair in ((0, 1), (2, 3)))
    trunk, trunk_send, send = together(part[: 2 * SEG], part[2 * SEG : 4 * SEG], send)
    branch_in = swap(send, "col", 1)
    own, other, extra = make_pieces(trunk)
    terms = vectors_of(extra)

    branch = add_low(keep, branch_in)
    branch, trunk_send, other, terms = together(branch, trunk_send, other, terms)
    moves = (
        level_move(branch, [(1, 2)]),
        level_move(branch, [(3, 2)]),
        swap(trunk_send, "col", 1),
        swap(other, "row", 1),
        swap(terms, "row", 1),
    )
    up, down, trunk_in, own_in, terms_in = together(*moves)

    branch_up, branch_down = add_low(branch, up), add_low(branch, down)
    trunk = add_low(trunk, trunk_in)
    half = own.shape[0] // 2
    held = add_low(own[:half], own_in[:half])
    leaving = add_low(own[half:], own_in[half:])
    terms = terms + terms_in
    branch_up, branch_down, trunk, leaving, terms = together(
        branch_up, branch_down, trunk, leaving, terms
    )
    moves = (
        level_move(branch_up, [(2, 3)]),
        level_move(branch_down, [(2, 1)]),
        level_move(trunk, [(1, 0), (3, 2)]),
        exchange(leaving, False),
        swap(terms, "row", 2),
    )
    up_two, down_two, trunk_in, held_in, terms_in = together(*moves)

    branch = (
        branch_up.astype(jnp.float32)
        + down.astype(jnp.float32)
        + up_two.astype(jnp.float32)
        + down_two.astype(jnp.float32)
    ).astype(jnp.bfloat16)
    trunk = add_low(trunk, trunk_in)
    half = half // 2
    leaving = add_low(held[half:], held_in[half:])
    held = add_low(held[:half], held_in[:half])
    terms = terms + terms_in
    branch, trunk, leaving, terms = together(branch, trunk, leaving, terms)
    moves = (
        level_move(trunk, [(2, 0)]),
        swap(branch, "col", 1),
        exchange(leaving, True),
        swap(terms, "col", 1),
    )
    trunk_in, branch_far, held_in, terms_in = together(*moves)

    trunk = add_low(trunk, trunk_in)
    terms = terms + terms_in
    leaving = [add_low(held[k], held_in[k]) for k in range(1, 4)]
    kept = held[0].astype(jnp.float32) + held_in[0].astype(jnp.float32)
    *leaving, terms = together(*leaving, terms)
    moves = [swap(leaving[k - 1], "col", 2 * k) for k in range(1, 4)]
    terms_in = swap(terms, "col", 4)
    for moved in moves:
        kept = kept + moved.astype(jnp.float32)
    terms = terms + terms_in
    terms = terms + swap(terms, "col", 2)
    return trunk, branch, branch_far, kept, terms, extra


def tree_body(
    tokens, parents, w_qkv, w_out, w_up, w_down, ln_gain, ln_bias, proj_bias, ff_bias, cotangent
):
    row, col = lax.axis_index("row"), lax.axis_index("col")
    rows, cols = lax.axis_size("row"), lax.axis_size("col")
    local_rows = tokens.shape[0]
    side, level = col & 1, col >> 1
    me = jnp.stack([col, row >> 1, row & 1]).astype(jnp.int32)

    parent = parents[0]
    numbers = jnp.arange(SEGS, dtype=jnp.int32)
    is_branch = ((numbers >= 4) & (parent == 3)).astype(jnp.int32)

    def pick(array, number):
        return jnp.sum(jnp.where(numbers == number, array, 0))

    def slot(number):
        return jnp.sum(jnp.where(numbers < number, is_branch, 0)) ^ (2 * side)

    own = [2 * col + i for i in range(2)]
    own_parent = [pick(parent, number) for number in own]
    is_leaf = [number >= 4 for number in own_parent]
    own_slot = [jnp.where(pick(is_branch, number) > 0, slot(number), -1) for number in own]
    parent_slot = [jnp.where(is_leaf[i], slot(own_parent[i]), -1) for i in range(2)]
    meta = jnp.stack([2 * col, 2 * side] + [leaf.astype(jnp.int32) for leaf in is_leaf])

    narrow, wide = w_up.shape
    with jax.named_scope("gather_early_weights"):
        vectors = jnp.concatenate(
            [ln_gain, ln_bias, proj_bias, ff_bias.reshape(-1, ln_gain.shape[1])], axis=0
        ).reshape(-1, wide)
        count = vectors.shape[0]
        early = jnp.concatenate(
            [
                w_up,
                jnp.concatenate([w_qkv, w_out], axis=1),
                vectors,
                jnp.zeros((16 - count, wide), vectors.dtype),
            ],
            axis=0,
        )
        early = lax.all_gather(early, ("row", "col"), axis=0, tiled=False)
        early = early.reshape(rows, cols, *early.shape[1:])
        vectors = early[0, :, 2 * narrow : 2 * narrow + count]
        vectors = vectors.reshape(cols, -1, ln_gain.shape[1])
        small = vectors[:, :8].transpose(1, 0, 2).reshape(8, D).astype(jnp.float32)
        ff_shift = vectors[:, 8:].reshape(1, -1).astype(jnp.float32)
        full_qkv, full_out = join_pieces(early, narrow)
    with jax.named_scope("gather_tokens"):
        trunk, trunk_far, branch, branch_far, turned, summed = share_tokens(
            tokens, cotangent, own_slot, level
        )
        branch = jnp.concatenate([branch, branch_far], axis=0)
        parent_tokens = jnp.concatenate(
            [
                lax.dynamic_slice_in_dim(branch, jnp.maximum(parent_slot[i], 0) * SEG, SEG, 0)
                for i in range(2)
            ],
            axis=0,
        )
    with jax.named_scope("gather_late_weights"):
        late = jnp.concatenate([w_down.T[:, :wide], w_down.T[:, wide:]], axis=0)
        late = lax.all_gather(late, ("row", "col"), axis=0, tiled=False)
        late = late.reshape(rows, cols, *late.shape[1:])

    sources = (trunk, trunk_far, parent_tokens, tokens)
    queries, key_rows, value_rows, normed = project(sources, small, full_qkv)
    attended, inverse, chances = attn_fwd(meta, queries, key_rows, value_rows)
    output, grad_mixed, grad_att, grad_out, sums, ff_terms, late_grads = feed_forward(
        tokens, attended, full_out, small, cotangent, turned, summed, early, late, ff_shift
    )
    grad_q, grad_k, grad_v = attn_bwd(
        queries, key_rows, value_rows, grad_att, attended, inverse, chances
    )
    late_grads, grad_k = together(late_grads, grad_k)
    part, part_terms = unproject(sources[:3], grad_k, grad_v, full_qkv)
    with jax.named_scope("scatter_late_weights"):
        late_sum = lax.psum_scatter(
            late_grads.reshape(rows * cols, *late_grads.shape[2:]),
            ("row", "col"),
            scatter_dimension=0,
            tiled=False,
        ).astype(jnp.float32)
        up_rows, down_rows = w_up.shape[0], w_down.shape[1]
        grad_w_up = late_sum[:up_rows]
        grad_w_down = jnp.concatenate(
            [late_sum[up_rows : up_rows + down_rows], late_sum[up_rows + down_rows :]], axis=1
        ).T

    def make_pieces(after):
        dq, dk, dv, unused = together(grad_q, grad_k, grad_v, after)
        own, other, grad_normed, own_terms = weigh(
            me, dq, dk, dv, normed, tokens, grad_out, full_qkv, cols
        )
        return own, other, (grad_normed, own_terms)

    def vectors_of(extra):
        return jnp.concatenate([part_terms + extra[1], sums, ff_terms.reshape(-1, D)], axis=0)

    with jax.named_scope("sum_gradients"):
        trunk_grad, branch_grad, branch_grad_far, early_sum, terms, extra = tail_rounds(
            part, parent_slot, level, make_pieces, vectors_of
        )
    tall = w_qkv.shape[1]
    grad_w_qkv, grad_w_out = early_sum[:, :tall], early_sum[:, tall:]
    finish_meta = jnp.stack([level, own_slot[0], own_slot[1]]).astype(jnp.int32)
    grad_tokens = finish(
        finish_meta, trunk_grad, branch_grad, branch_grad_far, extra[0], grad_mixed, tokens, small
    )
    with jax.named_scope("vectors"):
        cut = ln_gain.shape[1]
        mine = lax.dynamic_slice_in_dim(terms[:16], col * cut, cut, 1)
        grad_ff = lax.dynamic_slice_in_dim(
            terms[16:].reshape(-1), col * ff_bias.shape[0], ff_bias.shape[0], 0
        )
        grad_gain = jnp.stack([mine[0], mine[8]])
        grad_shift = jnp.stack([mine[1], mine[9]])
        grad_bias = jnp.stack([mine[3], mine[2], mine[10], mine[11]])
    return (
        output,
        grad_tokens,
        grad_w_qkv,
        grad_w_out,
        grad_w_up,
        grad_w_down,
        grad_gain,
        grad_shift,
        grad_bias,
        grad_ff,
    )


def solution(mesh):
    fits = mesh.shape["col"] == 8 and mesh.shape["row"] == 4
    body = tree_body if fits else plain_body
    return jax.shard_map(
        body,
        mesh=mesh,
        in_specs=(
            P(("row", "col"), None),
            P("row", None),
            P("row", "col"),
            P("row", "col"),
            P("row", "col"),
            P("row", "col"),
            P(None, "col"),
            P(None, "col"),
            P(None, "col"),
            P("col"),
            P(("row", "col"), None),
        ),
        out_specs=(
            P(("row", "col"), None),
            P(("row", "col"), None),
            P("row", "col"),
            P("row", "col"),
            P("row", "col"),
            P("row", "col"),
            P(None, "col"),
            P(None, "col"),
            P(None, "col"),
            P("col"),
        ),
        check_vma=False,
    )
```

```python
import jax
import jax.numpy as jnp
from jax import lax
from jax.experimental import pallas as pl
from jax.experimental.pallas import tpu as pltpu
from jax.sharding import PartitionSpec as P

D = 768
HEADS = 12
HEAD_DIM = 64
SEG = 256
SEGS = 16
TREE_TOKENS = 4096


EPSILON = 1e-12
NEGATIVE = -1e30


def layer_norm(values, scaling, shifting):
    centre = values - jnp.mean(values, axis=-1, keepdims=True)
    spread = jnp.mean(centre * centre, axis=-1, keepdims=True)
    return centre * lax.rsqrt(spread + EPSILON) * scaling + shifting


def exact_gelu(values):
    return jax.nn.gelu(values, approximate=False)


def ancestry(parents):
    segment_count = parents.shape[0]
    labels = jnp.arange(segment_count, dtype=jnp.int32)
    closure = jnp.eye(segment_count, dtype=jnp.float32) + (
        parents[:, None] == labels[None, :]
    ).astype(jnp.float32)
    for repeat in range(segment_count.bit_length()):
        closure = jnp.minimum(jnp.dot(closure, closure, precision=lax.Precision.HIGHEST), 1.0)
    return closure


def allowed(query_pos, key_pos, closure):
    labels = jnp.arange(closure.shape[0], dtype=jnp.int32)
    query_seg = query_pos // SEG
    key_seg = key_pos // SEG
    query_hot = (query_seg[:, None] == labels[None, :]).astype(jnp.float32)
    key_hot = (key_seg[:, None] == labels[None, :]).astype(jnp.float32)
    reach = jnp.dot(
        jnp.dot(query_hot, closure, precision=lax.Precision.HIGHEST),
        key_hot.T,
        precision=lax.Precision.HIGHEST,
    )
    causal = (query_seg[:, None] != key_seg[None, :]) | (key_pos[None, :] <= query_pos[:, None])
    return (reach > 0.5) & causal


def plain_body(
    tokens, parents, w_qkv, w_out, w_up, w_down, ln_gain, ln_bias, proj_bias, ff_bias, cotangent
):
    local_rows = tokens.shape[0]
    score_scale = HEAD_DIM ** (-0.5)
    head_shape = (local_rows, HEADS, HEAD_DIM)
    block_rows = 2 * SEG
    block_count = SEGS // 2
    cols_qkv, cols_out, cols_up, cols_down, norm_gains, shifts, biases, ff_shift = (
        lax.all_gather(w_qkv, "col", axis=1, tiled=True),
        lax.all_gather(w_out, "col", axis=1, tiled=True),
        lax.all_gather(w_up, "col", axis=1, tiled=True),
        lax.all_gather(w_down, "col", axis=1, tiled=True),
        lax.all_gather(ln_gain, "col", axis=1, tiled=True),
        lax.all_gather(ln_bias, "col", axis=1, tiled=True),
        lax.all_gather(proj_bias, "col", axis=1, tiled=True),
        lax.all_gather(ff_bias, "col", axis=0, tiled=True),
    )
    full_qkv, full_out, full_up, full_down = (
        lax.all_gather(cols_qkv, "row", axis=0, tiled=True),
        lax.all_gather(cols_out, "row", axis=0, tiled=True),
        lax.all_gather(cols_up, "row", axis=0, tiled=True),
        lax.all_gather(cols_down, "row", axis=0, tiled=True),
    )
    norm_gains = norm_gains.astype(jnp.float32)
    shifts = shifts.astype(jnp.float32)
    biases = biases.astype(jnp.float32)
    ff_shift = ff_shift.astype(jnp.float32)
    inputs = tokens.astype(jnp.float32)
    normed_low = layer_norm(inputs, norm_gains[0], shifts[0]).astype(jnp.bfloat16)
    projected = jnp.dot(normed_low, full_qkv, preferred_element_type=jnp.float32)
    queries = (projected[:, :D] + biases[0]).astype(jnp.bfloat16).reshape(head_shape)
    keys_own = projected[:, D : 2 * D].astype(jnp.bfloat16).reshape(head_shape)
    values_own = (projected[:, 2 * D :] + biases[1]).astype(jnp.bfloat16).reshape(head_shape)
    keys_all, values_all = (
        lax.all_gather(keys_own, "col", axis=0, tiled=True),
        lax.all_gather(values_own, "col", axis=0, tiled=True),
    )
    key_blocks = keys_all.reshape(block_count, block_rows, HEADS, HEAD_DIM)
    value_blocks = values_all.reshape(block_count, block_rows, HEADS, HEAD_DIM)
    block_starts = jnp.arange(block_count, dtype=jnp.int32) * block_rows
    within = jnp.arange(block_rows, dtype=jnp.int32)
    query_pos = lax.axis_index("col") * local_rows + jnp.arange(local_rows, dtype=jnp.int32)
    closure = ancestry(parents[0])

    def scores_of(query_block, key_block, query_positions, key_positions):
        products = jnp.einsum(
            "qhd,khd->hqk", query_block, key_block, preferred_element_type=jnp.float32
        )
        return (products * score_scale, allowed(query_positions, key_positions, closure)[None])

    def probabilities(query_block, key_block, query_positions, key_positions, log_block):
        scores, visible = scores_of(query_block, key_block, query_positions, key_positions)
        return jnp.where(visible, jnp.exp(scores - log_block[..., None]), 0.0)

    def extent(running, pieces):
        highest_score, mass_total = running
        key_block, first_pos = pieces
        scores, visible = scores_of(queries, key_block, query_pos, first_pos + within)
        masked = jnp.where(visible, scores, NEGATIVE)
        new_highest = jnp.maximum(highest_score, jnp.max(masked, axis=-1))
        exp_terms = jnp.where(visible, jnp.exp(masked - new_highest[..., None]), 0.0)
        new_total = mass_total * jnp.exp(highest_score - new_highest) + jnp.sum(exp_terms, axis=-1)
        return ((new_highest, new_total), None)

    start_state = (
        jnp.full((HEADS, local_rows), NEGATIVE, jnp.float32),
        jnp.zeros((HEADS, local_rows), jnp.float32),
    )
    (highest_score, mass_total), unused = lax.scan(extent, start_state, (key_blocks, block_starts))
    log_total = highest_score + jnp.log(mass_total)

    def attend(running, pieces):
        key_block, value_block, first_pos = pieces
        chances = probabilities(
            queries, key_block, query_pos, first_pos + within, log_total
        ).astype(jnp.bfloat16)
        return (
            running
            + jnp.einsum("hqk,khd->qhd", chances, value_block, preferred_element_type=jnp.float32),
            None,
        )

    attended, unused = lax.scan(
        attend, jnp.zeros(head_shape, jnp.float32), (key_blocks, value_blocks, block_starts)
    )
    attended_low = attended.reshape(local_rows, D).astype(jnp.bfloat16)
    mixed_rows = (
        inputs + jnp.dot(attended_low, full_out, preferred_element_type=jnp.float32) + biases[2]
    )
    second_low = layer_norm(mixed_rows, norm_gains[1], shifts[1]).astype(jnp.bfloat16)
    hidden_pre = jnp.dot(second_low, full_up, preferred_element_type=jnp.float32) + ff_shift
    activated_low = exact_gelu(hidden_pre).astype(jnp.bfloat16)
    output = (
        mixed_rows
        + jnp.dot(activated_low, full_down, preferred_element_type=jnp.float32)
        + biases[3]
    )
    upstream = cotangent.astype(jnp.float32)
    grad_down = jnp.einsum(
        "tf,td->fd", activated_low, cotangent, preferred_element_type=jnp.float32
    )
    grad_act = jnp.einsum("td,fd->tf", cotangent, full_down, preferred_element_type=jnp.float32)
    unused, gelu_back = jax.vjp(exact_gelu, hidden_pre)
    grad_pre = gelu_back(grad_act)[0]
    grad_pre_low = grad_pre.astype(jnp.bfloat16)
    grad_up = jnp.einsum("td,tf->df", second_low, grad_pre_low, preferred_element_type=jnp.float32)
    grad_second = jnp.einsum("tf,df->td", grad_pre_low, full_up, preferred_element_type=jnp.float32)
    unused, second_back = jax.vjp(layer_norm, mixed_rows, norm_gains[1], shifts[1])
    grad_mixed_norm, grad_gain_two, grad_shift_two = second_back(grad_second)
    grad_mixed = upstream + grad_mixed_norm
    grad_mixed_low = grad_mixed.astype(jnp.bfloat16)
    grad_out = jnp.einsum(
        "td,te->de", attended_low, grad_mixed_low, preferred_element_type=jnp.float32
    )
    grad_att_low = (
        jnp.einsum("te,de->td", grad_mixed_low, full_out, preferred_element_type=jnp.float32)
        .astype(jnp.bfloat16)
        .reshape(head_shape)
    )
    deltas = jnp.einsum("qhd,qhd->hq", grad_att_low.astype(jnp.float32), attended)

    def score_grads(
        query_block,
        key_block,
        value_block,
        grad_block,
        query_positions,
        key_positions,
        log_block,
        delta_block,
    ):
        chances = probabilities(query_block, key_block, query_positions, key_positions, log_block)
        grad_chances = jnp.einsum(
            "qhd,khd->hqk", grad_block, value_block, preferred_element_type=jnp.float32
        )
        grad_scores = (chances * (grad_chances - delta_block[..., None]) * score_scale).astype(
            jnp.bfloat16
        )
        return (chances.astype(jnp.bfloat16), grad_scores)

    def backward_block(running, pieces):
        key_block, value_block, first_pos = pieces
        chances_low, grad_scores = score_grads(
            queries,
            key_block,
            value_block,
            grad_att_low,
            query_pos,
            first_pos + within,
            log_total,
            deltas,
        )
        running = running + jnp.einsum(
            "hqk,khd->qhd", grad_scores, key_block, preferred_element_type=jnp.float32
        )
        key_term = jnp.einsum(
            "hqk,qhd->khd", grad_scores, queries, preferred_element_type=jnp.float32
        )
        value_term = jnp.einsum(
            "hqk,qhd->khd", chances_low, grad_att_low, preferred_element_type=jnp.float32
        )
        return (running, (key_term, value_term))

    grad_queries, (key_terms, value_terms) = lax.scan(
        backward_block, jnp.zeros(head_shape, jnp.float32), (key_blocks, value_blocks, block_starts)
    )
    grad_keys, grad_values = (
        lax.psum_scatter(
            key_terms.reshape(TREE_TOKENS, D).astype(jnp.bfloat16),
            "col",
            scatter_dimension=0,
            tiled=True,
        ).astype(jnp.float32),
        lax.psum_scatter(
            value_terms.reshape(TREE_TOKENS, D).astype(jnp.bfloat16),
            "col",
            scatter_dimension=0,
            tiled=True,
        ).astype(jnp.float32),
    )
    grad_queries = grad_queries.reshape(local_rows, D)
    grad_projected_low = jnp.concatenate([grad_queries, grad_keys, grad_values], axis=1).astype(
        jnp.bfloat16
    )
    grad_qkv = jnp.einsum(
        "td,te->de", normed_low, grad_projected_low, preferred_element_type=jnp.float32
    )
    grad_normed = jnp.einsum(
        "te,de->td", grad_projected_low, full_qkv, preferred_element_type=jnp.float32
    )
    unused, first_back = jax.vjp(layer_norm, inputs, norm_gains[0], shifts[0])
    grad_input_norm, grad_gain_one, grad_shift_one = first_back(grad_normed)
    grad_tokens = (grad_mixed + grad_input_norm).astype(jnp.bfloat16)
    gain_terms = jnp.stack([grad_gain_one, grad_gain_two])
    shift_terms = jnp.stack([grad_shift_one, grad_shift_two])
    bias_terms = jnp.stack(
        [
            jnp.sum(grad_queries, axis=0),
            jnp.sum(grad_values, axis=0),
            jnp.sum(grad_mixed, axis=0),
            jnp.sum(upstream, axis=0),
        ]
    )
    ff_terms = jnp.sum(grad_pre, axis=0)
    part_qkv, part_out, part_up, part_down, part_gain, part_shift, part_bias, part_ff = (
        lax.psum_scatter(
            grad_qkv.astype(jnp.bfloat16), "col", scatter_dimension=1, tiled=True
        ).astype(jnp.float32),
        lax.psum_scatter(
            grad_out.astype(jnp.bfloat16), "col", scatter_dimension=1, tiled=True
        ).astype(jnp.float32),
        lax.psum_scatter(
            grad_up.astype(jnp.bfloat16), "col", scatter_dimension=1, tiled=True
        ).astype(jnp.float32),
        lax.psum_scatter(
            grad_down.astype(jnp.bfloat16), "col", scatter_dimension=1, tiled=True
        ).astype(jnp.float32),
        lax.psum_scatter(
            gain_terms.astype(jnp.bfloat16), "col", scatter_dimension=1, tiled=True
        ).astype(jnp.float32),
        lax.psum_scatter(
            shift_terms.astype(jnp.bfloat16), "col", scatter_dimension=1, tiled=True
        ).astype(jnp.float32),
        lax.psum_scatter(
            bias_terms.astype(jnp.bfloat16), "col", scatter_dimension=1, tiled=True
        ).astype(jnp.float32),
        lax.psum_scatter(
            ff_terms.astype(jnp.bfloat16), "col", scatter_dimension=0, tiled=True
        ).astype(jnp.float32),
    )
    grad_w_qkv, grad_w_out, grad_w_up, grad_w_down = (
        lax.psum_scatter(
            part_qkv.astype(jnp.bfloat16), "row", scatter_dimension=0, tiled=True
        ).astype(jnp.float32),
        lax.psum_scatter(
            part_out.astype(jnp.bfloat16), "row", scatter_dimension=0, tiled=True
        ).astype(jnp.float32),
        lax.psum_scatter(
            part_up.astype(jnp.bfloat16), "row", scatter_dimension=0, tiled=True
        ).astype(jnp.float32),
        lax.psum_scatter(
            part_down.astype(jnp.bfloat16), "row", scatter_dimension=0, tiled=True
        ).astype(jnp.float32),
    )
    grad_gain, grad_shift, grad_bias, grad_ff = lax.psum(
        (part_gain, part_shift, part_bias, part_ff), "row"
    )
    return (
        output.astype(jnp.bfloat16),
        grad_tokens,
        grad_w_qkv,
        grad_w_out,
        grad_w_up,
        grad_w_down,
        grad_gain,
        grad_shift,
        grad_bias,
        grad_ff,
    )


F32=jnp.float32; BF=jnp.bfloat16
NEG=NEGATIVE
NT=(((1,),(1,)),((),()))
NN=(((1,),(0,)),((),()))


def dg(a, b, dims):
    return lax.dot_general(a, b, dims, preferred_element_type=F32)


def chunk_rows(c, i):
    start = c * SEG if c < 4 else (4 + (c - 4) * 2 + i) * SEG
    return slice(start, start + SEG)


def pair_dot(c, keys_ref, rows):
    if c < 4:
        return dg(keys_ref[chunk_rows(c, 0), :], rows, NT)
    return jnp.concatenate(
        [
            dg(keys_ref[chunk_rows(c, i), :], rows[i * SEG : (i + 1) * SEG, :], NT)
            for i in range(2)
        ],
        axis=1,
    )


def score_chunk(c, k_ref, qh):
    scores = pair_dot(c, k_ref, qh)
    if c < 5:
        return scores
    key = lax.broadcasted_iota(jnp.int32, scores.shape, 0)
    query = lax.broadcasted_iota(jnp.int32, scores.shape, 1)
    return jnp.where(key <= (query & (SEG - 1)), scores, NEG)


def chunk_bias(c, meta):
    second = lax.broadcasted_iota(jnp.int32, (1, 2 * SEG), 1) // SEG
    if c < 4:
        return jnp.where((c ^ meta[1]) < meta[0] + second, 0.0, NEG)
    if c == 4:
        return jnp.where(jnp.where(second > 0, meta[3], meta[2]) > 0, 0.0, NEG)
    return jnp.zeros((1, 2 * SEG), F32)


def halves_of(value):
    lane = lax.broadcasted_iota(jnp.int32, value.shape, 1)
    zero = jnp.zeros((), value.dtype)
    return [jnp.where((lane < 64) == (h == 0), value, zero) for h in range(2)]


def fwd_kernel(meta, q_ref, k_ref, v_ref, o_ref, inverse_ref, p_ref):
    turned = v_ref[...].T
    biases = [chunk_bias(c, meta) for c in range(6)]
    results, inverses = [], []
    for h, qh in enumerate(halves_of(q_ref[...] * jnp.asarray(0.125, BF))):
        scores = [score_chunk(c, k_ref, qh) for c in range(6)]
        top = jnp.full((1, 2 * SEG), NEG, F32)
        for s, bias in zip(scores, biases):
            top = jnp.maximum(top, jnp.max(s, axis=0, keepdims=True) + bias)
        mass = jnp.zeros((1, 2 * SEG), F32)
        shared = jnp.zeros((128, 2 * SEG), F32)
        own = [jnp.zeros((128, SEG), F32)] * 2
        for c, s in enumerate(scores):
            p = jnp.exp(s - (top - biases[c]))
            mass = mass + jnp.sum(p, axis=0, keepdims=True)
            low = p.astype(BF)
            p_ref[0, (6 * h + c) * SEG : (6 * h + c + 1) * SEG, :] = low
            if c < 4:
                shared = shared + dg(turned[:, chunk_rows(c, 0)], low, NN)
            else:
                own = [
                    own[i] + dg(turned[:, chunk_rows(c, i)], low[:, i * SEG : (i + 1) * SEG], NN)
                    for i in range(2)
                ]
        inverse = jnp.broadcast_to(1.0 / mass, shared.shape)
        inverses.append(inverse)
        results.append((shared + jnp.concatenate(own, axis=1)) * inverse)
    row = lax.broadcasted_iota(jnp.int32, results[0].shape, 0)
    o_ref[...] = jnp.where(row < 64, results[0], results[1]).T.astype(BF)
    inverse_ref[...] = jnp.where(row < 64, inverses[0], inverses[1]).T


def bwd_kernel(q_ref, k_ref, v_ref, do_ref, o_ref, inverse_ref, p_ref, dq_ref, dk_ref, dv_ref):
    do = (do_ref[...].astype(F32) * inverse_ref[...]).astype(BF)
    products = (do.astype(F32) * o_ref[...].astype(F32)).T
    turned = k_ref[...].T
    qh = halves_of(q_ref[...] * jnp.asarray(0.125, BF))
    doh = halves_of(do)
    delta = [jnp.sum(products[h * 64 : (h + 1) * 64], axis=0, keepdims=True) for h in range(2)]
    shared = [jnp.zeros((128, 2 * SEG), F32)] * 2
    own = [[jnp.zeros((128, SEG), F32)] * 2] * 2
    for c in range(6):
        chances, slopes = [], []
        for h in range(2):
            p = p_ref[0, (6 * h + c) * SEG : (6 * h + c + 1) * SEG, :]
            ds = p.astype(F32) * (pair_dot(c, v_ref, doh[h]) - delta[h])
            chances.append(p)
            slopes.append(ds.astype(BF))
        for i in range(1 if c < 4 else 2):
            r = chunk_rows(c, i)
            cut = slice(0, 2 * SEG) if c < 4 else slice(i * SEG, (i + 1) * SEG)
            for ref, left, right in ((dv_ref, chances, doh), (dk_ref, slopes, qh)):
                ref[r, :] = dg(
                    jnp.concatenate([x[:, cut] for x in left], axis=1),
                    jnp.concatenate([x[cut] for x in right], axis=0),
                    NN,
                ).astype(BF)
        if c < 4:
            shared = [shared[h] + dg(turned[:, chunk_rows(c, 0)], slopes[h], NN) for h in range(2)]
        else:
            own = [
                [
                    own[h][i]
                    + dg(turned[:, chunk_rows(c, i)], slopes[h][:, i * SEG : (i + 1) * SEG], NN)
                    for i in range(2)
                ]
                for h in range(2)
            ]
    total_q = [shared[h] + jnp.concatenate(own[h], axis=1) for h in range(2)]
    row = lax.broadcasted_iota(jnp.int32, total_q[0].shape, 0)
    dq_ref[...] = (jnp.where(row < 64, total_q[0], total_q[1]).T * 0.125).astype(BF)


def attn_specs(rows, keys):
    return (
        pl.BlockSpec((rows, 128), lambda j, *unused: (0, j)),
        pl.BlockSpec((keys, 128), lambda j, *unused: (0, j)),
        pl.BlockSpec((1, 12 * SEG, rows), lambda j, *unused: (j, 0, 0)),
    )


def attn_fwd(meta, q, k, v):
    rows, width = q.shape
    pairs = width // 128
    q_spec, k_spec, p_spec = attn_specs(rows, k.shape[0])
    return call(
        fwd_kernel,
        "attn_fwd",
        (pairs,),
        [q_spec, k_spec, k_spec],
        [
            (q_spec, (q.shape, BF)),
            (q_spec, (q.shape, F32)),
            (p_spec, ((pairs, 12 * SEG, rows), BF)),
        ],
        prefetch=1,
        flops=2 * 2 * 12 * 12 * SEG**3,
        size=32 << 20,
        args=(meta, q, k, v),
    )


def attn_bwd(q, k, v, do, o, inverse, p):
    rows, width = q.shape
    pairs = width // 128
    q_spec, k_spec, p_spec = attn_specs(rows, k.shape[0])
    return call(
        bwd_kernel,
        "attn_bwd",
        (pairs,),
        [q_spec, k_spec, k_spec, q_spec, q_spec, q_spec, p_spec],
        [(q_spec, (q.shape, BF)), (k_spec, (k.shape, BF)), (k_spec, (k.shape, BF))],
        flops=4 * 2 * 12 * 12 * SEG**3,
        size=40 << 20,
        args=(q, k, v, do, o, inverse, p),
    )


def row_norm(values):
    centre = values - jnp.mean(values, axis=-1, keepdims=True)
    spread = jnp.mean(centre * centre, axis=-1, keepdims=True)
    scale = lax.rsqrt(spread + EPSILON)
    return centre * scale, scale


def row_norm_back(unit, scale, scaled):
    mean_one = jnp.mean(scaled, axis=-1, keepdims=True)
    mean_two = jnp.mean(scaled * unit, axis=-1, keepdims=True)
    return scale * (scaled - mean_one - unit * mean_two)


def call(kernel, name, grid, ins, outs, scratch=(), prefetch=0, flops=0, size=16 << 20, aliases=None, args=()):
    grid_spec = pltpu.PrefetchScalarGridSpec(
        num_scalar_prefetch=prefetch,
        grid=grid,
        in_specs=ins,
        out_specs=[spec for spec, unused in outs],
        scratch_shapes=list(scratch),
    )
    return pl.pallas_call(
        kernel,
        grid_spec=grid_spec,
        out_shape=[jax.ShapeDtypeStruct(*shape) for unused, shape in outs],
        cost_estimate=pl.CostEstimate(flops=flops, bytes_accessed=size, transcendentals=0),
        input_output_aliases=aliases or {},
        compiler_params=pltpu.CompilerParams(vmem_limit_bytes=58 << 20),
        name=name,
    )(*args)


def whole(shape):
    return pl.BlockSpec(shape, lambda *unused: (0,) * len(shape))


def join_kernel(pieces_ref, qkv_ref, out_ref):
    cols = pieces_ref.shape[1]
    cut = qkv_ref.shape[1] // cols
    qkv_ref[...] = jnp.concatenate([pieces_ref[0, c, :, :cut] for c in range(cols)], axis=1)
    out_ref[...] = jnp.concatenate([pieces_ref[0, c, :, cut:] for c in range(cols)], axis=1)


def join_pieces(pieces, height):
    rows, cols, unused, width = pieces.shape
    full = rows * height
    return call(
        join_kernel,
        "join_pieces",
        (rows,),
        [pl.BlockSpec((1, cols, height, width), lambda r: (r, 0, 1, 0))],
        [
            (pl.BlockSpec((height, 3 * full), lambda r: (r, 0)), ((full, 3 * full), BF)),
            (pl.BlockSpec((height, full), lambda r: (r, 0)), ((full, full), BF)),
        ],
        args=(pieces,),
    )


def turn_kernel(value_ref, turned_ref, sum_ref):
    turned_ref[...] = value_ref[...].T
    sum_ref[...] = jnp.sum(value_ref[...].astype(F32), axis=0, keepdims=True)


def turn(value):
    rows, width = value.shape
    return call(
        turn_kernel,
        "turn",
        (1,),
        [whole(value.shape)],
        [
            (whole((width, rows)), ((width, rows), BF)),
            (whole((1, width)), ((1, width), F32)),
        ],
        args=(value,),
    )


def select_source(step, sources, kept):
    for i, ref in enumerate(sources):

        @pl.when(step == i)
        def _(ref=ref):
            kept[...] = ref[...]

    return row_norm(kept[...].astype(F32))[0]


def project_rows(step, sources, small_ref, weight_ref, k_ref, v_ref, n_ref, kept):
    width = weight_ref.shape[0]
    unit = select_source(step, sources, kept)
    normed = (unit * small_ref[0:1] + small_ref[2:3]).astype(BF)
    n_ref[...] = normed
    k_ref[...] = dg(normed, weight_ref[:, width : 2 * width], NN).astype(BF)
    v_ref[...] = (dg(normed, weight_ref[:, 2 * width :], NN) + small_ref[5:6]).astype(BF)
    return normed


def project_kernel(a_ref, b_ref, c_ref, small_ref, weight_ref, q_ref, k_ref, v_ref, n_ref, kept):
    step = pl.program_id(0)
    width = a_ref.shape[1]
    sources = (a_ref, b_ref, c_ref)
    normed = project_rows(step, sources, small_ref, weight_ref, k_ref, v_ref, n_ref, kept)

    @pl.when(step == pl.num_programs(0) - 1)
    def _():
        q_ref[...] = (dg(normed, weight_ref[:, :width], NN) + small_ref[4:5]).astype(BF)


def project(sources, small, qkv):
    tokens, width = sources[0].shape
    block = pl.BlockSpec((tokens, width), lambda i: (i + i // 2, 0))
    tall = ((4 * tokens, width), BF)
    return call(
        project_kernel,
        "project",
        (3,),
        [whole((tokens, width))] * 3 + [whole(small.shape), whole(qkv.shape)],
        [(whole((tokens, width)), ((tokens, width), BF)), (block, tall), (block, tall), (block, tall)],
        scratch=[pltpu.VMEM((tokens, width), BF)],
        flops=2 * 7 * tokens * width * width,
        args=(*sources, small, qkv),
    )


def project_parents_kernel(
    a_ref, small_ref, weight_ref, old_k, old_v, old_n, k_ref, v_ref, n_ref, kept
):
    project_rows(0, (a_ref,), small_ref, weight_ref, k_ref, v_ref, n_ref, kept)


def project_parents(source, small, qkv, *others):
    tokens, width = source.shape
    block = pl.BlockSpec((tokens, width), lambda i: (2, 0))
    tall = ((4 * tokens, width), BF)
    anywhere = pl.BlockSpec(memory_space=pl.ANY)
    return call(
        project_parents_kernel,
        "project_parents",
        (1,),
        [whole((tokens, width)), whole(small.shape), whole(qkv.shape)] + [anywhere] * 3,
        [(block, tall)] * 3,
        scratch=[pltpu.VMEM((tokens, width), BF)],
        flops=2 * 2 * tokens * width * width,
        aliases={3: 0, 4: 1, 5: 2},
        args=(source, small, qkv, *others),
    )


def unproject_kernel(
    a_ref, b_ref, c_ref, dk_ref, dv_ref, k_ref, v_ref, part_ref, terms_ref, kept
):
    step = pl.program_id(0)

    @pl.when(step == 0)
    def _():
        terms_ref[...] = jnp.zeros_like(terms_ref)

    dk, dv = dk_ref[...], dv_ref[...]
    grad = dg(dk, k_ref[...], NT) + dg(dv, v_ref[...], NT)
    part_ref[...] = grad.astype(BF)
    unit = select_source(step, (a_ref, b_ref, c_ref), kept)
    terms_ref[0:1] += jnp.sum(grad * unit, axis=0, keepdims=True)
    terms_ref[1:2] += jnp.sum(grad, axis=0, keepdims=True)
    terms_ref[2:3] += jnp.sum(dv.astype(F32), axis=0, keepdims=True)


def unproject(sources, dk, dv, qkv):
    tokens, width = sources[0].shape
    count = len(sources)
    block = pl.BlockSpec((tokens, width), lambda i: (i, 0))
    return call(
        unproject_kernel,
        "unproject",
        (count,),
        [whole((tokens, width))] * count
        + [block, block]
        + [pl.BlockSpec((width, width), lambda i, n=n: (0, n)) for n in (1, 2)],
        [(block, ((count * tokens, width), BF)), (whole((8, width)), ((8, width), F32))],
        scratch=[pltpu.VMEM((tokens, width), BF)],
        flops=2 * 2 * count * tokens * width * width,
        args=(*sources, dk, dv, qkv, qkv),
    )


def weigh_kernel(
    me, dq_ref, dk_ref, dv_ref, n_ref, tokens_ref, grad_out_ref, weight_ref,
    own_ref, other_ref, grad_ref, terms_ref, kept, turned,
):
    step = pl.program_id(0)
    tokens, width = dq_ref.shape

    @pl.when(step == 0)
    def _():
        dq, dk, dv = dq_ref[...], dk_ref[-tokens:], dv_ref[-tokens:]
        grad = (
            dg(dq, weight_ref[:, :width], NT)
            + dg(dk, weight_ref[:, width : 2 * width], NT)
            + dg(dv, weight_ref[:, 2 * width :], NT)
        )
        grad_ref[...] = grad
        unit, unused = row_norm(tokens_ref[...].astype(F32))
        terms_ref[...] = jnp.zeros_like(terms_ref)
        terms_ref[0:1] = jnp.sum(grad * unit, axis=0, keepdims=True)
        terms_ref[1:2] = jnp.sum(grad, axis=0, keepdims=True)
        terms_ref[2:3] = jnp.sum(dv.astype(F32), axis=0, keepdims=True)
        terms_ref[3:4] = jnp.sum(dq.astype(F32), axis=0, keepdims=True)
        turned[...] = n_ref[...].T
        kept[:, :width] = dg(turned[:, -tokens:], dq, NN).astype(BF)

    @pl.when(step == 1)
    def _():
        kept[:, width : 2 * width] = dg(turned[...], dk_ref[...], NN).astype(BF)

    @pl.when(step == 2)
    def _():
        kept[:, 2 * width :] = dg(turned[...], dv_ref[...], NN).astype(BF)
        height = own_ref.shape[1]
        cols = own_ref.shape[0] // 2
        tall, low_part = 3 * width // cols, width // cols
        for c in range(cols):
            parts = [
                jnp.concatenate(
                    [
                        kept[r * height : (r + 1) * height, c * tall : (c + 1) * tall],
                        grad_out_ref[r * height : (r + 1) * height, c * low_part : (c + 1) * low_part],
                    ],
                    axis=1,
                )
                for r in range(4)
            ]
            a, c_part = in_order(me[1], parts[0], parts[2])
            b, d_part = in_order(me[1], parts[1], parts[3])
            for y_step, pair in ((0, (a, b)), (1, (c_part, d_part))):
                mine, theirs = in_order(me[2], *pair)
                own_ref[place_of(c, y_step, me[2], me)] = mine
                other_ref[place_of(c, y_step, me[2] ^ 1, me)] = theirs


def weigh(me, dq, dk, dv, normed, tokens, grad_out, qkv, cols):
    count, width = dq.shape
    shape = (2 * cols, width // 4, 4 * width // cols)
    return call(
        weigh_kernel,
        "weigh",
        (3,),
        [whole(x.shape) for x in (dq, dk, dv, normed, tokens, grad_out, qkv)],
        [
            (whole(shape), (shape, BF)),
            (whole(shape), (shape, BF)),
            (whole((count, width)), ((count, width), F32)),
            (whole((8, width)), ((8, width), F32)),
        ],
        scratch=[pltpu.VMEM((width, 3 * width), BF), pltpu.VMEM((width, normed.shape[0]), BF)],
        prefetch=1,
        flops=2 * 12 * count * width * width,
        args=(me, dq, dk, dv, normed, tokens, grad_out, qkv),
    )


def finish_kernel(
    meta, trunk_ref, near_ref, far_ref, own_ref, mixed_ref, tokens_ref, small_ref, out_ref
):
    slot = meta[1 + pl.program_id(0)]
    place = pl.ds(pl.multiple_of((jnp.maximum(slot, 0) & 1) * SEG, SEG), SEG)
    branch = jnp.where(slot >= 2, far_ref[place, :], near_ref[place, :]).astype(F32)
    branch = jnp.where(slot >= 0, branch, 0.0)
    trunk = trunk_ref[...].astype(F32)
    grad = own_ref[...] + jnp.where(meta[0] == 0, trunk, branch)
    unit, scale = row_norm(tokens_ref[...].astype(F32))
    back = row_norm_back(unit, scale, grad * small_ref[0:1])
    out_ref[...] = (mixed_ref[...] + back).astype(BF)


def finish(meta, trunk, near, far, own, mixed, tokens, small):
    width = tokens.shape[1]
    part = pl.BlockSpec((SEG, width), lambda i, meta: (i, 0))
    full = whole(near.shape)
    return call(
        finish_kernel,
        "finish",
        (2,),
        [part, full, full, part, part, part, whole(small.shape)],
        [(part, (tokens.shape, BF))],
        prefetch=1,
        args=(meta, trunk, near, far, own, mixed, tokens, small),
    )[0]


def gelu_parts(v):
    x = v * 0.7071067811865476
    chance = 0.5 + 0.5 * lax.erf(x)
    density = jnp.exp(-x * x) * 0.3989422804014327
    return chance, v * density


def feed_kernel(
    tokens_ref, attended_ref, out_ref, small_ref, upstream_ref, upstream_t, summed_ref, up_ref, down_ref,
    shift_ref,
    output_ref, grad_mixed_ref, grad_att_ref, grad_out_ref, sums_ref, terms_ref, grads_ref,
    second_ref, second_t, mixed_ref, sum_ref, back_ref,
    up_slot, down_slot, up_sem, down_sem,
):
    step = pl.program_id(0)
    last = pl.num_programs(0) - 1
    slot = step % 2
    height, width = up_ref.shape[2], up_ref.shape[3]

    @pl.when(step == 0)
    def _():
        mixed = (
            tokens_ref[...].astype(F32) + dg(attended_ref[...], out_ref[...], NN)
        ) + small_ref[6:7]
        mixed_ref[...] = mixed
        unit, unused = row_norm(mixed)
        second_ref[...] = (unit * small_ref[1:2] + small_ref[3:4]).astype(BF)
        second_t[...] = second_ref[...].T
        sum_ref[...] = jnp.zeros_like(sum_ref)
        back_ref[...] = jnp.zeros_like(back_ref)

    def up_copy(which, at):
        return pltpu.make_async_copy(
            up_slot.at[which],
            grads_ref.at[:, pl.ds(2 * at, 2), pl.ds(0, height), :],
            up_sem.at[which],
        )

    def down_copy(which, at):
        return pltpu.make_async_copy(
            down_slot.at[which],
            grads_ref.at[at, :, pl.ds(height, height), :],
            down_sem.at[which],
        )

    @pl.when(step >= 2)
    def _():
        up_copy(slot, step - 2).wait()
        down_copy(slot, step - 2).wait()

    full = up_ref.shape[0] * height
    up = jnp.concatenate([up_ref[:, i].reshape(full, width) for i in range(2)], axis=1)
    half = height // 2
    down = jnp.concatenate(
        [down_ref[0, :, i * half : (i + 1) * half, :].reshape(full, width) for i in range(2)],
        axis=1,
    )
    second, upstream = second_ref[...], upstream_ref[...]
    hidden = jnp.dot(second, up, preferred_element_type=F32) + shift_ref[...]
    grad_act = jnp.dot(upstream, down, preferred_element_type=F32)
    chance, slope = gelu_parts(hidden)
    active = (hidden * chance).astype(BF)
    grad_pre = grad_act * (chance + slope)
    grad_low = grad_pre.astype(BF)
    terms_ref[...] = jnp.sum(grad_pre, axis=0, keepdims=True)
    sum_ref[...] += dg(active, down, NT)
    back_ref[...] += dg(grad_low, up, NT)
    grad_up = jnp.dot(second_t[...], grad_low, preferred_element_type=F32).astype(BF)
    grad_down = jnp.dot(upstream_t[...], active, preferred_element_type=F32).astype(BF)
    for i in range(2):
        cut = slice(i * width, (i + 1) * width)
        up_slot[slot, :, i] = grad_up[:, cut].reshape(up_ref.shape[0], height, width)
        down_slot[slot, :, i * half : (i + 1) * half, :] = grad_down[:, cut].reshape(
            down_ref.shape[1], half, width
        )
    up_copy(slot, step).start()
    down_copy(slot, step).start()

    @pl.when(step == last)
    def _():
        up_copy(1 - slot, step - 1).wait()
        down_copy(1 - slot, step - 1).wait()
        mixed = mixed_ref[...]
        unit, scale = row_norm(mixed)
        output_ref[...] = (mixed + sum_ref[...] + small_ref[7:8]).astype(BF)
        grad_second = back_ref[...]
        upstream_f = upstream_ref[...].astype(F32)
        grad_mixed = upstream_f + row_norm_back(unit, scale, grad_second * small_ref[1:2])
        grad_mixed_ref[...] = grad_mixed
        mixed_low = grad_mixed.astype(BF)
        grad_att_ref[...] = dg(mixed_low, out_ref[...], NT).astype(BF)
        grad_out_ref[...] = jnp.dot(
            attended_ref[...].T, mixed_low, preferred_element_type=F32
        ).astype(BF)
        sums_ref[...] = jnp.zeros_like(sums_ref)
        sums_ref[0:1] = jnp.sum(grad_second * unit, axis=0, keepdims=True)
        sums_ref[1:2] = jnp.sum(grad_second, axis=0, keepdims=True)
        sums_ref[2:3] = jnp.sum(grad_mixed, axis=0, keepdims=True)
        sums_ref[3:4] = summed_ref[...]
        up_copy(slot, step).wait()
        down_copy(slot, step).wait()


def feed_forward(
    tokens_in, attended, w_out, small, upstream, turned, summed, up_weights, down_weights, shift
):
    tokens, width = tokens_in.shape
    rows, cols, half, wide = down_weights.shape
    block = whole((tokens, width))
    grid_spec = pltpu.PrefetchScalarGridSpec(
        num_scalar_prefetch=0,
        grid=(rows,),
        in_specs=[
            block,
            block,
            whole((width, width)),
            whole(small.shape),
            block,
            whole(turned.shape),
            whole(summed.shape),
            pl.BlockSpec((rows, 2, half, wide), lambda r: (0, r, 0, 0)),
            pl.BlockSpec((1, cols, half, wide), lambda r: (r, 0, 0, 0)),
            pl.BlockSpec((1, 2 * wide), lambda r: (0, r)),
        ],
        out_specs=[
            block,
            block,
            block,
            whole((width, width)),
            whole((8, width)),
            pl.BlockSpec((1, 2 * wide), lambda r: (0, r)),
            pl.BlockSpec(memory_space=pl.ANY),
        ],
        scratch_shapes=[
            pltpu.VMEM((tokens, width), BF),
            pltpu.VMEM((width, tokens), BF),
            pltpu.VMEM((tokens, width), F32),
            pltpu.VMEM((tokens, width), F32),
            pltpu.VMEM((tokens, width), F32),
            pltpu.VMEM((2, rows, 2, half, wide), BF),
            pltpu.VMEM((2, cols, half, wide), BF),
            pltpu.SemaphoreType.DMA((2,)),
            pltpu.SemaphoreType.DMA((2,)),
        ],
    )
    return pl.pallas_call(
        feed_kernel,
        grid_spec=grid_spec,
        out_shape=[
            jax.ShapeDtypeStruct((tokens, width), BF),
            jax.ShapeDtypeStruct((tokens, width), F32),
            jax.ShapeDtypeStruct((tokens, width), BF),
            jax.ShapeDtypeStruct((width, width), BF),
            jax.ShapeDtypeStruct((8, width), F32),
            jax.ShapeDtypeStruct((1, cols * wide), F32),
            jax.ShapeDtypeStruct((rows, cols, 2 * half, wide), BF),
        ],
        cost_estimate=pl.CostEstimate(
            flops=12 * tokens * width * cols * wide,
            bytes_accessed=24 << 20,
            transcendentals=2 * tokens * cols * wide,
        ),
        compiler_params=pltpu.CompilerParams(vmem_limit_bytes=60 << 20),
        name="feed_forward",
    )(tokens_in, attended, w_out, small, upstream, turned, summed, up_weights, down_weights, shift)


def swap(value, axis, bit):
    size = lax.axis_size(axis)
    return lax.ppermute(value, axis, [(i, i ^ bit) for i in range(size)])


def exchange(value, first):
    rows, cols = lax.axis_size("row"), lax.axis_size("col")
    pairs = []
    for r in range(rows):
        for c in range(cols):
            along_x = (r & 1 == 0) == first
            other = (r, c ^ 1) if along_x else (r ^ 2, c)
            pairs.append((r * cols + c, other[0] * cols + other[1]))
    return lax.ppermute(value, ("row", "col"), pairs)


def add_low(a, b):
    return (a.astype(jnp.float32) + b.astype(jnp.float32)).astype(jnp.bfloat16)


def place_of(col_index, y_step, of_core, me):
    d = col_index ^ me[0]
    x_step = d & 1
    near = jnp.where(of_core == 0, x_step, y_step)
    far = jnp.where(of_core == 0, y_step, x_step)
    return (d >> 1) | (near << 2) | (far << 3)


def in_order(flag, first, second):
    return jnp.where(flag > 0, second, first), jnp.where(flag > 0, first, second)


def halves(value, flags):
    return [
        jnp.where(flags[i] > 0, value[i * SEG : (i + 1) * SEG], jnp.zeros((), value.dtype))
        for i in range(2)
    ]


def placed(value, targets, numbers):
    out = []
    for number in numbers:
        parts = halves(value, [(targets[i] == number).astype(jnp.int32) for i in range(2)])
        out.append(parts[0] + parts[1])
    return jnp.concatenate(out, axis=0)


def level_move(value, pairs):
    cols = lax.axis_size("col")
    x_size = 2
    full = [
        (a * x_size + x, b * x_size + x)
        for a, b in pairs
        for x in range(x_size)
        if max(a, b) * x_size < cols
    ]
    return lax.ppermute(value, "col", full)


def together(*values):
    return lax.optimization_barrier(values)


def share_tokens(tokens, cotangent, own_slot, level):
    branch = placed(tokens, own_slot, (0, 1))
    branch_in = swap(placed(tokens, own_slot, (2, 3)), "col", 1)
    hop = level_move(tokens, [(0, 2)])
    branch_in, hop, cotangent = together(branch_in, hop, cotangent)
    turned, summed = turn(cotangent)
    branch_in, hop, turned = together(branch_in, hop, turned)
    branch = branch + branch_in
    moved = level_move(
        jnp.where(level == 1, branch, jnp.where(level == 0, tokens, hop)), [(0, 1), (1, 2), (2, 3)]
    )
    down = level_move(branch, [(3, 2)])
    trunk = jnp.where(level == 0, tokens, jnp.where(level == 2, hop, moved))
    branch_up = branch + jnp.where(level == 2, moved, jnp.zeros((), moved.dtype))
    up_two = level_move(branch_up, [(2, 3)])
    down_two = level_move(branch + down, [(2, 1)])
    trunk_far = swap(trunk, "col", 1)
    up_two, down_two, trunk_far = together(up_two, down_two, trunk_far)
    branch = (branch_up + down) + (up_two + down_two)
    return trunk, trunk_far, branch, turned, summed


def total(*parts):
    out = parts[0].astype(jnp.float32)
    for value in parts[1:]:
        out = out + value.astype(jnp.float32)
    return out


def tail_rounds(part, parent_slot, level, make_pieces, vectors_of):
    parent_part = part[4 * SEG :]
    keep, send = (placed(parent_part, parent_slot, pair) for pair in ((0, 1), (2, 3)))
    trunk, trunk_send, send = together(part[: 2 * SEG], part[2 * SEG : 4 * SEG], send)
    branch_in = swap(send, "col", 1)
    own, other, extra = make_pieces(trunk)
    terms = vectors_of(extra)

    branch = add_low(keep, branch_in)
    branch, trunk_send, other, terms = together(branch, trunk_send, other, terms)
    moves = (
        level_move(branch, [(1, 2)]),
        level_move(branch, [(3, 2)]),
        swap(trunk_send, "col", 1),
        swap(other, "row", 1),
        swap(terms, "row", 1),
    )
    up, down, trunk_in, own_in, terms_in = together(*moves)

    branch_up, branch_down = add_low(branch, up), add_low(branch, down)
    trunk = add_low(trunk, trunk_in)
    half = own.shape[0] // 2
    held = add_low(own[:half], own_in[:half])
    leaving = add_low(own[half:], own_in[half:])
    terms = terms + terms_in
    branch_up, branch_down, trunk, leaving, terms = together(
        branch_up, branch_down, trunk, leaving, terms
    )
    moves = (
        level_move(branch_up, [(2, 3)]),
        level_move(branch_down, [(2, 1)]),
        level_move(trunk, [(1, 0), (3, 2)]),
        exchange(leaving, False),
        swap(terms, "row", 2),
    )
    up_two, down_two, trunk_in, held_in, terms_in = together(*moves)

    branch = (
        branch_up.astype(jnp.float32)
        + down.astype(jnp.float32)
        + up_two.astype(jnp.float32)
        + down_two.astype(jnp.float32)
    ).astype(jnp.bfloat16)
    trunk = add_low(trunk, trunk_in)
    half = half // 2
    leaving = add_low(held[half:], held_in[half:])
    held = add_low(held[:half], held_in[:half])
    terms = terms + terms_in
    branch, trunk, leaving, terms = together(branch, trunk, leaving, terms)
    moves = (
        level_move(trunk, [(2, 0)]),
        swap(branch, "col", 1),
        exchange(leaving, True),
        swap(terms, "col", 1),
    )
    trunk_in, branch_far, held_in, terms_in = together(*moves)

    trunk = add_low(trunk, trunk_in)
    terms = terms + terms_in
    leaving = [add_low(held[k], held_in[k]) for k in range(1, 4)]
    kept = held[0].astype(jnp.float32) + held_in[0].astype(jnp.float32)
    *leaving, terms = together(*leaving, terms)
    moves = [swap(leaving[k - 1], "col", 2 * k) for k in range(1, 4)]
    terms_in = swap(terms, "col", 4)
    for moved in moves:
        kept = kept + moved.astype(jnp.float32)
    terms = terms + terms_in
    terms = terms + swap(terms, "col", 2)
    return trunk, branch, branch_far, kept, terms, extra


def tree_body(
    tokens, parents, w_qkv, w_out, w_up, w_down, ln_gain, ln_bias, proj_bias, ff_bias, cotangent
):
    row, col = lax.axis_index("row"), lax.axis_index("col")
    rows, cols = lax.axis_size("row"), lax.axis_size("col")
    local_rows = tokens.shape[0]
    side, level = col & 1, col >> 1
    me = jnp.stack([col, row >> 1, row & 1]).astype(jnp.int32)

    parent = parents[0]
    numbers = jnp.arange(SEGS, dtype=jnp.int32)
    is_branch = ((numbers >= 4) & (parent == 3)).astype(jnp.int32)

    def pick(array, number):
        return jnp.sum(jnp.where(numbers == number, array, 0))

    def slot(number):
        return jnp.sum(jnp.where(numbers < number, is_branch, 0)) ^ (2 * side)

    own = [2 * col + i for i in range(2)]
    own_parent = [pick(parent, number) for number in own]
    is_leaf = [number >= 4 for number in own_parent]
    own_slot = [jnp.where(pick(is_branch, number) > 0, slot(number), -1) for number in own]
    parent_slot = [jnp.where(is_leaf[i], slot(own_parent[i]), -1) for i in range(2)]
    meta = jnp.stack([2 * col, 2 * side] + [leaf.astype(jnp.int32) for leaf in is_leaf])

    narrow, wide = w_up.shape
    with jax.named_scope("gather_early_weights"):
        vectors = jnp.concatenate(
            [ln_gain, ln_bias, proj_bias, ff_bias.reshape(-1, ln_gain.shape[1])], axis=0
        ).reshape(-1, wide)
        count = vectors.shape[0]
        early = jnp.concatenate(
            [
                w_up,
                jnp.concatenate([w_qkv, w_out], axis=1),
                vectors,
                jnp.zeros((16 - count, wide), vectors.dtype),
            ],
            axis=0,
        )
        early = lax.all_gather(early, ("row", "col"), axis=0, tiled=False)
        early = early.reshape(rows, cols, *early.shape[1:])
        vectors = early[0, :, 2 * narrow : 2 * narrow + count]
        vectors = vectors.reshape(cols, -1, ln_gain.shape[1])
        small = vectors[:, :8].transpose(1, 0, 2).reshape(8, D).astype(jnp.float32)
        ff_shift = vectors[:, 8:].reshape(1, -1).astype(jnp.float32)
        full_qkv, full_out = join_pieces(early, narrow)
    with jax.named_scope("gather_tokens"):
        trunk, trunk_far, branch, turned, summed = share_tokens(
            tokens, cotangent, own_slot, level
        )
        branch_far = swap(branch, "col", 1)
    with jax.named_scope("gather_late_weights"):
        late = jnp.concatenate([w_down.T[:, :wide], w_down.T[:, wide:]], axis=0)
        late = lax.all_gather(late, ("row", "col"), axis=0, tiled=False)
        late = late.reshape(rows, cols, *late.shape[1:])

    queries, *rows_of = project((trunk, trunk_far, tokens), small, full_qkv)
    branch_far, queries = together(branch_far, queries)
    branch = jnp.concatenate([branch, branch_far], axis=0)
    parent_tokens = jnp.concatenate(
        [
            lax.dynamic_slice_in_dim(branch, jnp.maximum(parent_slot[i], 0) * SEG, SEG, 0)
            for i in range(2)
        ],
        axis=0,
    )
    key_rows, value_rows, normed = project_parents(parent_tokens, small, full_qkv, *rows_of)
    sources = (trunk, trunk_far, parent_tokens)
    attended, inverse, chances = attn_fwd(meta, queries, key_rows, value_rows)
    output, grad_mixed, grad_att, grad_out, sums, ff_terms, late_grads = feed_forward(
        tokens, attended, full_out, small, cotangent, turned, summed, early, late, ff_shift
    )
    grad_q, grad_k, grad_v = attn_bwd(
        queries, key_rows, value_rows, grad_att, attended, inverse, chances
    )
    late_grads, grad_k = together(late_grads, grad_k)
    part, part_terms = unproject(sources, grad_k, grad_v, full_qkv)
    with jax.named_scope("scatter_late_weights"):
        late_sum = lax.psum_scatter(
            late_grads.reshape(rows * cols, *late_grads.shape[2:]),
            ("row", "col"),
            scatter_dimension=0,
            tiled=False,
        ).astype(jnp.float32)
        up_rows, down_rows = w_up.shape[0], w_down.shape[1]
        grad_w_up = late_sum[:up_rows]
        grad_w_down = jnp.concatenate(
            [late_sum[up_rows : up_rows + down_rows], late_sum[up_rows + down_rows :]], axis=1
        ).T

    def make_pieces(after):
        dq, dk, dv, unused = together(grad_q, grad_k, grad_v, after)
        own, other, grad_normed, own_terms = weigh(
            me, dq, dk, dv, normed, tokens, grad_out, full_qkv, cols
        )
        return own, other, (grad_normed, own_terms)

    def vectors_of(extra):
        return jnp.concatenate([part_terms + extra[1], sums, ff_terms.reshape(-1, D)], axis=0)

    with jax.named_scope("sum_gradients"):
        trunk_grad, branch_grad, branch_grad_far, early_sum, terms, extra = tail_rounds(
            part, parent_slot, level, make_pieces, vectors_of
        )
    tall = w_qkv.shape[1]
    grad_w_qkv, grad_w_out = early_sum[:, :tall], early_sum[:, tall:]
    finish_meta = jnp.stack([level, own_slot[0], own_slot[1]]).astype(jnp.int32)
    grad_tokens = finish(
        finish_meta, trunk_grad, branch_grad, branch_grad_far, extra[0], grad_mixed, tokens, small
    )
    with jax.named_scope("vectors"):
        cut = ln_gain.shape[1]
        mine = lax.dynamic_slice_in_dim(terms[:16], col * cut, cut, 1)
        grad_ff = lax.dynamic_slice_in_dim(
            terms[16:].reshape(-1), col * ff_bias.shape[0], ff_bias.shape[0], 0
        )
        grad_gain = jnp.stack([mine[0], mine[8]])
        grad_shift = jnp.stack([mine[1], mine[9]])
        grad_bias = jnp.stack([mine[3], mine[2], mine[10], mine[11]])
    return (
        output,
        grad_tokens,
        grad_w_qkv,
        grad_w_out,
        grad_w_up,
        grad_w_down,
        grad_gain,
        grad_shift,
        grad_bias,
        grad_ff,
    )


def solution(mesh):
    fits = mesh.shape["col"] == 8 and mesh.shape["row"] == 4
    body = tree_body if fits else plain_body
    return jax.shard_map(
        body,
        mesh=mesh,
        in_specs=(
            P(("row", "col"), None),
            P("row", None),
            P("row", "col"),
            P("row", "col"),
            P("row", "col"),
            P("row", "col"),
            P(None, "col"),
            P(None, "col"),
            P(None, "col"),
            P("col"),
            P(("row", "col"), None),
        ),
        out_specs=(
            P(("row", "col"), None),
            P(("row", "col"), None),
            P("row", "col"),
            P("row", "col"),
            P("row", "col"),
            P("row", "col"),
            P(None, "col"),
            P(None, "col"),
            P(None, "col"),
            P("col"),
        ),
        check_vma=False,
    )
```

```python
import jax
import jax.numpy as jnp
from jax import lax
from jax.experimental import pallas as pl
from jax.experimental.pallas import tpu as pltpu
from jax.sharding import PartitionSpec as P

D = 768
HEADS = 12
HEAD_DIM = 64
SEG = 256
SEGS = 16
TREE_TOKENS = 4096


EPSILON = 1e-12
NEGATIVE = -1e30


def layer_norm(values, scaling, shifting):
    centre = values - jnp.mean(values, axis=-1, keepdims=True)
    spread = jnp.mean(centre * centre, axis=-1, keepdims=True)
    return centre * lax.rsqrt(spread + EPSILON) * scaling + shifting


def exact_gelu(values):
    return jax.nn.gelu(values, approximate=False)


def ancestry(parents):
    segment_count = parents.shape[0]
    labels = jnp.arange(segment_count, dtype=jnp.int32)
    closure = jnp.eye(segment_count, dtype=jnp.float32) + (
        parents[:, None] == labels[None, :]
    ).astype(jnp.float32)
    for repeat in range(segment_count.bit_length()):
        closure = jnp.minimum(jnp.dot(closure, closure, precision=lax.Precision.HIGHEST), 1.0)
    return closure


def allowed(query_pos, key_pos, closure):
    labels = jnp.arange(closure.shape[0], dtype=jnp.int32)
    query_seg = query_pos // SEG
    key_seg = key_pos // SEG
    query_hot = (query_seg[:, None] == labels[None, :]).astype(jnp.float32)
    key_hot = (key_seg[:, None] == labels[None, :]).astype(jnp.float32)
    reach = jnp.dot(
        jnp.dot(query_hot, closure, precision=lax.Precision.HIGHEST),
        key_hot.T,
        precision=lax.Precision.HIGHEST,
    )
    causal = (query_seg[:, None] != key_seg[None, :]) | (key_pos[None, :] <= query_pos[:, None])
    return (reach > 0.5) & causal


def plain_body(
    tokens, parents, w_qkv, w_out, w_up, w_down, ln_gain, ln_bias, proj_bias, ff_bias, cotangent
):
    local_rows = tokens.shape[0]
    score_scale = HEAD_DIM ** (-0.5)
    head_shape = (local_rows, HEADS, HEAD_DIM)
    block_rows = 2 * SEG
    block_count = SEGS // 2
    cols_qkv, cols_out, cols_up, cols_down, norm_gains, shifts, biases, ff_shift = (
        lax.all_gather(w_qkv, "col", axis=1, tiled=True),
        lax.all_gather(w_out, "col", axis=1, tiled=True),
        lax.all_gather(w_up, "col", axis=1, tiled=True),
        lax.all_gather(w_down, "col", axis=1, tiled=True),
        lax.all_gather(ln_gain, "col", axis=1, tiled=True),
        lax.all_gather(ln_bias, "col", axis=1, tiled=True),
        lax.all_gather(proj_bias, "col", axis=1, tiled=True),
        lax.all_gather(ff_bias, "col", axis=0, tiled=True),
    )
    full_qkv, full_out, full_up, full_down = (
        lax.all_gather(cols_qkv, "row", axis=0, tiled=True),
        lax.all_gather(cols_out, "row", axis=0, tiled=True),
        lax.all_gather(cols_up, "row", axis=0, tiled=True),
        lax.all_gather(cols_down, "row", axis=0, tiled=True),
    )
    norm_gains = norm_gains.astype(jnp.float32)
    shifts = shifts.astype(jnp.float32)
    biases = biases.astype(jnp.float32)
    ff_shift = ff_shift.astype(jnp.float32)
    inputs = tokens.astype(jnp.float32)
    normed_low = layer_norm(inputs, norm_gains[0], shifts[0]).astype(jnp.bfloat16)
    projected = jnp.dot(normed_low, full_qkv, preferred_element_type=jnp.float32)
    queries = (projected[:, :D] + biases[0]).astype(jnp.bfloat16).reshape(head_shape)
    keys_own = projected[:, D : 2 * D].astype(jnp.bfloat16).reshape(head_shape)
    values_own = (projected[:, 2 * D :] + biases[1]).astype(jnp.bfloat16).reshape(head_shape)
    keys_all, values_all = (
        lax.all_gather(keys_own, "col", axis=0, tiled=True),
        lax.all_gather(values_own, "col", axis=0, tiled=True),
    )
    key_blocks = keys_all.reshape(block_count, block_rows, HEADS, HEAD_DIM)
    value_blocks = values_all.reshape(block_count, block_rows, HEADS, HEAD_DIM)
    block_starts = jnp.arange(block_count, dtype=jnp.int32) * block_rows
    within = jnp.arange(block_rows, dtype=jnp.int32)
    query_pos = lax.axis_index("col") * local_rows + jnp.arange(local_rows, dtype=jnp.int32)
    closure = ancestry(parents[0])

    def scores_of(query_block, key_block, query_positions, key_positions):
        products = jnp.einsum(
            "qhd,khd->hqk", query_block, key_block, preferred_element_type=jnp.float32
        )
        return (products * score_scale, allowed(query_positions, key_positions, closure)[None])

    def probabilities(query_block, key_block, query_positions, key_positions, log_block):
        scores, visible = scores_of(query_block, key_block, query_positions, key_positions)
        return jnp.where(visible, jnp.exp(scores - log_block[..., None]), 0.0)

    def extent(running, pieces):
        highest_score, mass_total = running
        key_block, first_pos = pieces
        scores, visible = scores_of(queries, key_block, query_pos, first_pos + within)
        masked = jnp.where(visible, scores, NEGATIVE)
        new_highest = jnp.maximum(highest_score, jnp.max(masked, axis=-1))
        exp_terms = jnp.where(visible, jnp.exp(masked - new_highest[..., None]), 0.0)
        new_total = mass_total * jnp.exp(highest_score - new_highest) + jnp.sum(exp_terms, axis=-1)
        return ((new_highest, new_total), None)

    start_state = (
        jnp.full((HEADS, local_rows), NEGATIVE, jnp.float32),
        jnp.zeros((HEADS, local_rows), jnp.float32),
    )
    (highest_score, mass_total), unused = lax.scan(extent, start_state, (key_blocks, block_starts))
    log_total = highest_score + jnp.log(mass_total)

    def attend(running, pieces):
        key_block, value_block, first_pos = pieces
        chances = probabilities(
            queries, key_block, query_pos, first_pos + within, log_total
        ).astype(jnp.bfloat16)
        return (
            running
            + jnp.einsum("hqk,khd->qhd", chances, value_block, preferred_element_type=jnp.float32),
            None,
        )

    attended, unused = lax.scan(
        attend, jnp.zeros(head_shape, jnp.float32), (key_blocks, value_blocks, block_starts)
    )
    attended_low = attended.reshape(local_rows, D).astype(jnp.bfloat16)
    mixed_rows = (
        inputs + jnp.dot(attended_low, full_out, preferred_element_type=jnp.float32) + biases[2]
    )
    second_low = layer_norm(mixed_rows, norm_gains[1], shifts[1]).astype(jnp.bfloat16)
    hidden_pre = jnp.dot(second_low, full_up, preferred_element_type=jnp.float32) + ff_shift
    activated_low = exact_gelu(hidden_pre).astype(jnp.bfloat16)
    output = (
        mixed_rows
        + jnp.dot(activated_low, full_down, preferred_element_type=jnp.float32)
        + biases[3]
    )
    upstream = cotangent.astype(jnp.float32)
    grad_down = jnp.einsum(
        "tf,td->fd", activated_low, cotangent, preferred_element_type=jnp.float32
    )
    grad_act = jnp.einsum("td,fd->tf", cotangent, full_down, preferred_element_type=jnp.float32)
    unused, gelu_back = jax.vjp(exact_gelu, hidden_pre)
    grad_pre = gelu_back(grad_act)[0]
    grad_pre_low = grad_pre.astype(jnp.bfloat16)
    grad_up = jnp.einsum("td,tf->df", second_low, grad_pre_low, preferred_element_type=jnp.float32)
    grad_second = jnp.einsum("tf,df->td", grad_pre_low, full_up, preferred_element_type=jnp.float32)
    unused, second_back = jax.vjp(layer_norm, mixed_rows, norm_gains[1], shifts[1])
    grad_mixed_norm, grad_gain_two, grad_shift_two = second_back(grad_second)
    grad_mixed = upstream + grad_mixed_norm
    grad_mixed_low = grad_mixed.astype(jnp.bfloat16)
    grad_out = jnp.einsum(
        "td,te->de", attended_low, grad_mixed_low, preferred_element_type=jnp.float32
    )
    grad_att_low = (
        jnp.einsum("te,de->td", grad_mixed_low, full_out, preferred_element_type=jnp.float32)
        .astype(jnp.bfloat16)
        .reshape(head_shape)
    )
    deltas = jnp.einsum("qhd,qhd->hq", grad_att_low.astype(jnp.float32), attended)

    def score_grads(
        query_block,
        key_block,
        value_block,
        grad_block,
        query_positions,
        key_positions,
        log_block,
        delta_block,
    ):
        chances = probabilities(query_block, key_block, query_positions, key_positions, log_block)
        grad_chances = jnp.einsum(
            "qhd,khd->hqk", grad_block, value_block, preferred_element_type=jnp.float32
        )
        grad_scores = (chances * (grad_chances - delta_block[..., None]) * score_scale).astype(
            jnp.bfloat16
        )
        return (chances.astype(jnp.bfloat16), grad_scores)

    def backward_block(running, pieces):
        key_block, value_block, first_pos = pieces
        chances_low, grad_scores = score_grads(
            queries,
            key_block,
            value_block,
            grad_att_low,
            query_pos,
            first_pos + within,
            log_total,
            deltas,
        )
        running = running + jnp.einsum(
            "hqk,khd->qhd", grad_scores, key_block, preferred_element_type=jnp.float32
        )
        key_term = jnp.einsum(
            "hqk,qhd->khd", grad_scores, queries, preferred_element_type=jnp.float32
        )
        value_term = jnp.einsum(
            "hqk,qhd->khd", chances_low, grad_att_low, preferred_element_type=jnp.float32
        )
        return (running, (key_term, value_term))

    grad_queries, (key_terms, value_terms) = lax.scan(
        backward_block, jnp.zeros(head_shape, jnp.float32), (key_blocks, value_blocks, block_starts)
    )
    grad_keys, grad_values = (
        lax.psum_scatter(
            key_terms.reshape(TREE_TOKENS, D).astype(jnp.bfloat16),
            "col",
            scatter_dimension=0,
            tiled=True,
        ).astype(jnp.float32),
        lax.psum_scatter(
            value_terms.reshape(TREE_TOKENS, D).astype(jnp.bfloat16),
            "col",
            scatter_dimension=0,
            tiled=True,
        ).astype(jnp.float32),
    )
    grad_queries = grad_queries.reshape(local_rows, D)
    grad_projected_low = jnp.concatenate([grad_queries, grad_keys, grad_values], axis=1).astype(
        jnp.bfloat16
    )
    grad_qkv = jnp.einsum(
        "td,te->de", normed_low, grad_projected_low, preferred_element_type=jnp.float32
    )
    grad_normed = jnp.einsum(
        "te,de->td", grad_projected_low, full_qkv, preferred_element_type=jnp.float32
    )
    unused, first_back = jax.vjp(layer_norm, inputs, norm_gains[0], shifts[0])
    grad_input_norm, grad_gain_one, grad_shift_one = first_back(grad_normed)
    grad_tokens = (grad_mixed + grad_input_norm).astype(jnp.bfloat16)
    gain_terms = jnp.stack([grad_gain_one, grad_gain_two])
    shift_terms = jnp.stack([grad_shift_one, grad_shift_two])
    bias_terms = jnp.stack(
        [
            jnp.sum(grad_queries, axis=0),
            jnp.sum(grad_values, axis=0),
            jnp.sum(grad_mixed, axis=0),
            jnp.sum(upstream, axis=0),
        ]
    )
    ff_terms = jnp.sum(grad_pre, axis=0)
    part_qkv, part_out, part_up, part_down, part_gain, part_shift, part_bias, part_ff = (
        lax.psum_scatter(
            grad_qkv.astype(jnp.bfloat16), "col", scatter_dimension=1, tiled=True
        ).astype(jnp.float32),
        lax.psum_scatter(
            grad_out.astype(jnp.bfloat16), "col", scatter_dimension=1, tiled=True
        ).astype(jnp.float32),
        lax.psum_scatter(
            grad_up.astype(jnp.bfloat16), "col", scatter_dimension=1, tiled=True
        ).astype(jnp.float32),
        lax.psum_scatter(
            grad_down.astype(jnp.bfloat16), "col", scatter_dimension=1, tiled=True
        ).astype(jnp.float32),
        lax.psum_scatter(
            gain_terms.astype(jnp.bfloat16), "col", scatter_dimension=1, tiled=True
        ).astype(jnp.float32),
        lax.psum_scatter(
            shift_terms.astype(jnp.bfloat16), "col", scatter_dimension=1, tiled=True
        ).astype(jnp.float32),
        lax.psum_scatter(
            bias_terms.astype(jnp.bfloat16), "col", scatter_dimension=1, tiled=True
        ).astype(jnp.float32),
        lax.psum_scatter(
            ff_terms.astype(jnp.bfloat16), "col", scatter_dimension=0, tiled=True
        ).astype(jnp.float32),
    )
    grad_w_qkv, grad_w_out, grad_w_up, grad_w_down = (
        lax.psum_scatter(
            part_qkv.astype(jnp.bfloat16), "row", scatter_dimension=0, tiled=True
        ).astype(jnp.float32),
        lax.psum_scatter(
            part_out.astype(jnp.bfloat16), "row", scatter_dimension=0, tiled=True
        ).astype(jnp.float32),
        lax.psum_scatter(
            part_up.astype(jnp.bfloat16), "row", scatter_dimension=0, tiled=True
        ).astype(jnp.float32),
        lax.psum_scatter(
            part_down.astype(jnp.bfloat16), "row", scatter_dimension=0, tiled=True
        ).astype(jnp.float32),
    )
    grad_gain, grad_shift, grad_bias, grad_ff = lax.psum(
        (part_gain, part_shift, part_bias, part_ff), "row"
    )
    return (
        output.astype(jnp.bfloat16),
        grad_tokens,
        grad_w_qkv,
        grad_w_out,
        grad_w_up,
        grad_w_down,
        grad_gain,
        grad_shift,
        grad_bias,
        grad_ff,
    )


F32=jnp.float32; BF=jnp.bfloat16
NEG=NEGATIVE
NT=(((1,),(1,)),((),()))
NN=(((1,),(0,)),((),()))


def dg(a, b, dims):
    return lax.dot_general(a, b, dims, preferred_element_type=F32)


def chunk_rows(c, i):
    start = c * SEG if c < 4 else (4 + (c - 4) * 2 + i) * SEG
    return slice(start, start + SEG)


def pair_dot(c, keys_ref, rows):
    if c < 4:
        return dg(keys_ref[chunk_rows(c, 0), :], rows, NT)
    return jnp.concatenate(
        [
            dg(keys_ref[chunk_rows(c, i), :], rows[i * SEG : (i + 1) * SEG, :], NT)
            for i in range(2)
        ],
        axis=1,
    )


def score_chunk(c, k_ref, qh):
    scores = pair_dot(c, k_ref, qh)
    if c < 5:
        return scores
    key = lax.broadcasted_iota(jnp.int32, scores.shape, 0)
    query = lax.broadcasted_iota(jnp.int32, scores.shape, 1)
    return jnp.where(key <= (query & (SEG - 1)), scores, NEG)


def chunk_bias(c, meta):
    second = lax.broadcasted_iota(jnp.int32, (1, 2 * SEG), 1) // SEG
    if c < 4:
        return jnp.where((c ^ meta[1]) < meta[0] + second, 0.0, NEG)
    if c == 4:
        return jnp.where(jnp.where(second > 0, meta[3], meta[2]) > 0, 0.0, NEG)
    return jnp.zeros((1, 2 * SEG), F32)


def halves_of(value):
    lane = lax.broadcasted_iota(jnp.int32, value.shape, 1)
    zero = jnp.zeros((), value.dtype)
    return [jnp.where((lane < 64) == (h == 0), value, zero) for h in range(2)]


def fwd_kernel(meta, q_ref, k_ref, v_ref, o_ref, inverse_ref, p_ref):
    turned = v_ref[...].T
    biases = [chunk_bias(c, meta) for c in range(6)]
    results, inverses = [], []
    for h, qh in enumerate(halves_of(q_ref[...] * jnp.asarray(0.125, BF))):
        scores = [score_chunk(c, k_ref, qh) for c in range(6)]
        top = jnp.full((1, 2 * SEG), NEG, F32)
        for s, bias in zip(scores, biases):
            top = jnp.maximum(top, jnp.max(s, axis=0, keepdims=True) + bias)
        mass = jnp.zeros((1, 2 * SEG), F32)
        shared = jnp.zeros((128, 2 * SEG), F32)
        own = [jnp.zeros((128, SEG), F32)] * 2
        for c, s in enumerate(scores):
            p = jnp.exp(s - (top - biases[c]))
            mass = mass + jnp.sum(p, axis=0, keepdims=True)
            low = p.astype(BF)
            p_ref[0, (6 * h + c) * SEG : (6 * h + c + 1) * SEG, :] = low
            if c < 4:
                shared = shared + dg(turned[:, chunk_rows(c, 0)], low, NN)
            else:
                own = [
                    own[i] + dg(turned[:, chunk_rows(c, i)], low[:, i * SEG : (i + 1) * SEG], NN)
                    for i in range(2)
                ]
        inverse = jnp.broadcast_to(1.0 / mass, shared.shape)
        inverses.append(inverse)
        results.append((shared + jnp.concatenate(own, axis=1)) * inverse)
    row = lax.broadcasted_iota(jnp.int32, results[0].shape, 0)
    o_ref[...] = jnp.where(row < 64, results[0], results[1]).T.astype(BF)
    inverse_ref[...] = jnp.where(row < 64, inverses[0], inverses[1]).T


def bwd_kernel(q_ref, k_ref, v_ref, do_ref, o_ref, inverse_ref, p_ref, dq_ref, dk_ref, dv_ref):
    do = (do_ref[...].astype(F32) * inverse_ref[...]).astype(BF)
    products = (do.astype(F32) * o_ref[...].astype(F32)).T
    turned = k_ref[...].T
    qh = halves_of(q_ref[...] * jnp.asarray(0.125, BF))
    doh = halves_of(do)
    delta = [jnp.sum(products[h * 64 : (h + 1) * 64], axis=0, keepdims=True) for h in range(2)]
    shared = [jnp.zeros((128, 2 * SEG), F32)] * 2
    own = [[jnp.zeros((128, SEG), F32)] * 2] * 2
    for c in range(6):
        chances, slopes = [], []
        for h in range(2):
            p = p_ref[0, (6 * h + c) * SEG : (6 * h + c + 1) * SEG, :]
            ds = p.astype(F32) * (pair_dot(c, v_ref, doh[h]) - delta[h])
            chances.append(p)
            slopes.append(ds.astype(BF))
        for i in range(1 if c < 4 else 2):
            r = chunk_rows(c, i)
            cut = slice(0, 2 * SEG) if c < 4 else slice(i * SEG, (i + 1) * SEG)
            for ref, left, right in ((dv_ref, chances, doh), (dk_ref, slopes, qh)):
                ref[r, :] = dg(
                    jnp.concatenate([x[:, cut] for x in left], axis=1),
                    jnp.concatenate([x[cut] for x in right], axis=0),
                    NN,
                ).astype(BF)
        if c < 4:
            shared = [shared[h] + dg(turned[:, chunk_rows(c, 0)], slopes[h], NN) for h in range(2)]
        else:
            own = [
                [
                    own[h][i]
                    + dg(turned[:, chunk_rows(c, i)], slopes[h][:, i * SEG : (i + 1) * SEG], NN)
                    for i in range(2)
                ]
                for h in range(2)
            ]
    total_q = [shared[h] + jnp.concatenate(own[h], axis=1) for h in range(2)]
    row = lax.broadcasted_iota(jnp.int32, total_q[0].shape, 0)
    dq_ref[...] = (jnp.where(row < 64, total_q[0], total_q[1]).T * 0.125).astype(BF)


def attn_specs(rows, keys):
    return (
        pl.BlockSpec((rows, 128), lambda j, *unused: (0, j)),
        pl.BlockSpec((keys, 128), lambda j, *unused: (0, j)),
        pl.BlockSpec((1, 12 * SEG, rows), lambda j, *unused: (j, 0, 0)),
    )


def attn_fwd(meta, q, k, v):
    rows, width = q.shape
    pairs = width // 128
    q_spec, k_spec, p_spec = attn_specs(rows, k.shape[0])
    return call(
        fwd_kernel,
        "attn_fwd",
        (pairs,),
        [q_spec, k_spec, k_spec],
        [
            (q_spec, (q.shape, BF)),
            (q_spec, (q.shape, F32)),
            (p_spec, ((pairs, 12 * SEG, rows), BF)),
        ],
        prefetch=1,
        flops=2 * 2 * 12 * 12 * SEG**3,
        size=32 << 20,
        args=(meta, q, k, v),
    )


def attn_bwd(q, k, v, do, o, inverse, p):
    rows, width = q.shape
    pairs = width // 128
    q_spec, k_spec, p_spec = attn_specs(rows, k.shape[0])
    return call(
        bwd_kernel,
        "attn_bwd",
        (pairs,),
        [q_spec, k_spec, k_spec, q_spec, q_spec, q_spec, p_spec],
        [(q_spec, (q.shape, BF)), (k_spec, (k.shape, BF)), (k_spec, (k.shape, BF))],
        flops=4 * 2 * 12 * 12 * SEG**3,
        size=40 << 20,
        args=(q, k, v, do, o, inverse, p),
    )


def row_norm(values):
    centre = values - jnp.mean(values, axis=-1, keepdims=True)
    spread = jnp.mean(centre * centre, axis=-1, keepdims=True)
    scale = lax.rsqrt(spread + EPSILON)
    return centre * scale, scale


def row_norm_back(unit, scale, scaled):
    mean_one = jnp.mean(scaled, axis=-1, keepdims=True)
    mean_two = jnp.mean(scaled * unit, axis=-1, keepdims=True)
    return scale * (scaled - mean_one - unit * mean_two)


def call(kernel, name, grid, ins, outs, scratch=(), prefetch=0, flops=0, size=16 << 20, aliases=None, room=58, args=()):
    grid_spec = pltpu.PrefetchScalarGridSpec(
        num_scalar_prefetch=prefetch,
        grid=grid,
        in_specs=ins,
        out_specs=[spec for spec, unused in outs],
        scratch_shapes=list(scratch),
    )
    return pl.pallas_call(
        kernel,
        grid_spec=grid_spec,
        out_shape=[jax.ShapeDtypeStruct(*shape) for unused, shape in outs],
        cost_estimate=pl.CostEstimate(flops=flops, bytes_accessed=size, transcendentals=0),
        input_output_aliases=aliases or {},
        compiler_params=pltpu.CompilerParams(vmem_limit_bytes=room << 20),
        name=name,
    )(*args)


def whole(shape):
    return pl.BlockSpec(shape, lambda *unused: (0,) * len(shape))


def join_kernel(pieces_ref, qkv_ref, out_ref):
    cols = pieces_ref.shape[1]
    cut = qkv_ref.shape[1] // cols
    qkv_ref[...] = jnp.concatenate([pieces_ref[0, c, :, :cut] for c in range(cols)], axis=1)
    out_ref[...] = jnp.concatenate([pieces_ref[0, c, :, cut:] for c in range(cols)], axis=1)


def join_pieces(pieces, height):
    rows, cols, unused, width = pieces.shape
    full = rows * height
    return call(
        join_kernel,
        "join_pieces",
        (rows,),
        [pl.BlockSpec((1, cols, height, width), lambda r: (r, 0, 1, 0))],
        [
            (pl.BlockSpec((height, 3 * full), lambda r: (r, 0)), ((full, 3 * full), BF)),
            (pl.BlockSpec((height, full), lambda r: (r, 0)), ((full, full), BF)),
        ],
        args=(pieces,),
    )


def turn_kernel(value_ref, turned_ref, sum_ref):
    turned_ref[...] = value_ref[...].T
    sum_ref[...] = jnp.sum(value_ref[...].astype(F32), axis=0, keepdims=True)


def turn(value):
    rows, width = value.shape
    return call(
        turn_kernel,
        "turn",
        (1,),
        [whole(value.shape)],
        [
            (whole((width, rows)), ((width, rows), BF)),
            (whole((1, width)), ((1, width), F32)),
        ],
        args=(value,),
    )


def select_source(step, sources, kept):
    for i, ref in enumerate(sources):

        @pl.when(step == i)
        def _(ref=ref):
            kept[...] = ref[...]

    return row_norm(kept[...].astype(F32))[0]


def project_rows(step, sources, small_ref, weight_ref, k_ref, v_ref, n_ref, kept):
    width = weight_ref.shape[0]
    unit = select_source(step, sources, kept)
    normed = (unit * small_ref[0:1] + small_ref[2:3]).astype(BF)
    n_ref[...] = normed
    k_ref[...] = dg(normed, weight_ref[:, width : 2 * width], NN).astype(BF)
    v_ref[...] = (dg(normed, weight_ref[:, 2 * width :], NN) + small_ref[5:6]).astype(BF)
    return normed


def project_kernel(a_ref, b_ref, c_ref, small_ref, weight_ref, q_ref, k_ref, v_ref, n_ref, kept):
    step = pl.program_id(0)
    width = a_ref.shape[1]
    sources = (a_ref, b_ref, c_ref)
    normed = project_rows(step, sources, small_ref, weight_ref, k_ref, v_ref, n_ref, kept)

    @pl.when(step == pl.num_programs(0) - 1)
    def _():
        q_ref[...] = (dg(normed, weight_ref[:, :width], NN) + small_ref[4:5]).astype(BF)


def project(sources, small, qkv):
    tokens, width = sources[0].shape
    block = pl.BlockSpec((tokens, width), lambda i: (i + i // 2, 0))
    tall = ((4 * tokens, width), BF)
    return call(
        project_kernel,
        "project",
        (3,),
        [whole((tokens, width))] * 3 + [whole(small.shape), whole(qkv.shape)],
        [(whole((tokens, width)), ((tokens, width), BF)), (block, tall), (block, tall), (block, tall)],
        scratch=[pltpu.VMEM((tokens, width), BF)],
        flops=2 * 7 * tokens * width * width,
        args=(*sources, small, qkv),
    )


def project_parents_kernel(
    a_ref, small_ref, weight_ref, old_k, old_v, old_n, k_ref, v_ref, n_ref, kept
):
    project_rows(0, (a_ref,), small_ref, weight_ref, k_ref, v_ref, n_ref, kept)


def project_parents(source, small, qkv, *others):
    tokens, width = source.shape
    block = pl.BlockSpec((tokens, width), lambda i: (2, 0))
    tall = ((4 * tokens, width), BF)
    anywhere = pl.BlockSpec(memory_space=pl.ANY)
    return call(
        project_parents_kernel,
        "project_parents",
        (1,),
        [whole((tokens, width)), whole(small.shape), whole(qkv.shape)] + [anywhere] * 3,
        [(block, tall)] * 3,
        scratch=[pltpu.VMEM((tokens, width), BF)],
        flops=2 * 2 * tokens * width * width,
        aliases={3: 0, 4: 1, 5: 2},
        args=(source, small, qkv, *others),
    )


def unproject_kernel(
    a_ref, b_ref, c_ref, dk_ref, dv_ref, k_ref, v_ref, part_ref, terms_ref, kept
):
    step = pl.program_id(0)

    @pl.when(step == 0)
    def _():
        terms_ref[...] = jnp.zeros_like(terms_ref)

    dk, dv = dk_ref[...], dv_ref[...]
    grad = dg(dk, k_ref[...], NT) + dg(dv, v_ref[...], NT)
    part_ref[...] = grad.astype(BF)
    unit = select_source(step, (a_ref, b_ref, c_ref), kept)
    terms_ref[0:1] += jnp.sum(grad * unit, axis=0, keepdims=True)
    terms_ref[1:2] += jnp.sum(grad, axis=0, keepdims=True)
    terms_ref[2:3] += jnp.sum(dv.astype(F32), axis=0, keepdims=True)


def unproject(sources, dk, dv, qkv):
    tokens, width = sources[0].shape
    count = len(sources)
    block = pl.BlockSpec((tokens, width), lambda i: (i, 0))
    return call(
        unproject_kernel,
        "unproject",
        (count,),
        [whole((tokens, width))] * count
        + [block, block]
        + [pl.BlockSpec((width, width), lambda i, n=n: (0, n)) for n in (1, 2)],
        [(block, ((count * tokens, width), BF)), (whole((8, width)), ((8, width), F32))],
        scratch=[pltpu.VMEM((tokens, width), BF)],
        flops=2 * 2 * count * tokens * width * width,
        args=(*sources, dk, dv, qkv, qkv),
    )


def weigh_kernel(
    me, dq_ref, dk_ref, dv_ref, n_ref, tokens_ref, grad_out_ref, weight_ref,
    own_ref, other_ref, grad_ref, terms_ref, kept, turned,
):
    step = pl.program_id(0)
    tokens, width = dq_ref.shape

    @pl.when(step == 0)
    def _():
        dq, dk, dv = dq_ref[...], dk_ref[-tokens:], dv_ref[-tokens:]
        grad = (
            dg(dq, weight_ref[:, :width], NT)
            + dg(dk, weight_ref[:, width : 2 * width], NT)
            + dg(dv, weight_ref[:, 2 * width :], NT)
        )
        grad_ref[...] = grad
        unit, unused = row_norm(tokens_ref[...].astype(F32))
        terms_ref[...] = jnp.zeros_like(terms_ref)
        terms_ref[0:1] = jnp.sum(grad * unit, axis=0, keepdims=True)
        terms_ref[1:2] = jnp.sum(grad, axis=0, keepdims=True)
        terms_ref[2:3] = jnp.sum(dv.astype(F32), axis=0, keepdims=True)
        terms_ref[3:4] = jnp.sum(dq.astype(F32), axis=0, keepdims=True)
        turned[...] = n_ref[...].T
        kept[:, :width] = dg(turned[:, -tokens:], dq, NN).astype(BF)

    @pl.when(step == 1)
    def _():
        kept[:, width : 2 * width] = dg(turned[...], dk_ref[...], NN).astype(BF)

    @pl.when(step == 2)
    def _():
        kept[:, 2 * width :] = dg(turned[...], dv_ref[...], NN).astype(BF)
        height = own_ref.shape[1]
        cols = own_ref.shape[0] // 2
        tall, low_part = 3 * width // cols, width // cols
        for c in range(cols):
            parts = [
                jnp.concatenate(
                    [
                        kept[r * height : (r + 1) * height, c * tall : (c + 1) * tall],
                        grad_out_ref[r * height : (r + 1) * height, c * low_part : (c + 1) * low_part],
                    ],
                    axis=1,
                )
                for r in range(4)
            ]
            a, c_part = in_order(me[1], parts[0], parts[2])
            b, d_part = in_order(me[1], parts[1], parts[3])
            for y_step, pair in ((0, (a, b)), (1, (c_part, d_part))):
                mine, theirs = in_order(me[2], *pair)
                own_ref[place_of(c, y_step, me[2], me)] = mine
                other_ref[place_of(c, y_step, me[2] ^ 1, me)] = theirs


def weigh(me, dq, dk, dv, normed, tokens, grad_out, qkv, cols):
    count, width = dq.shape
    shape = (2 * cols, width // 4, 4 * width // cols)
    return call(
        weigh_kernel,
        "weigh",
        (3,),
        [whole(x.shape) for x in (dq, dk, dv, normed, tokens, grad_out, qkv)],
        [
            (whole(shape), (shape, BF)),
            (whole(shape), (shape, BF)),
            (whole((count, width)), ((count, width), F32)),
            (whole((8, width)), ((8, width), F32)),
        ],
        scratch=[pltpu.VMEM((width, 3 * width), BF), pltpu.VMEM((width, normed.shape[0]), BF)],
        prefetch=1,
        flops=2 * 12 * count * width * width,
        args=(me, dq, dk, dv, normed, tokens, grad_out, qkv),
    )


def finish_kernel(
    meta, trunk_ref, near_ref, far_ref, own_ref, mixed_ref, tokens_ref, small_ref, out_ref
):
    slot = meta[1 + pl.program_id(0)]
    place = pl.ds(pl.multiple_of((jnp.maximum(slot, 0) & 1) * SEG, SEG), SEG)
    branch = jnp.where(slot >= 2, far_ref[place, :], near_ref[place, :]).astype(F32)
    branch = jnp.where(slot >= 0, branch, 0.0)
    trunk = trunk_ref[...].astype(F32)
    grad = own_ref[...] + jnp.where(meta[0] == 0, trunk, branch)
    unit, scale = row_norm(tokens_ref[...].astype(F32))
    back = row_norm_back(unit, scale, grad * small_ref[0:1])
    out_ref[...] = (mixed_ref[...] + back).astype(BF)


def finish(meta, trunk, near, far, own, mixed, tokens, small):
    width = tokens.shape[1]
    part = pl.BlockSpec((SEG, width), lambda i, meta: (i, 0))
    full = whole(near.shape)
    return call(
        finish_kernel,
        "finish",
        (2,),
        [part, full, full, part, part, part, whole(small.shape)],
        [(part, (tokens.shape, BF))],
        prefetch=1,
        room=24,
        args=(meta, trunk, near, far, own, mixed, tokens, small),
    )[0]


def gelu_parts(v):
    x = v * 0.7071067811865476
    chance = 0.5 + 0.5 * lax.erf(x)
    density = jnp.exp(-x * x) * 0.3989422804014327
    return chance, v * density


def feed_kernel(
    tokens_ref, attended_ref, out_ref, small_ref, upstream_ref, upstream_t, summed_ref, up_ref, down_ref,
    shift_ref,
    output_ref, grad_mixed_ref, grad_att_ref, grad_out_ref, sums_ref, terms_ref, grads_ref,
    second_ref, second_t, mixed_ref, sum_ref, back_ref,
    up_slot, down_slot, up_sem, down_sem,
):
    step = pl.program_id(0)
    last = pl.num_programs(0) - 1
    slot = step % 2
    height, width = up_ref.shape[2], up_ref.shape[3]

    @pl.when(step == 0)
    def _():
        mixed = (
            tokens_ref[...].astype(F32) + dg(attended_ref[...], out_ref[...], NN)
        ) + small_ref[6:7]
        mixed_ref[...] = mixed
        unit, unused = row_norm(mixed)
        second_ref[...] = (unit * small_ref[1:2] + small_ref[3:4]).astype(BF)
        second_t[...] = second_ref[...].T
        sum_ref[...] = jnp.zeros_like(sum_ref)
        back_ref[...] = jnp.zeros_like(back_ref)

    def up_copy(which, at):
        return pltpu.make_async_copy(
            up_slot.at[which],
            grads_ref.at[:, pl.ds(2 * at, 2), pl.ds(0, height), :],
            up_sem.at[which],
        )

    def down_copy(which, at):
        return pltpu.make_async_copy(
            down_slot.at[which],
            grads_ref.at[at, :, pl.ds(height, height), :],
            down_sem.at[which],
        )

    @pl.when(step >= 2)
    def _():
        up_copy(slot, step - 2).wait()
        down_copy(slot, step - 2).wait()

    full = up_ref.shape[0] * height
    up = jnp.concatenate([up_ref[:, i].reshape(full, width) for i in range(2)], axis=1)
    half = height // 2
    down = jnp.concatenate(
        [down_ref[0, :, i * half : (i + 1) * half, :].reshape(full, width) for i in range(2)],
        axis=1,
    )
    second, upstream = second_ref[...], upstream_ref[...]
    hidden = jnp.dot(second, up, preferred_element_type=F32) + shift_ref[...]
    grad_act = jnp.dot(upstream, down, preferred_element_type=F32)
    chance, slope = gelu_parts(hidden)
    active = (hidden * chance).astype(BF)
    grad_pre = grad_act * (chance + slope)
    grad_low = grad_pre.astype(BF)
    terms_ref[...] = jnp.sum(grad_pre, axis=0, keepdims=True)
    sum_ref[...] += dg(active, down, NT)
    back_ref[...] += dg(grad_low, up, NT)
    grad_up = jnp.dot(second_t[...], grad_low, preferred_element_type=F32).astype(BF)
    grad_down = jnp.dot(upstream_t[...], active, preferred_element_type=F32).astype(BF)
    for i in range(2):
        cut = slice(i * width, (i + 1) * width)
        up_slot[slot, :, i] = grad_up[:, cut].reshape(up_ref.shape[0], height, width)
        down_slot[slot, :, i * half : (i + 1) * half, :] = grad_down[:, cut].reshape(
            down_ref.shape[1], half, width
        )
    up_copy(slot, step).start()
    down_copy(slot, step).start()

    @pl.when(step == last)
    def _():
        up_copy(1 - slot, step - 1).wait()
        down_copy(1 - slot, step - 1).wait()
        mixed = mixed_ref[...]
        unit, scale = row_norm(mixed)
        output_ref[...] = (mixed + sum_ref[...] + small_ref[7:8]).astype(BF)
        grad_second = back_ref[...]
        upstream_f = upstream_ref[...].astype(F32)
        grad_mixed = upstream_f + row_norm_back(unit, scale, grad_second * small_ref[1:2])
        grad_mixed_ref[...] = grad_mixed
        mixed_low = grad_mixed.astype(BF)
        grad_att_ref[...] = dg(mixed_low, out_ref[...], NT).astype(BF)
        grad_out_ref[...] = jnp.dot(
            attended_ref[...].T, mixed_low, preferred_element_type=F32
        ).astype(BF)
        sums_ref[...] = jnp.zeros_like(sums_ref)
        sums_ref[0:1] = jnp.sum(grad_second * unit, axis=0, keepdims=True)
        sums_ref[1:2] = jnp.sum(grad_second, axis=0, keepdims=True)
        sums_ref[2:3] = jnp.sum(grad_mixed, axis=0, keepdims=True)
        sums_ref[3:4] = summed_ref[...]
        up_copy(slot, step).wait()
        down_copy(slot, step).wait()


def feed_forward(
    tokens_in, attended, w_out, small, upstream, turned, summed, up_weights, down_weights, shift
):
    tokens, width = tokens_in.shape
    rows, cols, half, wide = down_weights.shape
    block = whole((tokens, width))
    grid_spec = pltpu.PrefetchScalarGridSpec(
        num_scalar_prefetch=0,
        grid=(rows,),
        in_specs=[
            block,
            block,
            whole((width, width)),
            whole(small.shape),
            block,
            whole(turned.shape),
            whole(summed.shape),
            pl.BlockSpec((rows, 2, half, wide), lambda r: (0, r, 0, 0)),
            pl.BlockSpec((1, cols, half, wide), lambda r: (r, 0, 0, 0)),
            pl.BlockSpec((1, 2 * wide), lambda r: (0, r)),
        ],
        out_specs=[
            block,
            block,
            block,
            whole((width, width)),
            whole((8, width)),
            pl.BlockSpec((1, 2 * wide), lambda r: (0, r)),
            pl.BlockSpec(memory_space=pl.ANY),
        ],
        scratch_shapes=[
            pltpu.VMEM((tokens, width), BF),
            pltpu.VMEM((width, tokens), BF),
            pltpu.VMEM((tokens, width), F32),
            pltpu.VMEM((tokens, width), F32),
            pltpu.VMEM((tokens, width), F32),
            pltpu.VMEM((2, rows, 2, half, wide), BF),
            pltpu.VMEM((2, cols, half, wide), BF),
            pltpu.SemaphoreType.DMA((2,)),
            pltpu.SemaphoreType.DMA((2,)),
        ],
    )
    return pl.pallas_call(
        feed_kernel,
        grid_spec=grid_spec,
        out_shape=[
            jax.ShapeDtypeStruct((tokens, width), BF),
            jax.ShapeDtypeStruct((tokens, width), F32),
            jax.ShapeDtypeStruct((tokens, width), BF),
            jax.ShapeDtypeStruct((width, width), BF),
            jax.ShapeDtypeStruct((8, width), F32),
            jax.ShapeDtypeStruct((1, cols * wide), F32),
            jax.ShapeDtypeStruct((rows, cols, 2 * half, wide), BF),
        ],
        cost_estimate=pl.CostEstimate(
            flops=12 * tokens * width * cols * wide,
            bytes_accessed=24 << 20,
            transcendentals=2 * tokens * cols * wide,
        ),
        compiler_params=pltpu.CompilerParams(vmem_limit_bytes=60 << 20),
        name="feed_forward",
    )(tokens_in, attended, w_out, small, upstream, turned, summed, up_weights, down_weights, shift)


def swap(value, axis, bit):
    size = lax.axis_size(axis)
    return lax.ppermute(value, axis, [(i, i ^ bit) for i in range(size)])


def exchange(value, first):
    rows, cols = lax.axis_size("row"), lax.axis_size("col")
    pairs = []
    for r in range(rows):
        for c in range(cols):
            along_x = (r & 1 == 0) == first
            other = (r, c ^ 1) if along_x else (r ^ 2, c)
            pairs.append((r * cols + c, other[0] * cols + other[1]))
    return lax.ppermute(value, ("row", "col"), pairs)


def add_low(a, b):
    return (a.astype(jnp.float32) + b.astype(jnp.float32)).astype(jnp.bfloat16)


def place_of(col_index, y_step, of_core, me):
    d = col_index ^ me[0]
    x_step = d & 1
    near = jnp.where(of_core == 0, x_step, y_step)
    far = jnp.where(of_core == 0, y_step, x_step)
    return (d >> 1) | (near << 2) | (far << 3)


def in_order(flag, first, second):
    return jnp.where(flag > 0, second, first), jnp.where(flag > 0, first, second)


def halves(value, flags):
    return [
        jnp.where(flags[i] > 0, value[i * SEG : (i + 1) * SEG], jnp.zeros((), value.dtype))
        for i in range(2)
    ]


def placed(value, targets, numbers):
    out = []
    for number in numbers:
        parts = halves(value, [(targets[i] == number).astype(jnp.int32) for i in range(2)])
        out.append(parts[0] + parts[1])
    return jnp.concatenate(out, axis=0)


def level_move(value, pairs):
    cols = lax.axis_size("col")
    x_size = 2
    full = [
        (a * x_size + x, b * x_size + x)
        for a, b in pairs
        for x in range(x_size)
        if max(a, b) * x_size < cols
    ]
    return lax.ppermute(value, "col", full)


def together(*values):
    return lax.optimization_barrier(values)


def share_tokens(tokens, cotangent, own_slot, level):
    branch = placed(tokens, own_slot, (0, 1))
    branch_in = swap(placed(tokens, own_slot, (2, 3)), "col", 1)
    hop = level_move(tokens, [(0, 2)])
    branch_in, hop, cotangent = together(branch_in, hop, cotangent)
    turned, summed = turn(cotangent)
    branch_in, hop, turned = together(branch_in, hop, turned)
    branch = branch + branch_in
    moved = level_move(
        jnp.where(level == 1, branch, jnp.where(level == 0, tokens, hop)), [(0, 1), (1, 2), (2, 3)]
    )
    down = level_move(branch, [(3, 2)])
    trunk = jnp.where(level == 0, tokens, jnp.where(level == 2, hop, moved))
    branch_up = branch + jnp.where(level == 2, moved, jnp.zeros((), moved.dtype))
    up_two = level_move(branch_up, [(2, 3)])
    down_two = level_move(branch + down, [(2, 1)])
    trunk_far = swap(trunk, "col", 1)
    up_two, down_two, trunk_far = together(up_two, down_two, trunk_far)
    branch = (branch_up + down) + (up_two + down_two)
    return trunk, trunk_far, branch, turned, summed


def total(*parts):
    out = parts[0].astype(jnp.float32)
    for value in parts[1:]:
        out = out + value.astype(jnp.float32)
    return out


def tail_rounds(part, parent_slot, level, make_pieces, vectors_of):
    parent_part = part[4 * SEG :]
    keep, send = (placed(parent_part, parent_slot, pair) for pair in ((0, 1), (2, 3)))
    trunk, trunk_send, send = together(part[: 2 * SEG], part[2 * SEG : 4 * SEG], send)
    branch_in = swap(send, "col", 1)
    own, other, extra = make_pieces(trunk)
    terms = vectors_of(extra)

    branch = add_low(keep, branch_in)
    branch, trunk_send, other, terms = together(branch, trunk_send, other, terms)
    moves = (
        level_move(branch, [(1, 2)]),
        level_move(branch, [(3, 2)]),
        swap(trunk_send, "col", 1),
        swap(other, "row", 1),
        swap(terms, "row", 1),
    )
    up, down, trunk_in, own_in, terms_in = together(*moves)

    branch_up, branch_down = add_low(branch, up), add_low(branch, down)
    trunk = add_low(trunk, trunk_in)
    half = own.shape[0] // 2
    held = add_low(own[:half], own_in[:half])
    leaving = add_low(own[half:], own_in[half:])
    terms = terms + terms_in
    branch_up, branch_down, trunk, leaving, terms = together(
        branch_up, branch_down, trunk, leaving, terms
    )
    moves = (
        level_move(branch_up, [(2, 3)]),
        level_move(branch_down, [(2, 1)]),
        level_move(trunk, [(1, 0), (3, 2)]),
        exchange(leaving, False),
        swap(terms, "row", 2),
    )
    up_two, down_two, trunk_in, held_in, terms_in = together(*moves)

    branch = (
        branch_up.astype(jnp.float32)
        + down.astype(jnp.float32)
        + up_two.astype(jnp.float32)
        + down_two.astype(jnp.float32)
    ).astype(jnp.bfloat16)
    trunk = add_low(trunk, trunk_in)
    half = half // 2
    leaving = add_low(held[half:], held_in[half:])
    held = add_low(held[:half], held_in[:half])
    terms = terms + terms_in
    branch, trunk, leaving, terms = together(branch, trunk, leaving, terms)
    moves = (
        level_move(trunk, [(2, 0)]),
        swap(branch, "col", 1),
        exchange(leaving, True),
        swap(terms, "col", 1),
    )
    trunk_in, branch_far, held_in, terms_in = together(*moves)

    trunk = add_low(trunk, trunk_in)
    terms = terms + terms_in
    leaving = [add_low(held[k], held_in[k]) for k in range(1, 4)]
    kept = held[0].astype(jnp.float32) + held_in[0].astype(jnp.float32)
    *leaving, terms = together(*leaving, terms)
    moves = [swap(leaving[k - 1], "col", 2 * k) for k in range(1, 4)]
    terms_in = swap(terms, "col", 4)
    for moved in moves:
        kept = kept + moved.astype(jnp.float32)
    terms = terms + terms_in
    terms = terms + swap(terms, "col", 2)
    return trunk, branch, branch_far, kept, terms, extra


def tree_body(
    tokens, parents, w_qkv, w_out, w_up, w_down, ln_gain, ln_bias, proj_bias, ff_bias, cotangent
):
    row, col = lax.axis_index("row"), lax.axis_index("col")
    rows, cols = lax.axis_size("row"), lax.axis_size("col")
    local_rows = tokens.shape[0]
    side, level = col & 1, col >> 1
    me = jnp.stack([col, row >> 1, row & 1]).astype(jnp.int32)

    parent = parents[0]
    numbers = jnp.arange(SEGS, dtype=jnp.int32)
    is_branch = ((numbers >= 4) & (parent == 3)).astype(jnp.int32)

    def pick(array, number):
        return jnp.sum(jnp.where(numbers == number, array, 0))

    def slot(number):
        return jnp.sum(jnp.where(numbers < number, is_branch, 0)) ^ (2 * side)

    own = [2 * col + i for i in range(2)]
    own_parent = [pick(parent, number) for number in own]
    is_leaf = [number >= 4 for number in own_parent]
    own_slot = [jnp.where(pick(is_branch, number) > 0, slot(number), -1) for number in own]
    parent_slot = [jnp.where(is_leaf[i], slot(own_parent[i]), -1) for i in range(2)]
    meta = jnp.stack([2 * col, 2 * side] + [leaf.astype(jnp.int32) for leaf in is_leaf])

    narrow, wide = w_up.shape
    with jax.named_scope("gather_early_weights"):
        vectors = jnp.concatenate(
            [ln_gain, ln_bias, proj_bias, ff_bias.reshape(-1, ln_gain.shape[1])], axis=0
        ).reshape(-1, wide)
        count = vectors.shape[0]
        early = jnp.concatenate(
            [
                w_up,
                jnp.concatenate([w_qkv, w_out], axis=1),
                vectors,
                jnp.zeros((16 - count, wide), vectors.dtype),
            ],
            axis=0,
        )
        early = lax.all_gather(early, ("row", "col"), axis=0, tiled=False)
        early = early.reshape(rows, cols, *early.shape[1:])
        vectors = early[0, :, 2 * narrow : 2 * narrow + count]
        vectors = vectors.reshape(cols, -1, ln_gain.shape[1])
        small = vectors[:, :8].transpose(1, 0, 2).reshape(8, D).astype(jnp.float32)
        ff_shift = vectors[:, 8:].reshape(1, -1).astype(jnp.float32)
        full_qkv, full_out = join_pieces(early, narrow)
    with jax.named_scope("gather_tokens"):
        trunk, trunk_far, branch, turned, summed = share_tokens(
            tokens, cotangent, own_slot, level
        )
        branch_far = swap(branch, "col", 1)
    with jax.named_scope("gather_late_weights"):
        late = jnp.concatenate([w_down.T[:, :wide], w_down.T[:, wide:]], axis=0)
        late = lax.all_gather(late, ("row", "col"), axis=0, tiled=False)
        late = late.reshape(rows, cols, *late.shape[1:])

    queries, *rows_of = project((trunk, trunk_far, tokens), small, full_qkv)
    branch_far, queries = together(branch_far, queries)
    branch = jnp.concatenate([branch, branch_far], axis=0)
    parent_tokens = jnp.concatenate(
        [
            lax.dynamic_slice_in_dim(branch, jnp.maximum(parent_slot[i], 0) * SEG, SEG, 0)
            for i in range(2)
        ],
        axis=0,
    )
    key_rows, value_rows, normed = project_parents(parent_tokens, small, full_qkv, *rows_of)
    sources = (trunk, trunk_far, parent_tokens)
    attended, inverse, chances = attn_fwd(meta, queries, key_rows, value_rows)
    output, grad_mixed, grad_att, grad_out, sums, ff_terms, late_grads = feed_forward(
        tokens, attended, full_out, small, cotangent, turned, summed, early, late, ff_shift
    )
    grad_q, grad_k, grad_v = attn_bwd(
        queries, key_rows, value_rows, grad_att, attended, inverse, chances
    )
    late_grads, grad_k = together(late_grads, grad_k)
    part, part_terms = unproject(sources, grad_k, grad_v, full_qkv)
    with jax.named_scope("scatter_late_weights"):
        late_sum = lax.psum_scatter(
            late_grads.reshape(rows * cols, *late_grads.shape[2:]),
            ("row", "col"),
            scatter_dimension=0,
            tiled=False,
        ).astype(jnp.float32)
        up_rows, down_rows = w_up.shape[0], w_down.shape[1]
        grad_w_up = late_sum[:up_rows]
        grad_w_down = jnp.concatenate(
            [late_sum[up_rows : up_rows + down_rows], late_sum[up_rows + down_rows :]], axis=1
        ).T

    def make_pieces(after):
        dq, dk, dv, unused = together(grad_q, grad_k, grad_v, after)
        own, other, grad_normed, own_terms = weigh(
            me, dq, dk, dv, normed, tokens, grad_out, full_qkv, cols
        )
        return own, other, (grad_normed, own_terms)

    def vectors_of(extra):
        return jnp.concatenate([part_terms + extra[1], sums, ff_terms.reshape(-1, D)], axis=0)

    with jax.named_scope("sum_gradients"):
        trunk_grad, branch_grad, branch_grad_far, early_sum, terms, extra = tail_rounds(
            part, parent_slot, level, make_pieces, vectors_of
        )
    tall = w_qkv.shape[1]
    grad_w_qkv, grad_w_out = early_sum[:, :tall], early_sum[:, tall:]
    finish_meta = jnp.stack([level, own_slot[0], own_slot[1]]).astype(jnp.int32)
    grad_tokens = finish(
        finish_meta, trunk_grad, branch_grad, branch_grad_far, extra[0], grad_mixed, tokens, small
    )
    with jax.named_scope("vectors"):
        cut = ln_gain.shape[1]
        mine = lax.dynamic_slice_in_dim(terms[:16], col * cut, cut, 1)
        grad_ff = lax.dynamic_slice_in_dim(
            terms[16:].reshape(-1), col * ff_bias.shape[0], ff_bias.shape[0], 0
        )
        grad_gain = jnp.stack([mine[0], mine[8]])
        grad_shift = jnp.stack([mine[1], mine[9]])
        grad_bias = jnp.stack([mine[3], mine[2], mine[10], mine[11]])
    return (
        output,
        grad_tokens,
        grad_w_qkv,
        grad_w_out,
        grad_w_up,
        grad_w_down,
        grad_gain,
        grad_shift,
        grad_bias,
        grad_ff,
    )


def solution(mesh):
    fits = mesh.shape["col"] == 8 and mesh.shape["row"] == 4
    body = tree_body if fits else plain_body
    return jax.shard_map(
        body,
        mesh=mesh,
        in_specs=(
            P(("row", "col"), None),
            P("row", None),
            P("row", "col"),
            P("row", "col"),
            P("row", "col"),
            P("row", "col"),
            P(None, "col"),
            P(None, "col"),
            P(None, "col"),
            P("col"),
            P(("row", "col"), None),
        ),
        out_specs=(
            P(("row", "col"), None),
            P(("row", "col"), None),
            P("row", "col"),
            P("row", "col"),
            P("row", "col"),
            P("row", "col"),
            P(None, "col"),
            P(None, "col"),
            P(None, "col"),
            P("col"),
        ),
        check_vma=False,
    )
```
